32 devices in a mesh: bins: 4 (over y, x), fsdp: 8 (over z, core).
Axes of the slice: x: 2, y: 2, z: 4, core: 2. Of those that a mesh axis runs over, the one named last changes fastest.
Arguments:
- tokens: bfloat16 [2, 8, 1024, 576], P(None, 'fsdp', 'bins'), may hold values from -6 to 6
- cotangent: bfloat16 [2, 8, 1024, 576], P(None, 'fsdp', 'bins'), may hold values from -6 to 6
- token_slots: int32 [2, 8, 1024], P(None, 'fsdp', 'bins'), may hold values from -1 to 1023, as said below
- sequence_lengths: int32 [2, 8, 4, 8], P(None, 'fsdp', 'bins'), may hold values from 0 to 256, as said below
- sequence_starts: int32 [2, 8, 4, 8], P(None, 'fsdp', 'bins'), may hold values from 0 to 256, as said below
- query_weight: bfloat16 [576, 576], P('fsdp', 'bins'), may hold values from -0.25 to 0.25
- key_weight: bfloat16 [576, 192], P('fsdp', 'bins'), may hold values from -0.25 to 0.25
- value_weight: bfloat16 [576, 192], P('fsdp', 'bins'), may hold values from -0.25 to 0.25
- output_weight: bfloat16 [576, 576], P('fsdp', 'bins'), may hold values from -1 to 1
- gate_weight: bfloat16 [576, 1536], P('fsdp', 'bins'), may hold values from -0.25 to 0.25
- up_weight: bfloat16 [576, 1536], P('fsdp', 'bins'), may hold values from -0.25 to 0.25
- down_weight: bfloat16 [1536, 576], P('bins', 'fsdp'), may hold values from -0.15625 to 0.15625
- attention_gain: bfloat16 [576], P('fsdp'), may hold values from 0.5 to 1.5
- feedforward_gain: bfloat16 [576], P('fsdp'), may hold values from 0.5 to 1.5
- query_moment: float32 [576, 576], P('fsdp', 'bins'), may hold values from -160 to 160
- key_moment: float32 [576, 192], P('fsdp', 'bins'), may hold values from -160 to 160
- value_moment: float32 [576, 192], P('fsdp', 'bins'), may hold values from -160 to 160
- output_moment: float32 [576, 576], P('fsdp', 'bins'), may hold values from -160 to 160
- gate_moment: float32 [576, 1536], P('fsdp', 'bins'), may hold values from -160 to 160
- up_moment: float32 [576, 1536], P('fsdp', 'bins'), may hold values from -160 to 160
- down_moment: float32 [1536, 576], P('bins', 'fsdp'), may hold values from -160 to 160
- attention_moment: float32 [576], P('fsdp'), may hold values from -384 to 384
- feedforward_moment: float32 [576], P('fsdp'), may hold values from -384 to 384
Outputs:
- block_output: bfloat16 [2, 8, 1024, 576], P(None, 'fsdp', 'bins')
- input_gradient: bfloat16 [2, 8, 1024, 576], P(None, 'fsdp', 'bins')
- query_state: float32 [576, 576], P('fsdp', 'bins')
- query_step: float32 [576, 576], P('fsdp', 'bins')
- key_state: float32 [576, 192], P('fsdp', 'bins')
- key_step: float32 [576, 192], P('fsdp', 'bins')
- value_state: float32 [576, 192], P('fsdp', 'bins')
- value_step: float32 [576, 192], P('fsdp', 'bins')
- output_state: float32 [576, 576], P('fsdp', 'bins')
- output_step: float32 [576, 576], P('fsdp', 'bins')
- gate_state: float32 [576, 1536], P('fsdp', 'bins')
- gate_step: float32 [576, 1536], P('fsdp', 'bins')
- up_state: float32 [576, 1536], P('fsdp', 'bins')
- up_step: float32 [576, 1536], P('fsdp', 'bins')
- down_state: float32 [1536, 576], P('bins', 'fsdp')
- down_step: float32 [1536, 576], P('bins', 'fsdp')
- attention_state: float32 [576], P('fsdp')
- attention_step: float32 [576], P('fsdp')
- feedforward_state: float32 [576], P('fsdp')
- feedforward_step: float32 [576], P('fsdp')
The draws below stay inside these ranges and needn't reach their ends.
Inputs may be any that keep to these rules, and one draw needn't show every extreme that they name: `token_slots`: each entry is -1 (a padding row) or bin * 256 + slot; no slot is named twice. Of the 256 rows of one device in a micro-batch, at most 64 go to any one bin; in every micro-batch of every fsdp index one bin takes exactly 64 from every device. The slots that rows fill in a bin are exactly those that its sequences cover. `sequence_lengths`: some lengths are zero; the lengths of a bin add up to its number of filled slots, which is at most 256. `sequence_starts`: each start is the sum of the lengths before it in its bin.
All inputs are finite; a program needn't handle non-finite values.
Results may differ from the reference program's by a relative error of at most 0.019.
The reference program's roundings to bfloat16 on the way count: a program that leaves them out, or rounds other values in their place, can miss the bound.
Values may be sent and summed in bfloat16 or wider, within the bound.
No kernel may reach another device: no remote copies, remote signals or barrier semaphores. Data moves between devices by JAX's collectives and lax.ppermute only.
A program may use at most 128 MiB of HBM per device.

```python
import math
import jax
import jax.numpy as jnp
from jax import lax

D = 576
HEADS = 9
KV_HEADS = 3
HEAD_DIM = 64
FF = 1536
BIN = 256
SEQ_BIN = 8
MICRO = 2
NS_STEPS = 5
QW = 576
KW = 192
CAP = 64
ROWS = 1024
N_BINS = 4
N_FSDP = 8


def row_order(key_item):
    return jax.random.permutation(key_item, BIN).astype(jnp.int32)


def deal_group(group_key):
    key_list = jax.random.split(group_key, 6)
    bin_index = jnp.arange(N_BINS, dtype=jnp.int32)
    full_bin = jax.random.randint(key_list[0], (), 0, N_BINS)
    upper_count = jax.random.randint(key_list[1], (N_BINS,), CAP // 2, CAP)
    lower_count = upper_count // 4
    raw_bits = jax.random.randint(key_list[2], (N_BINS, N_BINS), 0, 1 << 20)
    counts = lower_count[None, :] + raw_bits % (upper_count - lower_count + 1)[None, :]
    counts = jnp.where(bin_index[None, :] == full_bin, CAP, counts).astype(jnp.int32)
    bin_loads = jnp.sum(counts, axis=0)
    earlier = jnp.cumsum(counts, axis=0) - counts
    slot_index = jnp.arange(BIN, dtype=jnp.int32)
    slot_ranks = jax.vmap(row_order)(jax.random.split(key_list[3], N_BINS))
    order_keys = jnp.where(slot_index[None, :] < bin_loads[:, None], slot_ranks, BIN + slot_index[None, :])
    slot_order = jnp.argsort(order_keys, axis=1, stable=True).astype(jnp.int32)
    end_count = jnp.cumsum(counts, axis=1)
    start_count = end_count - counts
    target = jnp.sum((slot_index[None, :, None] >= end_count[:, None, :]).astype(jnp.int32), axis=2)
    is_valid = slot_index[None, :] < end_count[:, -1:]
    target_bin = jnp.minimum(target, N_BINS - 1)
    within = slot_index[None, :] - jnp.take_along_axis(start_count, target_bin, axis=1)
    arrival = jnp.clip(jnp.take_along_axis(earlier, target_bin, axis=1) + within, 0, BIN - 1)
    chosen = slot_order[target_bin, arrival]
    assigned = jnp.where(is_valid, target_bin * BIN + chosen, -1).astype(jnp.int32)
    row_shuffle = jax.vmap(row_order)(jax.random.split(key_list[4], N_BINS))
    source_index = jnp.broadcast_to(bin_index[:, None], (N_BINS, BIN))
    slot_table = jnp.zeros((N_BINS, BIN), jnp.int32).at[source_index, row_shuffle].set(assigned)
    cut_points = jax.random.randint(key_list[5], (N_BINS, SEQ_BIN - 1), 0, bin_loads[:, None] + 1)
    cut_points = jnp.where(bin_index[:, None] == full_bin, bin_loads[:, None], cut_points)
    cut_points = jnp.sort(cut_points, axis=1).astype(jnp.int32)
    boundary = jnp.concatenate([jnp.zeros((N_BINS, 1), jnp.int32), cut_points, bin_loads[:, None].astype(jnp.int32)], axis=1)
    return (slot_table.reshape(ROWS), boundary[:, 1:] - boundary[:, :-1], boundary[:, :-1])


def deal_all(key):
    group_keys = jax.random.split(jax.random.fold_in(key, 9173), MICRO * N_FSDP)
    slot_table, lengths, starts = jax.vmap(deal_group)(group_keys)
    return (slot_table.reshape(MICRO, N_FSDP, ROWS), lengths.reshape(MICRO, N_FSDP, N_BINS, SEQ_BIN), starts.reshape(MICRO, N_FSDP, N_BINS, SEQ_BIN))


def draw_token_slots(key, part):
    return deal_all(key)[0]


def draw_sequence_lengths(key, part):
    return deal_all(key)[1]


def draw_sequence_starts(key, part):
    return deal_all(key)[2]


def shard_levels(rng, shape, pieces, least, high):
    factor_of, own = 1.0, jax.random.fold_in(rng, 6)
    for dim, shards_of in pieces:
        heights = jnp.exp(jax.random.uniform(jax.random.fold_in(own, dim), (shards_of,), jnp.float32, least / len(pieces), high / len(pieces)))
        factor_of = factor_of * jnp.repeat(heights, shape[dim] // shards_of).reshape([-1 if axis == dim else 1 for axis in range(len(shape))])
    return factor_of


def noise(stream_key, extent, deviation, limit, cuts=(), kind=jnp.bfloat16):
    level = shard_levels(stream_key, extent, cuts, -0.22, 0.18) if cuts else 1.0
    result = jax.random.normal(stream_key, extent, jnp.float32) * deviation * level
    return jnp.minimum(jnp.maximum(result, -limit), limit).astype(kind)


def setup_inputs(seed: int = 0) -> dict:
    splits = jax.random.split(jax.random.key(seed), 24)
    tokens = noise(splits[0], (MICRO, N_FSDP, ROWS, D), 1.0, 6.0, ((1, 8), (2, 4)))
    cotangent = noise(splits[1], (MICRO, N_FSDP, ROWS, D), 1.0, 6.0, ((1, 8), (2, 4)))
    token_slots = draw_token_slots(jax.random.fold_in(splits[23], 71), 0)
    sequence_lengths = draw_sequence_lengths(jax.random.fold_in(splits[23], 71), 0)
    sequence_starts = draw_sequence_starts(jax.random.fold_in(splits[23], 71), 0)
    query_weight = noise(splits[5], (D, QW), D ** -0.5, 0.25, ((0, 8), (1, 4)))
    key_weight = noise(splits[6], (D, KW), D ** -0.5, 0.25, ((0, 8), (1, 4)))
    value_weight = noise(splits[7], (D, KW), D ** -0.5, 0.25, ((0, 8), (1, 4)))
    output_weight = noise(splits[8], (QW, D), (D // 16) ** -0.5, 1.0, ((0, 8), (1, 4)))
    gate_weight = noise(splits[9], (D, FF), D ** -0.5, 0.25, ((0, 8), (1, 4)))
    up_weight = noise(splits[10], (D, FF), D ** -0.5, 0.25, ((0, 8), (1, 4)))
    down_weight = noise(splits[11], (FF, D), FF ** -0.5, 0.15625, ((0, 4), (1, 8)))
    attention_gain = jnp.clip(1.0 + 0.1 * jax.random.normal(splits[12], (D,), jnp.float32), 0.5, 1.5).astype(jnp.bfloat16)
    feedforward_gain = jnp.clip(1.0 + 0.1 * jax.random.normal(splits[13], (D,), jnp.float32), 0.5, 1.5).astype(jnp.bfloat16)
    query_moment = noise(splits[14], (D, QW), (0.2 * (MICRO * N_BINS * N_FSDP * BIN) ** 0.5), 160.0, ((0, 8), (1, 4)), jnp.float32)
    key_moment = noise(splits[15], (D, KW), (0.2 * (MICRO * N_BINS * N_FSDP * BIN) ** 0.5), 160.0, ((0, 8), (1, 4)), jnp.float32)
    value_moment = noise(splits[16], (D, KW), (0.2 * (MICRO * N_BINS * N_FSDP * BIN) ** 0.5), 160.0, ((0, 8), (1, 4)), jnp.float32)
    output_moment = noise(splits[17], (QW, D), (0.2 * (MICRO * N_BINS * N_FSDP * BIN) ** 0.5), 160.0, ((0, 8), (1, 4)), jnp.float32)
    gate_moment = noise(splits[18], (D, FF), (0.2 * (MICRO * N_BINS * N_FSDP * BIN) ** 0.5), 160.0, ((0, 8), (1, 4)), jnp.float32)
    up_moment = noise(splits[19], (D, FF), (0.2 * (MICRO * N_BINS * N_FSDP * BIN) ** 0.5), 160.0, ((0, 8), (1, 4)), jnp.float32)
    down_moment = noise(splits[20], (FF, D), (0.2 * (MICRO * N_BINS * N_FSDP * BIN) ** 0.5), 160.0, ((0, 4), (1, 8)), jnp.float32)
    attention_moment = noise(splits[21], (D,), (0.5 * (MICRO * N_BINS * N_FSDP * BIN) ** 0.5), 384.0, ((0, 8),), jnp.float32)
    feedforward_moment = noise(splits[22], (D,), (0.5 * (MICRO * N_BINS * N_FSDP * BIN) ** 0.5), 384.0, ((0, 8),), jnp.float32)
    return {"tokens": tokens, "cotangent": cotangent, "token_slots": token_slots, "sequence_lengths": sequence_lengths, "sequence_starts": sequence_starts, "query_weight": query_weight, "key_weight": key_weight, "value_weight": value_weight, "output_weight": output_weight, "gate_weight": gate_weight, "up_weight": up_weight, "down_weight": down_weight, "attention_gain": attention_gain, "feedforward_gain": feedforward_gain, "query_moment": query_moment, "key_moment": key_moment, "value_moment": value_moment, "output_moment": output_moment, "gate_moment": gate_moment, "up_moment": up_moment, "down_moment": down_moment, "attention_moment": attention_moment, "feedforward_moment": feedforward_moment}


EPSILON = 1e-05
NEGATIVE = -1e+30
ROPE_BASE = 10000.0
COEFF_A = 3.4445
COEFF_B = -4.775
COEFF_C = 2.0315
DECAY = 0.5
HIGHEST = lax.Precision.HIGHEST

@jax.custom_vjp
def low(v):
    return lax.optimization_barrier(v.astype(jnp.bfloat16)).astype(jnp.float32)

@jax.custom_vjp
def low_back(v):
    return v

def low_keep(v):
    return (low(v), None)

def low_pass(kept, grad):
    return (grad,)

def back_keep(v):
    return (v, None)

def back_low(kept, grad):
    return (low(grad),)
low.defvjp(low_keep, low_pass)
low_back.defvjp(back_keep, back_low)

def matmul(left, right):
    return jnp.dot(left, right, precision=HIGHEST, preferred_element_type=jnp.float32)

def norm_rows(values, gain):
    inverse = lax.rsqrt(lax.optimization_barrier(jnp.mean(values * values, axis=-1, keepdims=True)) + EPSILON)
    return values * inverse * gain

def rope_tables(positions):
    half_dim = HEAD_DIM // 2
    frequency = jnp.exp(-math.log(ROPE_BASE) * 2.0 * jnp.arange(half_dim, dtype=jnp.float32) / HEAD_DIM)
    angles = positions.astype(jnp.float32)[:, None] * frequency[None, :]
    return (jnp.cos(angles), jnp.sin(angles))

def rotate(values, cosine, sine_table, direction):
    half_dim = values.shape[-1] // 2
    first_half = values[..., :half_dim]
    second_half = values[..., half_dim:]
    cos_part = cosine[:, None, :]
    sin_part = sine_table[:, None, :] * direction
    return jnp.concatenate([first_half * cos_part - second_half * sin_part, second_half * cos_part + first_half * sin_part], axis=-1)

def slot_layout(lengths, starts):
    slot_index = jnp.arange(BIN, dtype=jnp.int32)
    inside = ((slot_index[:, None] >= starts[None, :]) & (slot_index[:, None] < starts[None, :] + lengths[None, :])).astype(jnp.int32)
    number = jnp.arange(lengths.shape[0], dtype=jnp.int32)
    covered = jnp.minimum(lax.optimization_barrier(jnp.sum(inside, axis=1)), 1)
    segment = lax.optimization_barrier(jnp.sum(inside * number[None, :], axis=1)) + (1 - covered) * (lengths.shape[0] + slot_index)
    first_slot = lax.optimization_barrier(jnp.sum(inside * starts[None, :], axis=1))
    return (segment, slot_index - first_slot)

def bin_forward(packed_bin, weights):
    tokens_bin, segment, position = packed_bin
    query_matrix, key_matrix, value_matrix, output_matrix, gate_matrix, up_matrix, down_matrix, attention_gain, feed_gain = weights
    slot_count = tokens_bin.shape[0]
    groups = HEADS // KV_HEADS
    normed_one = low(norm_rows(tokens_bin, attention_gain))
    query_raw = low_back(matmul(normed_one, query_matrix)).reshape(slot_count, HEADS, HEAD_DIM)
    key_raw = low_back(matmul(normed_one, key_matrix)).reshape(slot_count, KV_HEADS, HEAD_DIM)
    value_low = low(low_back(matmul(normed_one, value_matrix))).reshape(slot_count, KV_HEADS, HEAD_DIM)
    cosine, sine_table = rope_tables(position)
    query_rot = low(rotate(query_raw, cosine, sine_table, 1.0)).reshape(slot_count, KV_HEADS, groups, HEAD_DIM)
    key_rot = low(rotate(key_raw, cosine, sine_table, 1.0))
    score_scale = 1.0 / math.sqrt(HEAD_DIM)
    scores = low_back(jnp.einsum('qkgd,tkd->kgqt', query_rot, key_rot, precision=HIGHEST) * score_scale)
    slot_index = jnp.arange(slot_count, dtype=jnp.int32)
    allowed = (segment[:, None] == segment[None, :]) & (slot_index[None, :] <= slot_index[:, None])
    scores = jnp.where(allowed, scores, NEGATIVE)
    soft_low = low(jax.nn.softmax(scores, axis=-1))
    attended = jnp.einsum('kgqt,tkd->qkgd', soft_low, value_low, precision=HIGHEST).reshape(slot_count, HEADS * HEAD_DIM)
    attended = low(low_back(attended))
    hidden = tokens_bin + low_back(matmul(attended, output_matrix))
    normed_two = low(norm_rows(hidden, feed_gain))
    gate_linear = low_back(matmul(normed_two, gate_matrix))
    up_linear = low_back(matmul(normed_two, up_matrix))
    active = low(jax.nn.silu(gate_linear) * up_linear)
    return hidden + low_back(matmul(active, down_matrix))

def group_forward(tokens_rows, slot_rows, segments, positions, weights):
    landing = jnp.where(slot_rows >= 0, slot_rows, ROWS)
    packed = jnp.zeros((ROWS, D), jnp.float32).at[landing].set(tokens_rows, mode='drop').reshape(N_BINS, BIN, D)

    def one_bin(packed_bin):
        return bin_forward(packed_bin, weights)
    results = lax.map(jax.checkpoint(one_bin), (packed, segments, positions))
    flattened = results.reshape(ROWS, D)
    picked = flattened[jnp.clip(slot_rows, 0, ROWS - 1)]
    return jnp.where(slot_rows[:, None] >= 0, picked, jnp.zeros_like(picked))

def newton_schulz(matrix_state):
    flipped = matrix_state.shape[0] > matrix_state.shape[1]
    iterate = matrix_state.T if flipped else matrix_state
    iterate = iterate / (jnp.sqrt(jnp.sum(iterate * iterate)) + 1e-07)
    for repeat in range(NS_STEPS):
        gram_matrix = matmul(iterate, iterate.T)
        poly_matrix = COEFF_B * gram_matrix + COEFF_C * matmul(gram_matrix, gram_matrix)
        iterate = COEFF_A * iterate + matmul(poly_matrix, iterate)
    return iterate.T if flipped else iterate

def reference(tokens, cotangent, token_slots, sequence_lengths, sequence_starts, query_weight, key_weight, value_weight, output_weight, gate_weight, up_weight, down_weight, attention_gain, feedforward_gain, query_moment, key_moment, value_moment, output_moment, gate_moment, up_moment, down_moment, attention_moment, feedforward_moment):
    weights = tuple((tensor.astype(jnp.float32) for tensor in (query_weight, key_weight, value_weight, output_weight, gate_weight, up_weight, down_weight, attention_gain, feedforward_gain)))
    group_count = MICRO * N_FSDP
    flat_tokens = tokens.reshape(group_count, ROWS, D)
    flat_upstream = cotangent.reshape(group_count, ROWS, D)
    flat_slots = token_slots.reshape(group_count, ROWS)
    flat_lengths = sequence_lengths.reshape(group_count, N_BINS, SEQ_BIN)
    flat_starts = sequence_starts.reshape(group_count, N_BINS, SEQ_BIN)

    def one_group(totals, group_item):
        tokens_rows, upstream_rows, slot_rows, lengths, starts = group_item
        segments, positions = jax.vmap(slot_layout)(lengths, starts)

        def forward(tokens_in, *params):
            return group_forward(tokens_in, slot_rows, segments, positions, params)
        outputs, pullback = jax.vjp(forward, tokens_rows.astype(jnp.float32), *weights)
        back_parts = pullback(upstream_rows.astype(jnp.float32))
        totals = tuple((total + addend for total, addend in zip(totals, back_parts[1:])))
        return (totals, (outputs.astype(jnp.bfloat16), back_parts[0].astype(jnp.bfloat16)))
    zero_grads = tuple((jnp.zeros(tensor.shape, jnp.float32) for tensor in weights))
    gradients, (block_rows, back_rows) = lax.scan(one_group, zero_grads, (flat_tokens, flat_upstream, flat_slots, flat_lengths, flat_starts))
    moments = (query_moment, key_moment, value_moment, output_moment, gate_moment, up_moment, down_moment, attention_moment, feedforward_moment)
    states = tuple((DECAY * moment + (1.0 - DECAY) * gradient for moment, gradient in zip(moments, gradients)))
    step_list = []
    for matrix_id in range(7):
        matrix_state = states[matrix_id]
        step_rate = math.sqrt(max(1.0, matrix_state.shape[0] / matrix_state.shape[1]))
        step_list.append(-step_rate * newton_schulz(matrix_state))
    gain_rate = 0.1 / math.sqrt(MICRO * N_BINS * N_FSDP * BIN)
    return (block_rows.reshape(MICRO, N_FSDP, ROWS, D), back_rows.reshape(MICRO, N_FSDP, ROWS, D), states[0], step_list[0], states[1], step_list[1], states[2], step_list[2], states[3], step_list[3], states[4], step_list[4], states[5], step_list[5], states[6], step_list[6], states[7], -gain_rate * states[7], states[8], -gain_rate * states[8])
```

```python
import math

import jax
import jax.numpy as jnp
from jax import lax
from jax.experimental import pallas as pl
from jax.experimental.pallas import tpu as pltpu
from jax.sharding import PartitionSpec as P

HEADS = 9
KV_HEADS = 3
HEAD_DIM = 64
GROUPS = HEADS // KV_HEADS
NS_STEPS = 5
EPSILON = 1e-05
NEGATIVE = -1e30
ROPE_BASE = 10000.0
COEFF_A = 3.4445
COEFF_B = -4.775
COEFF_C = 2.0315
BF = jnp.bfloat16
F32 = jnp.float32


def dot(left, right, dims):
    return lax.dot_general(left, right, (dims, ((), ())), preferred_element_type=F32)


def mm(left, right):
    return dot(left, right, ((left.ndim - 1,), (0,)))


def mm_t(left, right):
    return dot(left, right, ((left.ndim - 1,), (1,)))


def t_mm(left, right):
    return dot(left, right, ((0,), (0,)))


def swap(value, axis, count, step, keep=None):
    pairs = [(i, i ^ step) for i in range(count) if keep is None or keep(i ^ step)]
    return lax.ppermute(value, axis, pairs)


def bits_of(count):
    return [1 << i for i in range(count.bit_length() - 1)]


def ordered(pieces, index):
    result = list(pieces)
    for bit in bits_of(len(pieces)):
        flag = (index & bit) != 0
        result = [jnp.where(flag, result[j ^ bit], result[j]) for j in range(len(result))]
    return result


def join(mine, other, flag):
    return jnp.stack([jnp.where(flag, other, mine), jnp.where(flag, mine, other)])


def gather_bins(value, bins, b, order):
    for bit in order:
        value = join(value, swap(value, "bins", bins, bit), (b & bit) != 0)
    count = len(order)
    want = sorted(order, reverse=True)
    held = list(reversed(order))
    shape = value.shape[count:]
    value = jnp.transpose(
        value, [held.index(bit) for bit in want] + list(range(count, value.ndim))
    )
    return value.reshape((bins,) + shape)


def bin_orders(bins):
    bits = bits_of(bins)
    half = len(bits) // 2
    return bits, bits[half:] + bits[:half]


def gather_weights(piece, bins, fsdp, b, f):
    count, rows, width = piece.shape
    chips = fsdp // 2
    pieces = [piece] + [swap(piece, "fsdp", fsdp, 2 * k) for k in range(1, chips)]
    pieces = ordered(pieces, f // 2)
    half = chips // 2
    parts = []
    for start, order in zip((0, half), bin_orders(bins)):
        parts.append(gather_bins(jnp.stack(pieces[start : start + half]), bins, b, order))
    own = jnp.concatenate(parts, axis=1)
    other = swap(own, "fsdp", fsdp, 1)
    flag = (f & 1) != 0
    both = jnp.stack([jnp.where(flag, other, own), jnp.where(flag, own, other)], axis=2)
    both = jnp.transpose(both, (3, 0, 1, 2, 4, 5))
    return both.reshape(count, bins, fsdp * rows, width)


def add_low(left, right):
    return (left.astype(F32) + right.astype(F32)).astype(BF)


def pick(value, index, axis):
    return lax.dynamic_index_in_dim(value, index, axis, keepdims=False)


def reduce_blocks(grads, first, bins, fsdp, b, f):
    count, _, rows, width = grads.shape
    split = fsdp // 4
    for bit in bits_of(split)[::-1]:
        view = grads.reshape(count, bins, 2, grads.shape[2] // 2, width)
        flag = jnp.where((f & bit) != 0, 1, 0)
        got = swap(pick(view, 1 - flag, 2), "fsdp", fsdp, bit)
        grads = add_low(pick(view, flag, 2), got)
    half = grads.shape[2] // 2
    parts = []
    for start, order in zip((0, half), bin_orders(bins)):
        part = grads[:, :, start : start + half].reshape(
            (count,) + (2,) * len(order) + (half, width)
        )
        left = sorted(order, reverse=True)
        for bit in order:
            where = 1 + left.index(bit)
            flag = jnp.where((b & bit) != 0, 1, 0)
            got = swap(pick(part, 1 - flag, where), "bins", bins, bit)
            part = add_low(pick(part, flag, where), got)
            left.remove(bit)
        parts.append(part)
    part = jnp.concatenate(parts, axis=1)
    owner = f // split
    last = count - 1
    total = pick(part, jnp.clip(owner - first, 0, last), 0).astype(F32)
    for k in range(1, 4):
        sent = pick(part, jnp.clip((owner ^ k) - first, 0, last), 0)
        got = swap(
            sent, "fsdp", fsdp, k * split, lambda t: first <= t // split < first + count
        )
        total = total + got.astype(F32)
    return total


def feed_kernel(own_ref, a2_ref, up_grad_ref, w_ref, moment_ref, y_ref, dh2_ref, grad_ref,
                a2t_ref, gt_ref, act_ref, dg_ref, du_ref, acc_ref):
    step = pl.program_id(0)
    tokens = a2_ref.shape[0]
    chunk = 128

    @pl.when(step == 0)
    def _():
        a2t_ref[...] = a2_ref[...].T
        gt_ref[...] = up_grad_ref[...].T
        y_ref[...] = jnp.zeros_like(y_ref)
        dh2_ref[...] = jnp.zeros_like(dh2_ref)

    w_gate = w_ref[0, 0]
    w_up = w_ref[1, 0]
    w_down = w_ref[2, 0]
    for start in range(0, tokens, chunk):
        rows = pl.ds(start, chunk)
        a2 = a2_ref[rows, :]
        gate = mm(a2, w_gate)
        up = mm(a2, w_up)
        dact = mm(up_grad_ref[rows, :], w_down)
        sig = 1.0 / (1.0 + jnp.exp(-gate))
        silu = gate * sig
        act = (silu * up).astype(BF)
        dgate = (dact * up * sig * (1.0 + gate * (1.0 - sig))).astype(BF)
        dup = (dact * silu).astype(BF)
        act_ref[rows, :] = act
        dg_ref[rows, :] = dgate
        du_ref[rows, :] = dup
        y_ref[rows, :] += mm_t(act, w_down)
        dh2_ref[rows, :] += mm_t(dgate, w_gate) + mm_t(dup, w_up)
    for index, (left, right) in enumerate(
        ((a2t_ref, dg_ref), (a2t_ref, du_ref), (gt_ref, act_ref))
    ):
        acc_ref[...] = mm(left[...], right[...])

        @pl.when(step == own_ref[0])
        def _():
            high = moment_ref.shape[1]
            rows = pl.ds(pl.multiple_of(own_ref[1] * high, 4), high)
            acc_ref[rows, :] += moment_ref[index]

        grad_ref[index, 0] = acc_ref[...].astype(BF)


def feed_forward_back(own, a2, up_grad, weights, moments):
    tokens, model = a2.shape
    _, bins, _, width = weights.shape
    whole = lambda i, own_ref: (0, 0)
    block = pl.BlockSpec((3, 1, model, width), lambda i, own_ref: (0, i, 0, 0))
    return pl.pallas_call(
        feed_kernel,
        grid_spec=pltpu.PrefetchScalarGridSpec(
            num_scalar_prefetch=1,
            grid=(bins,),
            in_specs=[
                pl.BlockSpec((tokens, model), whole),
                pl.BlockSpec((tokens, model), whole),
                block,
                pl.BlockSpec(moments.shape, lambda i, own_ref: (0, 0, 0)),
            ],
            out_specs=[
                pl.BlockSpec((tokens, model), whole),
                pl.BlockSpec((tokens, model), whole),
                block,
            ],
            scratch_shapes=[
                pltpu.VMEM((model, tokens), BF),
                pltpu.VMEM((model, tokens), BF),
                pltpu.VMEM((tokens, width), BF),
                pltpu.VMEM((tokens, width), BF),
                pltpu.VMEM((tokens, width), BF),
                pltpu.VMEM((model, width), F32),
            ],
        ),
        out_shape=[
            jax.ShapeDtypeStruct((tokens, model), F32),
            jax.ShapeDtypeStruct((tokens, model), F32),
            jax.ShapeDtypeStruct(weights.shape, BF),
        ],
        name="feed",
    )(own, a2, up_grad, weights, moments)


def newton_kernel(kind_ref, state_ref, out_ref, z_ref, zb_ref, a_ref, ab_ref, p_ref):
    bins, size, width = state_ref.shape
    chunk = 144
    starts = tuple(range(0, size, chunk))
    quarter = width * 3 // 8
    eighth = width // 8
    if width % 128 == 0:
        lows, mids, highs = (0, 2 * 128), (128, 128), (128, 2 * 128)
    else:
        lows = mids = highs = (0, width)
    eye_col = lax.broadcasted_iota(jnp.int32, (chunk, size), 1)
    eye_row = lax.broadcasted_iota(jnp.int32, (chunk, size), 0)

    def run(window, low, high):
        first, wide = window
        cols = wide * bins
        lane = lax.broadcasted_iota(jnp.int32, (size, wide), 1) + first
        keep = (lane >= low) & (lane < high)
        total = jnp.zeros((), F32)
        for j in range(bins):
            piece = state_ref[j, :, first : first + wide].astype(F32)
            if (low, high) != (first, first + wide):
                piece = jnp.where(keep, piece, 0.0)
            z_ref[:, j * wide : (j + 1) * wide] = piece
            total = total + jnp.sum(piece * piece)
        scale = 1.0 / (jnp.sqrt(jnp.full((1, 1), total, F32)) + 1e-07)
        for start in starts:
            rows = pl.ds(start, chunk)
            value = z_ref[rows, :cols] * scale
            z_ref[rows, :cols] = value
            zb_ref[rows, :cols] = value.astype(BF)

        def one(step, carry):
            whole = zb_ref[:, :cols]
            row_diag = []
            for start in starts:
                rows = pl.ds(start, chunk)
                gram = mm_t(zb_ref[rows, :cols], whole)
                eye = eye_col == eye_row + start
                a_ref[rows, :] = gram
                ab_ref[rows, :] = jnp.where(eye, 0.0, gram).astype(BF)
                row_diag.append(jnp.sum(jnp.where(eye, gram, 0.0), axis=0, keepdims=True))
            across = row_diag[0]
            for item in row_diag[1:]:
                across = across + item
            off = ab_ref[...]
            for start in starts:
                rows = pl.ds(start, chunk)
                gram = a_ref[rows, :]
                eye = eye_col == eye_row + start
                down = jnp.sum(jnp.where(eye, gram, 0.0), axis=1, keepdims=True)
                outer = jnp.where(eye, 0.0, gram)
                square = mm(ab_ref[rows, :], off) + (down + across) * outer
                square = square + jnp.where(eye, gram * gram, 0.0)
                poly = COEFF_B * gram + COEFF_C * square
                p_ref[rows, :] = poly
            for start in starts:
                rows = pl.ds(start, chunk)
                poly = p_ref[rows, :]
                eye = eye_col == eye_row + start
                diag = jnp.sum(jnp.where(eye, poly, 0.0), axis=1, keepdims=True) + COEFF_A
                part = jnp.where(eye, 0.0, poly).astype(BF)
                z_ref[rows, :cols] = diag * z_ref[rows, :cols] + mm(part, whole)
            for start in starts:
                rows = pl.ds(start, chunk)
                zb_ref[rows, :cols] = z_ref[rows, :cols].astype(BF)
            return carry

        lax.fori_loop(0, NS_STEPS, one, 0)
        for j in range(bins):

            @pl.when(kind_ref[1] == j)
            def _():
                mine = zb_ref[:, j * wide : (j + 1) * wide]
                old = out_ref[:, first : first + wide]
                if (low, high) != (first, first + wide):
                    mine = jnp.where(keep, mine.astype(F32), old.astype(F32)).astype(BF)
                out_ref[:, first : first + wide] = mine

    out_ref[...] = jnp.zeros_like(out_ref)

    @pl.when(kind_ref[0] == 0)
    def _():
        run((0, width), 0, width)

    @pl.when(kind_ref[0] == 1)
    def _():
        run(lows, 0, quarter)
        run(mids, quarter, quarter + eighth)

    @pl.when(kind_ref[0] == 2)
    def _():
        run(mids, quarter + eighth, quarter + 2 * eighth)
        run(highs, quarter + 2 * eighth, width)


def newton(kind, state):
    bins, size, width = state.shape
    return pl.pallas_call(
        newton_kernel,
        in_specs=[
            pl.BlockSpec(memory_space=pltpu.SMEM),
            pl.BlockSpec(memory_space=pltpu.VMEM),
        ],
        out_specs=pl.BlockSpec(memory_space=pltpu.VMEM),
        out_shape=jax.ShapeDtypeStruct((size, width), BF),
        scratch_shapes=[
            pltpu.VMEM((size, bins * width), F32),
            pltpu.VMEM((size, bins * width), BF),
            pltpu.VMEM((size, size), F32),
            pltpu.VMEM((size, size), BF),
            pltpu.VMEM((size, size), F32),
        ],
        name="newton",
    )(kind, state)


def norm_rows(values, gain):
    inverse = lax.rsqrt(jnp.mean(values * values, axis=-1, keepdims=True) + EPSILON)
    return (values * inverse * gain, inverse)


def norm_back(values, inverse, gain, upstream):
    scaled = upstream * gain
    inner_sum = jnp.mean(scaled * values, axis=-1, keepdims=True)
    values_back = inverse * scaled - values * (inverse * inverse * inverse) * inner_sum
    gain_back = jnp.sum(upstream * values * inverse, axis=0)
    return (values_back, gain_back)


def rope_tables(positions):
    half_dim = HEAD_DIM // 2
    frequency = jnp.exp(
        -math.log(ROPE_BASE) * 2.0 * jnp.arange(half_dim, dtype=F32) / HEAD_DIM
    )
    angles = positions.astype(F32)[..., None] * frequency
    return (jnp.cos(angles), jnp.sin(angles))


def rotate(values, cosine, sine_table, direction):
    half_dim = values.shape[-1] // 2
    first_half = values[..., :half_dim]
    second_half = values[..., half_dim:]
    cos_part = cosine[..., None, :]
    sin_part = sine_table[..., None, :] * direction
    return jnp.concatenate(
        [
            first_half * cos_part - second_half * sin_part,
            second_half * cos_part + first_half * sin_part,
        ],
        axis=-1,
    )


def slot_layout(lengths, starts, bin_slots):
    slot_index = jnp.arange(bin_slots, dtype=jnp.int32)
    inside = (
        (slot_index[:, None] >= starts[..., None, :])
        & (slot_index[:, None] < starts[..., None, :] + lengths[..., None, :])
    ).astype(jnp.int32)
    number = jnp.arange(lengths.shape[-1], dtype=jnp.int32)
    covered = jnp.minimum(jnp.sum(inside, axis=-1), 1)
    segment = jnp.sum(inside * number, axis=-1) + (1 - covered) * (
        lengths.shape[-1] + slot_index
    )
    first_slot = jnp.sum(inside * starts[..., None, :], axis=-1)
    return (segment, slot_index - first_slot)


def on_device(
    tokens, cotangent, token_slots, sequence_lengths, sequence_starts,
    query_weight, key_weight, value_weight, output_weight,
    gate_weight, up_weight, down_weight, attention_gain, feedforward_gain,
    query_moment, key_moment, value_moment, output_moment,
    gate_moment, up_moment, down_moment, attention_moment, feedforward_moment,
):
    bins = lax.axis_size("bins")
    fsdp = lax.axis_size("fsdp")
    b = lax.axis_index("bins")
    f = lax.axis_index("fsdp")
    micro, _, slots, model = tokens.shape
    cap = slots // bins
    total = micro * slots
    rows_own = query_weight.shape[0]
    q_cols = query_weight.shape[1]
    k_cols = key_weight.shape[1]

    block_zero = jnp.concatenate(
        [query_weight, key_weight, value_weight, output_weight], axis=1
    )[None]
    blocks = jnp.stack([gate_weight, up_weight, down_weight.T])
    gains = jnp.stack([attention_gain, feedforward_gain])
    gain_pieces = [gains] + [swap(gains, "fsdp", fsdp, k) for k in range(1, fsdp)]
    gains_full = jnp.concatenate(ordered(gain_pieces, f), axis=1).astype(F32)
    width = block_zero.shape[2]
    attn_w = gather_weights(block_zero, bins, fsdp, b, f)[0]

    row_slots = token_slots[:, 0]
    is_valid = row_slots >= 0
    relative = jnp.where(is_valid, (row_slots // slots) ^ b, bins)
    onehot = relative[:, :, None] == jnp.arange(bins, dtype=jnp.int32)
    onehot_f = onehot.astype(BF)
    earlier = (
        jnp.arange(slots)[:, None] > jnp.arange(slots)[None, :]
    ).astype(BF)
    before = jnp.einsum("rs,msk->mrk", earlier, onehot_f, preferred_element_type=F32)
    rank = jnp.sum(before * onehot.astype(F32), axis=2).astype(jnp.int32)
    place = jnp.where(is_valid, relative * cap + rank, slots)
    send_map = (place[:, None, :] == jnp.arange(slots, dtype=jnp.int32)[:, None]).astype(BF)
    mark = jnp.where(is_valid, row_slots % slots + 1, 0).astype(BF)
    extra = jnp.pad(mark[:, :, None], ((0, 0), (0, 0), (0, (-model - 1) % 128)))
    payload = jnp.concatenate([tokens[:, 0], extra.astype(BF), cotangent[:, 0]], axis=2)
    sent = jnp.einsum("mbr,mrd->mbd", send_map, payload, preferred_element_type=F32)
    sent = sent.astype(BF).reshape(micro, bins, cap, payload.shape[2])
    got = [sent[:, 0]] + [swap(sent[:, k], "bins", bins, k) for k in range(1, bins)]
    got = jnp.concatenate(got, axis=1)
    got_slot = got[:, :, model].astype(jnp.int32) - 1
    land_map = (
        got_slot[:, None, :] == jnp.arange(slots, dtype=jnp.int32)[:, None]
    ).astype(BF)
    landed = jnp.einsum("msr,mrd->msd", land_map, got, preferred_element_type=F32).astype(BF)
    x_low = landed[:, :, :model].reshape(total, model)
    g_low = landed[:, :, payload.shape[2] - model :].reshape(total, model)

    def send_home(values):
        values = values.reshape(micro, slots, model)
        back = jnp.einsum("msr,msd->mrd", land_map, values, preferred_element_type=F32)
        back = back.astype(BF).reshape(micro, bins, cap, model)
        home = [back[:, 0]] + [swap(back[:, k], "bins", bins, k) for k in range(1, bins)]
        home = jnp.concatenate(home, axis=1)
        rows = jnp.einsum("mbr,mbd->mrd", send_map, home, preferred_element_type=F32)
        return rows.astype(BF)[:, None]

    segment, position = slot_layout(sequence_lengths[:, 0, 0], sequence_starts[:, 0, 0], slots)
    slot_index = jnp.arange(slots, dtype=jnp.int32)
    allowed = (segment[:, :, None] == segment[:, None, :]) & (
        slot_index[None, :] <= slot_index[:, None]
    )
    allowed = allowed[:, None, None]
    cosine, sine = rope_tables(position)

    feed_w = gather_weights(blocks, bins, fsdp, b, f)

    def columns(start, stop):
        return jnp.concatenate([attn_w[j, :, start:stop] for j in range(bins)], axis=1)

    edges = (0, q_cols, q_cols + k_cols, q_cols + 2 * k_cols, width)
    w_q, w_k, w_v, w_o = [columns(edges[i], edges[i + 1]) for i in range(4)]

    x = x_low.astype(F32)
    n1, r1 = norm_rows(x, gains_full[0])
    a1 = n1.astype(BF)
    q = mm(a1, w_q).reshape(micro, slots, HEADS, HEAD_DIM)
    k = mm(a1, w_k).reshape(micro, slots, KV_HEADS, HEAD_DIM)
    vb = mm(a1, w_v).astype(BF).reshape(micro, slots, KV_HEADS, HEAD_DIM)
    qr = rotate(q, cosine, sine, 1.0).astype(BF)
    qr = qr.reshape(micro, slots, KV_HEADS, GROUPS, HEAD_DIM)
    kr = rotate(k, cosine, sine, 1.0).astype(BF)
    scale = 1.0 / math.sqrt(HEAD_DIM)
    scores = jnp.einsum("mqkgd,mtkd->mkgqt", qr, kr, preferred_element_type=F32) * scale
    scores = jnp.where(allowed, scores, NEGATIVE)
    peak = jnp.max(scores, axis=-1, keepdims=True)
    raised = jnp.exp(scores - peak)
    soft = raised / jnp.sum(raised, axis=-1, keepdims=True)
    soft_low = soft.astype(BF)
    ob = jnp.einsum("mkgqt,mtkd->mqkgd", soft_low, vb, preferred_element_type=F32)
    ob = ob.reshape(total, HEADS * HEAD_DIM).astype(BF)
    h = x + mm(ob, w_o)
    n2, r2 = norm_rows(h, gains_full[1])
    a2 = n2.astype(BF)

    own = jnp.stack([b, f]).astype(jnp.int32)
    moments = jnp.stack([gate_moment, up_moment, down_moment.T])
    y_part, dh2, feed_grads = feed_forward_back(own, a2, g_low, feed_w, moments)
    block_output = send_home((h + y_part).astype(BF))
    part_one = reduce_blocks(feed_grads, 1, bins, fsdp, b, f)

    g = g_low.astype(F32)
    back, gain_two = norm_back(h, r2, gains_full[1], dh2)
    dh = g + back
    dhb = dh.astype(BF)
    dob = mm_t(dhb, w_o).astype(BF).reshape(micro, slots, KV_HEADS, GROUPS, HEAD_DIM)
    dp = jnp.einsum("mqkgd,mtkd->mkgqt", dob, vb, preferred_element_type=F32)
    inner = jnp.sum(soft * dp, axis=-1, keepdims=True)
    ds = (soft * (dp - inner)).astype(BF)
    dqr = jnp.einsum("mkgqt,mtkd->mqkgd", ds, kr, preferred_element_type=F32) * scale
    dkr = jnp.einsum("mkgqt,mqkgd->mtkd", ds, qr, preferred_element_type=F32) * scale
    dv = jnp.einsum("mkgqt,mqkgd->mtkd", soft_low, dob, preferred_element_type=F32)
    dvb = dv.reshape(total, KV_HEADS * HEAD_DIM).astype(BF)
    dq = rotate(dqr.reshape(micro, slots, HEADS, HEAD_DIM), cosine, sine, -1.0)
    dq = dq.reshape(total, HEADS * HEAD_DIM).astype(BF)
    dk = rotate(dkr, cosine, sine, -1.0).reshape(total, KV_HEADS * HEAD_DIM).astype(BF)
    dh1 = mm_t(dq, w_q) + mm_t(dk, w_k) + mm_t(dvb, w_v)
    back, gain_one = norm_back(x, r1, gains_full[0], dh1)
    input_gradient = send_home((dh + back).astype(BF))
    pieces = []
    for left, right, count in (
        (a1, dq, q_cols), (a1, dk, k_cols), (a1, dvb, k_cols), (ob, dhb, q_cols)
    ):
        pieces.append(t_mm(left, right).reshape(model, bins, count))
    attn_grads = jnp.transpose(jnp.concatenate(pieces, axis=2), (1, 0, 2))
    moment_zero = jnp.concatenate(
        [query_moment, key_moment, value_moment, output_moment], axis=1
    )
    spot = (b, f * rows_own, 0)
    here = lax.dynamic_slice(attn_grads, spot, (1, rows_own, width)) + moment_zero
    attn_grads = lax.dynamic_update_slice(attn_grads, here, spot).astype(BF)
    part_zero = reduce_blocks(attn_grads[None], 0, bins, fsdp, b, f)

    gain_sum = jnp.stack([gain_one, gain_two])
    for bit in bits_of(bins):
        gain_sum = gain_sum + swap(gain_sum, "bins", bins, bit)
    for bit in bits_of(fsdp):
        gain_sum = gain_sum + swap(gain_sum, "fsdp", fsdp, bit)
    gain_own = lax.dynamic_slice_in_dim(gain_sum, f * rows_own, rows_own, 1)

    split = fsdp // 4
    owner = f // split
    state = (0.5 * jnp.where(owner == 0, part_zero, part_one)).astype(BF)
    half = state.shape[0] // 2
    parts = [
        gather_bins(state[start : start + half], bins, b, order)
        for start, order in zip((0, half), bin_orders(bins))
    ]
    state = jnp.concatenate(parts, axis=1)
    for bit in bits_of(split):
        other = swap(state, "fsdp", fsdp, bit)
        flag = (f & bit) != 0
        state = jnp.concatenate(
            [jnp.where(flag, other, state), jnp.where(flag, state, other)], axis=1
        )

    kind = jnp.stack([jnp.where(owner == 0, 1 + (f & 1), 0), b]).astype(jnp.int32)
    ortho = newton(kind, state)
    other = swap(ortho, "fsdp", fsdp, 1)
    lane = jnp.arange(width, dtype=jnp.int32)
    first_core = (lane < edges[2]).astype(jnp.int32)
    ortho = jnp.where((owner == 0) & (first_core == (f & 1)), other, ortho)

    def spread(block):
        block = block.reshape(fsdp, rows_own, width)
        low = f % split
        pieces = [pick(block, f, 0)]
        for k in range(1, 4):
            sent = pick(block, (owner ^ k) * split + low, 0)
            pieces.append(swap(sent, "fsdp", fsdp, k * split))
        return [item.astype(F32) for item in ordered(pieces, owner)]

    states = spread(pick(state, b, 0))
    orthos = spread(ortho)
    full = {"q": (model, HEADS * HEAD_DIM), "k": (model, KV_HEADS * HEAD_DIM)}
    kv_rate = -math.sqrt(max(1.0, full["k"][0] / full["k"][1]))
    down_rate = -math.sqrt(max(1.0, down_weight.shape[0] * bins / model))
    gate_rate = -math.sqrt(max(1.0, model / (gate_weight.shape[1] * bins)))
    q_rate = -math.sqrt(max(1.0, full["q"][0] / full["q"][1]))
    rates = (q_rate, kv_rate, kv_rate, q_rate, gate_rate, gate_rate, down_rate)

    def unpack(blocks_now):
        cut = [blocks_now[0][:, edges[i] : edges[i + 1]] for i in range(4)]
        return cut + [blocks_now[1], blocks_now[2], blocks_now[3].T]

    outs = [block_output, input_gradient]
    for value, step, rate in zip(unpack(states), unpack(orthos), rates):
        outs += [value, rate * step]
    gain_rate = 0.1 / math.sqrt(micro * bins * fsdp * slots)
    for moment, grad in zip((attention_moment, feedforward_moment), gain_own):
        value = 0.5 * moment + 0.5 * grad
        outs += [value, -gain_rate * value]
    return tuple(outs)


def solution(mesh):
    rows = P(None, "fsdp", "bins", None)
    matrix = P("fsdp", "bins")
    turned = P("bins", "fsdp")
    vector = P("fsdp")
    params = (matrix,) * 6 + (turned, vector, vector)
    doubled = ()
    for spec in params:
        doubled += (spec, spec)
    return jax.shard_map(
        on_device,
        mesh=mesh,
        in_specs=(rows, rows, P(None, "fsdp", "bins"), rows, rows) + params + params,
        out_specs=(rows, rows) + doubled,
        check_vma=False,
    )
```

```python
import math

import jax
import jax.numpy as jnp
from jax import lax
from jax.experimental import pallas as pl
from jax.experimental.pallas import tpu as pltpu
from jax.sharding import PartitionSpec as P

HEADS = 9
KV_HEADS = 3
HEAD_DIM = 64
GROUPS = HEADS // KV_HEADS
NS_STEPS = 5
EPSILON = 1e-05
NEGATIVE = -1e30
ROPE_BASE = 10000.0
COEFF_A = 3.4445
COEFF_B = -4.775
COEFF_C = 2.0315
BF = jnp.bfloat16
F32 = jnp.float32


def dot(left, right, dims):
    return lax.dot_general(left, right, (dims, ((), ())), preferred_element_type=F32)


def mm(left, right):
    return dot(left, right, ((left.ndim - 1,), (0,)))


def mm_t(left, right):
    return dot(left, right, ((left.ndim - 1,), (1,)))


def t_mm(left, right):
    return dot(left, right, ((0,), (0,)))


def swap(value, axis, count, step, keep=None):
    pairs = [(i, i ^ step) for i in range(count) if keep is None or keep(i ^ step)]
    return lax.ppermute(value, axis, pairs)


def bits_of(count):
    return [1 << i for i in range(count.bit_length() - 1)]


def ordered(pieces, index):
    result = list(pieces)
    for bit in bits_of(len(pieces)):
        flag = (index & bit) != 0
        result = [jnp.where(flag, result[j ^ bit], result[j]) for j in range(len(result))]
    return result


def join(mine, other, flag):
    return jnp.stack([jnp.where(flag, other, mine), jnp.where(flag, mine, other)])


def after(value, *others):
    return lax.optimization_barrier((value,) + others)[0]


def bin_orders(bins):
    bits = bits_of(bins)
    half = len(bits) // 2
    return bits, bits[half:] + bits[:half]


def gather_bins(first, second, bins, stages=None):
    orders = bin_orders(bins)
    parts = [first, second]
    for pair in zip(*orders):
        parts = [
            jnp.stack([part, swap(part, "bins", bins, bit)]) for part, bit in zip(parts, pair)
        ]
        if stages is not None:
            stages.append(parts)
    result = []
    for part, order in zip(parts, orders):
        held = list(reversed(order))
        shape = part.shape[len(order) :]
        axes = [held.index(bit) for bit in sorted(order, reverse=True)]
        axes += range(len(order), part.ndim)
        result.append(jnp.transpose(part, axes).reshape((bins,) + shape))
    return jnp.concatenate(result, axis=1)


def gather_chips(piece, fsdp, f):
    chips = fsdp // 2
    pieces = [piece] + [swap(piece, "fsdp", fsdp, 2 * k) for k in range(1, chips)]
    pieces = ordered(pieces, f // 2)
    return jnp.stack(pieces[: chips // 2]), jnp.stack(pieces[chips // 2 :])


def gather_cores(own, fsdp, f):
    bins, chips, rows, width = own.shape
    other = swap(own, "fsdp", fsdp, 1)
    both = jnp.stack(ordered([own, other], f & 1), axis=2)
    return both.reshape(bins, fsdp * rows, width)


def add_low(left, right):
    return (left.astype(F32) + right.astype(F32)).astype(BF)


def pick(value, index, axis):
    return lax.dynamic_index_in_dim(value, index, axis, keepdims=False)


def reduce_blocks(kept, given, first, bins, fsdp, f, stages, beside=None):
    count, _, _, width = kept.shape
    split = fsdp // 4
    bits = bits_of(split)[::-1]
    grads = add_low(kept, swap(given, "fsdp", fsdp, bits[0]))
    for bit in bits[1:]:
        view = grads.reshape(count, bins, 2, grads.shape[2] // 2, width)
        flag = jnp.where((f & bit) != 0, 1, 0)
        got = swap(pick(view, 1 - flag, 2), "fsdp", fsdp, bit)
        grads = add_low(pick(view, flag, 2), got)
    if beside is not None:
        grads = after(grads, beside("fsdp", fsdp, 1))
    stages.append(grads)
    half = grads.shape[2] // 2
    orders = bin_orders(bins)
    parts, left = [], []
    for start, order in zip((0, half), orders):
        part = grads[:, :, start : start + half]
        parts.append(part.reshape((count,) + (2,) * len(order) + (half, width)))
        left.append(sorted(order, reverse=True))
    for pair in zip(*orders):
        for i, bit in enumerate(pair):
            where = 1 + left[i].index(bit)
            got = swap(lax.index_in_dim(parts[i], 1, where, False), "bins", bins, bit)
            parts[i] = add_low(lax.index_in_dim(parts[i], 0, where, False), got)
            left[i].remove(bit)
        if beside is not None:
            done = [beside("bins", bins, bit) for bit in sorted(set(pair))]
            parts = [after(part, *done) for part in parts]
        stages.append(tuple(parts))
    part = jnp.concatenate(parts, axis=1)
    owner = f // split
    last = count - 1
    total = pick(part, jnp.clip(owner - first, 0, last), 0).astype(F32)
    for k in range(1, 4):
        sent = pick(part, jnp.clip((owner ^ k) - first, 0, last), 0)
        got = swap(
            sent, "fsdp", fsdp, k * split, lambda t: first <= t // split < first + count
        )
        total = total + got.astype(F32)
    return total


def route_kernel(own_ref, slot_ref, tok_ref, cot_ref, tok_out, cot_out, map_out):
    slots, model = tok_ref.shape[2:]
    bins, _, cap, wide = tok_out.shape
    shift = slots.bit_length() - 1
    high = max(bins, 8)
    row_of = lax.broadcasted_iota(jnp.int32, (slots, slots), 0)
    col_of = lax.broadcasted_iota(jnp.int32, (slots, slots), 1)
    earlier = jnp.where(row_of < col_of, 1.0, 0.0).astype(BF)
    bin_of = lax.broadcasted_iota(jnp.int32, (high, slots), 0)
    slot = slot_ref[0]
    valid = slot >= 0
    safe = jnp.where(valid, slot, 0)
    relative = jnp.where(valid, (safe >> shift) ^ own_ref[0], high)
    onehot = jnp.where(bin_of == relative, 1.0, 0.0)
    before = mm(onehot.astype(BF), earlier)
    rank = jnp.sum(before * onehot, axis=0, keepdims=True).astype(jnp.int32)
    place = jnp.where(valid, relative * cap + rank, slots)
    send = jnp.where(row_of == place, 1.0, 0.0)
    map_out[0] = send.astype(BF)
    mark = jnp.where(valid, (safe & (slots - 1)) + 1, 0).astype(F32)
    marks = jnp.sum(send * mark, axis=1, keepdims=True)
    marks = jnp.broadcast_to(marks, (slots, wide - model)).astype(BF)
    tok = mm(send.astype(BF), tok_ref[0, 0]).astype(BF)
    cot = mm(send.astype(BF), cot_ref[0, 0]).astype(BF)
    for k in range(bins):
        rows = slice(k * cap, (k + 1) * cap)
        tok_out[k, 0, :, :model] = tok[rows]
        tok_out[k, 0, :, model:] = marks[rows]
        cot_out[k, 0] = cot[rows]


def vmem_specs(count):
    return [pl.BlockSpec(memory_space=pltpu.VMEM)] * count


def route(own, slot_rows, tokens, cotangent, bins):
    micro, _, slots, model = tokens.shape
    cap = slots // bins
    wide = model + (-model - 1) % 128 + 1
    block = pl.BlockSpec((1, 1, slots, model), lambda i: (i, 0, 0, 0))
    return pl.pallas_call(
        route_kernel,
        grid=(micro,),
        in_specs=[
            pl.BlockSpec(memory_space=pltpu.SMEM),
            pl.BlockSpec((1, 1, slots), lambda i: (i, 0, 0)),
            block,
            block,
        ],
        out_specs=[
            pl.BlockSpec((bins, 1, cap, wide), lambda i: (0, i, 0, 0)),
            pl.BlockSpec((bins, 1, cap, model), lambda i: (0, i, 0, 0)),
            pl.BlockSpec((1, slots, slots), lambda i: (i, 0, 0)),
        ],
        out_shape=[
            jax.ShapeDtypeStruct((bins, micro, cap, wide), BF),
            jax.ShapeDtypeStruct((bins, micro, cap, model), BF),
            jax.ShapeDtypeStruct((micro, slots, slots), BF),
        ],
        name="route",
    )(own, slot_rows, tokens, cotangent)


def unroute_kernel(*refs):
    map_ref = refs[0]
    out_one, out_two, home_ref = refs[-3:]
    pieces = refs[1:-3]
    cap = pieces[0].shape[2]
    for index, out in enumerate((out_one, out_two)):
        for k, piece in enumerate(pieces):
            home_ref[k * cap : (k + 1) * cap, :] = piece[index, 0]
        out[0, 0] = t_mm(map_ref[0], home_ref[...]).astype(BF)


def unroute(send_map, pieces):
    micro, slots, _ = send_map.shape
    cap, model = pieces[0].shape[2:]
    out = jax.ShapeDtypeStruct((micro, 1, slots, model), BF)
    block = pl.BlockSpec((1, 1, slots, model), lambda i: (i, 0, 0, 0))
    return pl.pallas_call(
        unroute_kernel,
        grid=(micro,),
        in_specs=[pl.BlockSpec((1, slots, slots), lambda i: (i, 0, 0))]
        + [pl.BlockSpec((2, 1, cap, model), lambda i: (0, i, 0, 0))] * len(pieces),
        out_specs=[block, block],
        out_shape=[out, out],
        scratch_shapes=[pltpu.VMEM((slots, model), BF)],
        name="unroute",
    )(send_map, *pieces)


def split_rows(acc_ref, own_ref, keep_ref, give_ref, index, start, width):
    half = keep_ref.shape[-2]
    mine = pl.ds(pl.multiple_of(own_ref[2] * half, 8), half)
    other = pl.ds(pl.multiple_of((1 - own_ref[2]) * half, 8), half)
    keep_ref[index] = acc_ref[mine, start : start + width].astype(BF)
    give_ref[index] = acc_ref[other, start : start + width].astype(BF)


def add_moment(acc_ref, own_ref, moment, start, width):
    high = moment.shape[0]
    if high % 8 == 0:
        rows = pl.ds(pl.multiple_of(own_ref[1] * high, 8), high)
        acc_ref[rows, start : start + width] += moment
        return
    for i in range(acc_ref.shape[0] // high):

        @pl.when(own_ref[1] == i)
        def _():
            acc_ref[i * high : (i + 1) * high, start : start + width] += moment


def give_back(values, land_ref, back_ref, m):
    bins, _, cap, _ = back_ref.shape
    back = mm(land_ref, values).astype(BF)
    for k in range(bins):
        back_ref[k, m] = back[k * cap : (k + 1) * cap]


def feed_kernel(own_ref, a2_ref, up_grad_ref, w_ref, moment_ref, h_ref, land_ref,
                dh2_ref, keep_ref, give_ref, back_ref,
                a2t_ref, gt_ref, act_ref, du_ref, acc_ref, y_ref):
    step = pl.program_id(0)
    tokens = a2_ref.shape[0]
    chunk = 256

    @pl.when(step == 0)
    def _():
        a2t_ref[...] = a2_ref[...].T
        gt_ref[...] = up_grad_ref[...].T
        y_ref[...] = h_ref[...]
        dh2_ref[...] = jnp.zeros_like(dh2_ref)

    width = w_ref.shape[3] // 3
    w_both = w_ref[0, 0, :, : 2 * width]
    w_down = w_ref[0, 0, :, 2 * width :]
    for start in range(0, tokens, chunk):
        rows = pl.ds(start, chunk)
        a2 = a2_ref[rows, :]
        both = mm(a2, w_both)
        gate = both[:, :width]
        up = both[:, width:]
        dact = mm(up_grad_ref[rows, :], w_down)
        sig = 1.0 / (1.0 + jnp.exp(-gate))
        silu = gate * sig
        act = (silu * up).astype(BF)
        dgate = (dact * up * sig * (1.0 + gate * (1.0 - sig))).astype(BF)
        dup = (dact * silu).astype(BF)
        act_ref[rows, :] = act
        du_ref[rows, :width] = dgate
        du_ref[rows, width:] = dup
        y_ref[rows, :] += mm_t(act, w_down)
        dh2_ref[rows, :] += mm_t(du_ref[rows, :], w_both)
    acc_ref[:, : 2 * width] = mm(a2t_ref[...], du_ref[...])
    acc_ref[:, 2 * width :] = mm(gt_ref[...], act_ref[...])

    @pl.when(step == 0)
    def _():
        for index in range(3):
            add_moment(acc_ref, own_ref, moment_ref[index], index * width, width)

    for index in range(3):
        split_rows(
            acc_ref, own_ref, keep_ref, give_ref, (index, 0), index * width, width
        )

    @pl.when(step == pl.num_programs(0) - 1)
    def _():
        micro, slots, _ = land_ref.shape
        for m in range(micro):
            rows = slice(m * slots, (m + 1) * slots)
            give_back(y_ref[rows, :].astype(BF), land_ref[m], back_ref, m)


def feed_forward_back(own, a2, up_grad, weights, moments, h, land):
    tokens, model = a2.shape
    _, bins, _, width = weights.shape
    width = width // 3
    micro, slots, _ = land.shape
    cap = slots // bins
    whole = pl.BlockSpec((tokens, model), lambda i, own_ref: (0, 0))
    halves = pl.BlockSpec((3, 1, model // 2, width), lambda i, own_ref: (0, i, 0, 0))
    block = pl.BlockSpec((1, 1, model, 3 * width), lambda i, own_ref: (0, i, 0, 0))
    return pl.pallas_call(
        feed_kernel,
        grid_spec=pltpu.PrefetchScalarGridSpec(
            num_scalar_prefetch=1,
            grid=(bins,),
            in_specs=[
                whole,
                whole,
                block,
                pl.BlockSpec(moments.shape, lambda i, own_ref: (0, 0, 0)),
                whole,
                pl.BlockSpec(land.shape, lambda i, own_ref: (0, 0, 0)),
            ],
            out_specs=[
                whole,
                halves,
                halves,
                pl.BlockSpec((bins, micro, cap, model), lambda i, own_ref: (0, 0, 0, 0)),
            ],
            scratch_shapes=[
                pltpu.VMEM((model, tokens), BF),
                pltpu.VMEM((model, tokens), BF),
                pltpu.VMEM((tokens, width), BF),
                pltpu.VMEM((tokens, 2 * width), BF),
                pltpu.VMEM((model, 3 * width), F32),
                pltpu.VMEM((tokens, model), F32),
            ],
        ),
        out_shape=[
            jax.ShapeDtypeStruct((tokens, model), F32),
            jax.ShapeDtypeStruct((3, bins, model // 2, width), BF),
            jax.ShapeDtypeStruct((3, bins, model // 2, width), BF),
            jax.ShapeDtypeStruct((bins, micro, cap, model), BF),
        ],
        name="feed",
    )(own, a2, up_grad, weights, moments, h, land)


def newton_kernel(kind_ref, state_ref, out_ref, z_ref, zb_ref, a_ref, ab_ref, pb_ref):
    bins, size, width = state_ref.shape
    quarter = width * 3 // 8
    eighth = width // 8
    groups = [(i, min(128, size - i)) for i in range(0, size, 128)]
    chunks = [(i, min(384, size - i)) for i in range(0, size, 384)]

    def run(wide, fetch):
        cols = wide * bins
        half = cols // 2
        total = jnp.zeros((), F32)
        for j in range(bins):
            piece = fetch(j)
            z_ref[:, j * wide : (j + 1) * wide] = piece
            total = total + jnp.sum(piece * piece)
        scale = 1.0 / (jnp.sqrt(jnp.full((1, 1), total, F32)) + 1e-07)
        for start, high in chunks:
            rows = slice(start, start + high)
            value = z_ref[rows, :cols] * scale
            z_ref[rows, :cols] = value
            zb_ref[rows, :cols] = value.astype(BF)

        def diagonal(ref, target, start, high):
            downs, acrosses = [], []
            for spot, count in groups:
                if start <= spot < start + high:
                    rows = slice(spot, spot + count)
                    tile = ref[spot - start : spot - start + count, rows]
                    row_of = lax.broadcasted_iota(jnp.int32, (count, count), 0)
                    eye = row_of == lax.broadcasted_iota(jnp.int32, (count, count), 1)
                    value = jnp.where(eye, tile, 0.0)
                    target[rows, rows] = jnp.where(eye, 0.0, tile).astype(BF)
                    downs.append(jnp.sum(value, axis=1, keepdims=True))
                    acrosses.append(jnp.sum(value, axis=0, keepdims=True))
            down = downs[0] if len(downs) == 1 else jnp.concatenate(downs, axis=0)
            return down, acrosses

        def step(index, carry):
            downs, across = [], []
            for start, high in chunks:
                rows = slice(start, start + high)
                gram = mm_t(zb_ref[rows, :cols], zb_ref[:, :cols])
                a_ref[rows, :] = gram
                ab_ref[rows, :] = gram.astype(BF)
                down, parts = diagonal(gram, ab_ref, start, high)
                downs.append(down)
                across += parts
            across = jnp.concatenate(across, axis=1)
            diags = []
            for (start, high), down in zip(chunks, downs):
                rows = slice(start, start + high)
                square = mm(ab_ref[rows, :], ab_ref[...])
                factor = (COEFF_B + COEFF_C * down) + COEFF_C * across
                poly = a_ref[rows, :] * factor + COEFF_C * square
                pb_ref[rows, :] = poly.astype(BF)
                diag, _ = diagonal(poly, pb_ref, start, high)
                diags.append(COEFF_A + diag - COEFF_C * down * down)
            for (start, high), diag in zip(chunks, diags):
                rows = slice(start, start + high)
                value = diag * z_ref[rows, :cols] + mm(pb_ref[rows, :], zb_ref[:, :cols])
                z_ref[rows, :cols] = value
            for start, high in chunks:
                rows = slice(start, start + high)
                zb_ref[rows, :cols] = z_ref[rows, :cols].astype(BF)
            return carry

        lax.fori_loop(0, NS_STEPS, step, 0)

    def keep_lanes(first, wide, low, high):
        lane = lax.broadcasted_iota(jnp.int32, (size, wide), 1) + first
        return (lane >= low) & (lane < high)

    def put(first, wide, low, high):
        keep = keep_lanes(first, wide, low, high)
        old = out_ref[:, first : first + wide].astype(F32)
        mine = zb_ref[:, :wide].astype(F32)
        out_ref[:, first : first + wide] = jnp.where(keep, mine, old).astype(BF)

    kind = kind_ref[0]

    @pl.when(kind == 0)
    def _():
        run(width, lambda j: state_ref[j].astype(F32))
        out_ref[...] = zb_ref[:, :width]

    large = 256 if width == 384 else width
    small = 128 if width == 384 else width
    middle = 128 if width == 384 else 0
    k_low = jnp.where(kind == 1, quarter, quarter + eighth)

    @pl.when(kind != 0)
    def _():
        out_ref[...] = jnp.zeros_like(out_ref)

        def large_piece(j):
            low = state_ref[j, :, :large].astype(F32)
            low = jnp.where(keep_lanes(0, large, 0, quarter), low, 0.0)
            high = state_ref[j, :, width - large :].astype(F32)
            high = jnp.where(
                keep_lanes(width - large, large, width - quarter, width), high, 0.0
            )
            return jnp.where(kind == 1, low, high)

        run(large, large_piece)

        @pl.when(kind == 1)
        def _():
            put(0, large, 0, quarter)

        @pl.when(kind != 1)
        def _():
            put(width - large, large, width - quarter, width)

        keep = keep_lanes(middle, small, k_low, k_low + eighth)
        run(
            small,
            lambda j: jnp.where(
                keep, state_ref[j, :, middle : middle + small].astype(F32), 0.0
            ),
        )
        put(middle, small, k_low, k_low + eighth)


def newton(kind, state):
    bins, size, width = state.shape
    cols = bins * width
    return pl.pallas_call(
        newton_kernel,
        in_specs=[
            pl.BlockSpec(memory_space=pltpu.SMEM),
            pl.BlockSpec(memory_space=pltpu.VMEM),
        ],
        out_specs=pl.BlockSpec(memory_space=pltpu.VMEM),
        out_shape=jax.ShapeDtypeStruct((size, width), BF),
        scratch_shapes=[
            pltpu.VMEM((size, cols), F32),
            pltpu.VMEM((size, cols), BF),
            pltpu.VMEM((size, size), F32),
            pltpu.VMEM((size, size), BF),
            pltpu.VMEM((size, size), BF),
        ],
        name="newton",
    )(kind, state)


def half_swap(value):
    lane = lax.broadcasted_iota(jnp.int32, value.shape, 1)
    low = (lane % HEAD_DIM) < HEAD_DIM // 2
    return jnp.where(low, pltpu.roll(value, 96, 1), pltpu.roll(value, 32, 1))


def twice(value, upper):
    lane = lax.broadcasted_iota(jnp.int32, value.shape, 1)
    keep = (lane >= HEAD_DIM) if upper else (lane < HEAD_DIM)
    part = jnp.where(keep, value, 0.0)
    return part + pltpu.roll(part, HEAD_DIM, 1)


def fold(value):
    return value + pltpu.roll(value, HEAD_DIM, 1)


PAIRS = (HEADS + 1) // 2
KV_PAIRS = (KV_HEADS + 1) // 2
Q_WIDE = PAIRS * 128
KV_WIDE = KV_PAIRS * 128
WIDE = Q_WIDE + 2 * KV_WIDE
SCALE = 1.0 / math.sqrt(HEAD_DIM)


def soft_rows(query, key, allowed):
    scores = jnp.where(allowed, mm_t(query, key) * SCALE, NEGATIVE)
    raised = jnp.exp(scores - jnp.max(scores, axis=1, keepdims=True))
    return raised * (1.0 / jnp.sum(raised, axis=1, keepdims=True))


def allow(seg_col, seg_row):
    size = seg_row.shape[1]
    row = lax.broadcasted_iota(jnp.int32, (size, size), 0)
    col = lax.broadcasted_iota(jnp.int32, (size, size), 1)
    return (seg_col == seg_row) & (col <= row)


def key_pair(qkv, base, kv):
    group = qkv[:, base + (kv // 2) * 128 : base + (kv // 2) * 128 + 128].astype(F32)
    return twice(group, kv % 2 == 1).astype(BF)


def masked_half(group, head):
    lane = lax.broadcasted_iota(jnp.int32, group.shape, 1)
    keep = (lane >= HEAD_DIM) if head % 2 else (lane < HEAD_DIM)
    return jnp.where(keep, group.astype(F32), 0.0).astype(BF)


def take_columns(w_ref, own, kind_start, cols, start, wide, bins):
    width = w_ref.shape[2]
    source = lax.broadcasted_iota(jnp.int32, (width, wide), 0)
    target = lax.broadcasted_iota(jnp.int32, (width, wide), 1) + start
    inside = (source >= kind_start) & (source < kind_start + cols)
    result = None
    for j in range(start // cols, min((start + wide - 1) // cols, bins - 1) + 1):
        chosen = inside & (source - kind_start == target - j * cols)
        part = mm(w_ref[own ^ j], jnp.where(chosen, 1.0, 0.0).astype(BF))
        result = part if result is None else result + part
    return result.astype(BF)


def attend_kernel(*refs):
    own_ref = refs[0]
    bins = (len(refs) - 21) // 2
    toks = refs[1 : 1 + bins]
    cots = refs[1 + bins : 1 + 2 * bins]
    (gain_in, w_ref, cos_ref, sin_ref, sc_ref, sr_ref,
     x_ref, g_ref, land_ref, a1_ref, qkv_ref, ob_ref, h_ref, a2_ref, wqkv_ref, wo_ref, gain_ref,
     got_ref, got2_ref, land_t) = refs[1 + 2 * bins :]
    slots, model = x_ref.shape
    cap = slots // bins
    width = w_ref.shape[2]
    q_cols = width * 3 // 8
    k_cols = width // 8

    @pl.when(pl.program_id(0) == 0)
    def _():
        row = lax.broadcasted_iota(jnp.int32, (model, model), 0)
        eye = row == lax.broadcasted_iota(jnp.int32, (model, model), 1)
        for i in range(2):
            column = gain_in[:, i : i + 1].astype(F32)
            gain_ref[i : i + 1, :] = jnp.sum(
                jnp.where(eye, column, 0.0), axis=0, keepdims=True
            )
        for tile in range(WIDE // 128):
            if tile < PAIRS:
                spot = (0, q_cols, tile * 128)
            elif tile < PAIRS + KV_PAIRS:
                spot = (q_cols, k_cols, (tile - PAIRS) * 128)
            else:
                spot = (q_cols + k_cols, k_cols, (tile - PAIRS - KV_PAIRS) * 128)
            wqkv_ref[:, tile * 128 : tile * 128 + 128] = take_columns(
                w_ref, own_ref[0], *spot, 128, bins
            )
        for tile in range(PAIRS):
            wo_ref[:, tile * 128 : tile * 128 + 128] = take_columns(
                w_ref, own_ref[0], q_cols + 2 * k_cols, q_cols, tile * 128, 128, bins
            )

    spot = lax.broadcasted_iota(jnp.int32, (cap, slots), 1)
    for k in range(bins):
        rows = slice(k * cap, (k + 1) * cap)
        place = toks[k][0, :, model : model + 1].astype(F32).astype(jnp.int32) - 1
        land = jnp.where(spot == place, 1.0, 0.0).astype(BF)
        land_t[rows, :] = land
        got_ref[rows, :] = toks[k][0, :, :model]
        got2_ref[rows, :] = cots[k][0]
    land_ref[0] = land_t[...]
    x = t_mm(land_t[...], got_ref[...])
    x_ref[...] = x.astype(BF)
    g_ref[...] = t_mm(land_t[...], got2_ref[...]).astype(BF)
    r1 = lax.rsqrt(jnp.mean(x * x, axis=1, keepdims=True) + EPSILON)
    a1 = (x * r1 * gain_ref[0:1, :]).astype(BF)
    a1_ref[...] = a1
    cosine = cos_ref[...]
    sine = sin_ref[...]
    for pair in range(WIDE // 128):
        lanes = slice(pair * 128, pair * 128 + 128)
        value = mm(a1, wqkv_ref[:, lanes])
        if pair * 128 < Q_WIDE + KV_WIDE:
            value = value * cosine + half_swap(value) * sine
        qkv_ref[:, lanes] = value.astype(BF)
    allowed = allow(sc_ref[0], sr_ref[0])
    keys = [key_pair(qkv_ref, Q_WIDE, kv) for kv in range(KV_HEADS)]
    values = [key_pair(qkv_ref, Q_WIDE + KV_WIDE, kv) for kv in range(KV_HEADS)]
    for pair in range(PAIRS):
        lanes = slice(pair * 128, pair * 128 + 128)
        group = qkv_ref[:, lanes]
        out = None
        for head in range(2 * pair, min(2 * pair + 2, HEADS)):
            kv = head // GROUPS
            soft = soft_rows(masked_half(group, head), keys[kv], allowed)
            part = mm(soft.astype(BF), values[kv])
            lane = lax.broadcasted_iota(jnp.int32, part.shape, 1)
            out = part if out is None else jnp.where(lane < HEAD_DIM, out, part)
        ob_ref[:, lanes] = out.astype(BF)
    h = x + mm(ob_ref[:, :model], wo_ref[:, :model])
    h_ref[...] = h
    r2 = lax.rsqrt(jnp.mean(h * h, axis=1, keepdims=True) + EPSILON)
    a2_ref[...] = (h * r2 * gain_ref[1:2, :]).astype(BF)


def row_spec(slots, width):
    return pl.BlockSpec((slots, width), lambda i: (i, 0))


def full_spec(shape):
    return pl.BlockSpec(shape, lambda i: (0,) * len(shape))


def attend(own, toks, cots, gains, weights, cosine, sine, seg_col, seg_row):
    bins, model, _ = weights.shape
    micro, _, slots = seg_row.shape
    total = micro * slots
    cap = slots // bins
    row_shapes = ((model, BF), (WIDE, BF), (Q_WIDE, BF), (model, F32), (model, BF))
    wide = toks[0].shape[2]
    return pl.pallas_call(
        attend_kernel,
        grid=(micro,),
        in_specs=[pl.BlockSpec(memory_space=pltpu.SMEM)]
        + [pl.BlockSpec((1, cap, wide), lambda i: (i, 0, 0))] * bins
        + [pl.BlockSpec((1, cap, model), lambda i: (i, 0, 0))] * bins
        + [
            full_spec(gains.shape), full_spec(weights.shape),
            row_spec(slots, 128), row_spec(slots, 128),
            pl.BlockSpec((1, slots, 1), lambda i: (i, 0, 0)),
            pl.BlockSpec((1, 1, slots), lambda i: (i, 0, 0)),
        ],
        out_specs=[
            row_spec(slots, model), row_spec(slots, model),
            pl.BlockSpec((1, slots, slots), lambda i: (i, 0, 0)),
        ]
        + [row_spec(slots, wide) for wide, _ in row_shapes]
        + [full_spec((model, WIDE)), full_spec((model, Q_WIDE)), full_spec((2, model))],
        out_shape=[
            jax.ShapeDtypeStruct((total, model), BF),
            jax.ShapeDtypeStruct((total, model), BF),
            jax.ShapeDtypeStruct((micro, slots, slots), BF),
        ]
        + [jax.ShapeDtypeStruct((total, wide), kind) for wide, kind in row_shapes]
        + [
            jax.ShapeDtypeStruct((model, WIDE), BF),
            jax.ShapeDtypeStruct((model, Q_WIDE), BF),
            jax.ShapeDtypeStruct((2, model), F32),
        ],
        scratch_shapes=[
            pltpu.VMEM((slots, model), BF),
            pltpu.VMEM((slots, model), BF),
            pltpu.VMEM((slots, slots), BF),
        ],
        name="attend",
    )(own, *toks, *cots, gains, weights, cosine, sine, seg_col, seg_row)


def attend_back_kernel(own_ref, x_ref, gain_ref, wqkv_ref, wo_ref, cos_ref, sin_ref, sc_ref,
                       sr_ref, a1_ref, qkv_ref, ob_ref, h_ref, dh2_ref, g_ref, land_ref,
                       moment_ref, back_ref, gains_ref, keep_ref, give_ref,
                       a1_all, ob_all, d_all, dhb_all, acc_ref):
    step = pl.program_id(0)
    slots, model = x_ref.shape
    rows = pl.ds(pl.multiple_of(step * slots, slots), slots)

    @pl.when(step == 0)
    def _():
        gains_ref[...] = jnp.zeros_like(gains_ref)

    h = h_ref[...]
    dh2 = dh2_ref[...]
    r2 = lax.rsqrt(jnp.mean(h * h, axis=1, keepdims=True) + EPSILON)
    scaled = dh2 * gain_ref[1:2, :]
    inner = jnp.mean(scaled * h, axis=1, keepdims=True)
    dh = g_ref[...].astype(F32) + r2 * scaled - h * (r2 * r2 * r2 * inner)
    gains_ref[1:2, :] += jnp.sum(dh2 * h * r2, axis=0, keepdims=True)
    dhb = dh.astype(BF)
    dhb_all[rows, :] = dhb
    a1_all[:, rows] = a1_ref[...].T
    ob_all[:, rows] = ob_ref[:, :model].T
    allowed = allow(sc_ref[0], sr_ref[0])
    keys = [key_pair(qkv_ref, Q_WIDE, kv) for kv in range(KV_HEADS)]
    values = [key_pair(qkv_ref, Q_WIDE + KV_WIDE, kv) for kv in range(KV_HEADS)]
    cosine = cos_ref[...]
    sine = sin_ref[...]
    dkeys = [None] * KV_HEADS
    dvalues = [None] * KV_HEADS
    for pair in range(PAIRS):
        group = qkv_ref[:, pair * 128 : pair * 128 + 128]
        top = min(pair * 128 + 128, model)
        dob = mm_t(dhb, wo_ref[pair * 128 : top, :model])
        if top < pair * 128 + 128:
            dob = jnp.concatenate([dob, jnp.zeros((slots, pair * 128 + 128 - top), F32)], axis=1)
        dob = dob.astype(BF)
        out = None
        for head in range(2 * pair, min(2 * pair + 2, HEADS)):
            kv = head // GROUPS
            query = masked_half(group, head)
            soft = soft_rows(query, keys[kv], allowed)
            mine = masked_half(dob, head)
            dp = mm_t(mine, values[kv])
            ds = (soft * (dp - jnp.sum(soft * dp, axis=1, keepdims=True))).astype(BF)
            part = mm(ds, keys[kv])
            lane = lax.broadcasted_iota(jnp.int32, part.shape, 1)
            out = part if out is None else jnp.where(lane < HEAD_DIM, out, part)
            dk = t_mm(ds, query)
            dv = t_mm(soft.astype(BF), mine)
            dkeys[kv] = dk if dkeys[kv] is None else dkeys[kv] + dk
            dvalues[kv] = dv if dvalues[kv] is None else dvalues[kv] + dv
        if 2 * pair + 2 > HEADS:
            lane = lax.broadcasted_iota(jnp.int32, out.shape, 1)
            out = jnp.where(lane < HEAD_DIM, out, 0.0)
        out = out * SCALE
        out = out * cosine - half_swap(out) * sine
        d_all[rows, pair * 128 : pair * 128 + 128] = out.astype(BF)
    for pair in range(KV_PAIRS):
        lane = lax.broadcasted_iota(jnp.int32, (slots, 128), 1)

        def both(parts):
            low = fold(parts[2 * pair])
            high = fold(parts[2 * pair + 1]) if 2 * pair + 1 < KV_HEADS else 0.0
            return jnp.where(lane < HEAD_DIM, low, high)

        dk = both(dkeys) * SCALE
        dk = dk * cosine - half_swap(dk) * sine
        start = Q_WIDE + pair * 128
        d_all[rows, start : start + 128] = dk.astype(BF)
        start += KV_WIDE
        d_all[rows, start : start + 128] = both(dvalues).astype(BF)
    dh1 = mm_t(d_all[rows, :], wqkv_ref[...])
    x = x_ref[...].astype(F32)
    r1 = lax.rsqrt(jnp.mean(x * x, axis=1, keepdims=True) + EPSILON)
    scaled = dh1 * gain_ref[0:1, :]
    inner = jnp.mean(scaled * x, axis=1, keepdims=True)
    dx = dh + r1 * scaled - x * (r1 * r1 * r1 * inner)
    gains_ref[0:1, :] += jnp.sum(dh1 * x * r1, axis=0, keepdims=True)
    give_back(dx.astype(BF), land_ref[0], back_ref, step)

    @pl.when(step == pl.num_programs(0) - 1)
    def _():
        width = acc_ref.shape[1]
        bins = keep_ref.shape[0]
        q_cols = width * 3 // 8
        k_cols = width // 8
        wide = 256 if width == 384 else width
        skip = width - wide
        spot = lax.broadcasted_iota(jnp.int32, (1, wide), 1)
        late = spot + skip - (q_cols + 2 * k_cols)
        for k in range(bins):
            j = own_ref[0] ^ k
            target = jnp.where(
                spot < q_cols,
                j * q_cols + spot,
                jnp.where(
                    spot < q_cols + k_cols,
                    Q_WIDE + j * k_cols + spot - q_cols,
                    jnp.where(
                        spot < q_cols + 2 * k_cols,
                        Q_WIDE + KV_WIDE + j * k_cols + spot - q_cols - k_cols,
                        -1,
                    ),
                ),
            )
            source = lax.broadcasted_iota(jnp.int32, (WIDE, wide), 0)
            chosen = mm(d_all[...], jnp.where(source == target, 1.0, 0.0).astype(BF))
            first = mm(a1_all[...], chosen.astype(BF))
            target = jnp.where(late >= 0, j * q_cols + late, -1)
            source = lax.broadcasted_iota(jnp.int32, (model, wide), 0)
            chosen = mm(dhb_all[...], jnp.where(source == target, 1.0, 0.0).astype(BF))
            second = mm(ob_all[...], chosen.astype(BF))
            if skip:
                acc_ref[:, :skip] = first[:, :skip]
                acc_ref[:, skip:wide] = first[:, skip:] + second[:, : wide - skip]
                acc_ref[:, wide:] = second[:, wide - skip :]
            else:
                acc_ref[...] = first + second
            if k == 0:
                add_moment(acc_ref, own_ref, moment_ref[...], 0, width)
            split_rows(acc_ref, own_ref, keep_ref, give_ref, k, 0, width)


def attend_back(own, x, gains, wqkv, wo, cosine, sine, seg_col, seg_row,
                a1, qkv, ob, h, dh2, g, land, moment, bins):
    total, model = x.shape
    micro, slots, _ = land.shape
    cap = slots // bins
    width = moment.shape[1]
    return pl.pallas_call(
        attend_back_kernel,
        grid=(micro,),
        in_specs=[
            pl.BlockSpec(memory_space=pltpu.SMEM),
            row_spec(slots, model), full_spec(gains.shape), full_spec(wqkv.shape),
            full_spec(wo.shape), row_spec(slots, 128), row_spec(slots, 128),
            pl.BlockSpec((1, slots, 1), lambda i: (i, 0, 0)),
            pl.BlockSpec((1, 1, slots), lambda i: (i, 0, 0)),
            row_spec(slots, model), row_spec(slots, WIDE), row_spec(slots, Q_WIDE),
            row_spec(slots, model), row_spec(slots, model), row_spec(slots, model),
            pl.BlockSpec((1, slots, slots), lambda i: (i, 0, 0)),
            full_spec(moment.shape),
        ],
        out_specs=[
            full_spec((bins, micro, cap, model)), full_spec((2, model)),
            full_spec((bins, model // 2, width)), full_spec((bins, model // 2, width)),
        ],
        out_shape=[
            jax.ShapeDtypeStruct((bins, micro, cap, model), BF),
            jax.ShapeDtypeStruct((2, model), F32),
            jax.ShapeDtypeStruct((bins, model // 2, width), BF),
            jax.ShapeDtypeStruct((bins, model // 2, width), BF),
        ],
        scratch_shapes=[
            pltpu.VMEM((model, total), BF),
            pltpu.VMEM((model, total), BF),
            pltpu.VMEM((total, WIDE), BF),
            pltpu.VMEM((total, model), BF),
            pltpu.VMEM((model, width), F32),
        ],
        name="attend_back",
    )(own, x, gains, wqkv, wo, cosine, sine, seg_col, seg_row,
      a1, qkv, ob, h, dh2, g, land, moment)


def rope_tables(positions):
    half_dim = HEAD_DIM // 2
    frequency = jnp.exp(
        -math.log(ROPE_BASE) * 2.0 * jnp.arange(half_dim, dtype=F32) / HEAD_DIM
    )
    angles = positions.reshape(-1).astype(F32)[:, None] * frequency
    cosine = jnp.cos(angles)
    sine = jnp.sin(angles)
    return (
        jnp.concatenate([cosine] * 4, axis=1),
        jnp.concatenate([-sine, sine, -sine, sine], axis=1),
    )


def slot_layout(lengths, starts, bin_slots):
    slot_index = jnp.arange(bin_slots, dtype=jnp.int32)
    inside = (
        (slot_index[:, None] >= starts[..., None, :])
        & (slot_index[:, None] < starts[..., None, :] + lengths[..., None, :])
    ).astype(jnp.int32)
    number = jnp.arange(lengths.shape[-1], dtype=jnp.int32)
    covered = jnp.minimum(jnp.sum(inside, axis=-1), 1)
    segment = jnp.sum(inside * number, axis=-1) + (1 - covered) * (
        lengths.shape[-1] + slot_index
    )
    first_slot = jnp.sum(inside * starts[..., None, :], axis=-1)
    return (segment, slot_index - first_slot)


def on_device(
    tokens, cotangent, token_slots, sequence_lengths, sequence_starts,
    query_weight, key_weight, value_weight, output_weight,
    gate_weight, up_weight, down_weight, attention_gain, feedforward_gain,
    query_moment, key_moment, value_moment, output_moment,
    gate_moment, up_moment, down_moment, attention_moment, feedforward_moment,
):
    bins = lax.axis_size("bins")
    fsdp = lax.axis_size("fsdp")
    b = lax.axis_index("bins")
    f = lax.axis_index("fsdp")
    micro, _, slots, model = tokens.shape
    total = micro * slots
    rows_own = query_weight.shape[0]
    q_cols = query_weight.shape[1]
    k_cols = key_weight.shape[1]
    split = fsdp // 4
    flag = jnp.where((f & (split // 2)) != 0, 1, 0)
    own = jnp.stack([b, f, flag]).astype(jnp.int32)

    block_zero = jnp.concatenate(
        [query_weight, key_weight, value_weight, output_weight], axis=1
    )[None]
    blocks = jnp.concatenate([gate_weight, up_weight, down_weight.T], axis=1)
    gain_lanes = jnp.pad(
        jnp.stack([attention_gain, feedforward_gain], axis=1), ((0, 0), (0, 126))
    )
    width = block_zero.shape[2]
    zero_chips = gather_chips(
        jnp.concatenate([block_zero[0], gain_lanes], axis=1), fsdp, f
    )
    gains_cols = jnp.concatenate([part[:, :, width:] for part in zero_chips])
    gains_cols = gather_cores(gains_cols[None], fsdp, f)[0]
    zero_chips = [part[:, :, :width] for part in zero_chips]

    tok_send, cot_send, send_map = route(
        own, token_slots, tokens, cotangent, bins
    )

    def exchange(pieces):
        return [pieces[0]] + [swap(pieces[k], "bins", bins, k) for k in range(1, bins)]

    toks = exchange(tok_send)
    feed_chips = gather_chips(after(blocks, tok_send), fsdp, f)
    zero_stages = []
    zero_bins = gather_bins(*zero_chips, bins, zero_stages)
    cots = exchange(after(cot_send, *zero_stages[0]))

    segment, position = slot_layout(sequence_lengths[:, 0, 0], sequence_starts[:, 0, 0], slots)
    cosine, sine = rope_tables(position)

    attn_w = gather_cores(zero_bins, fsdp, f)
    first, second = feed_chips
    feed_stages = []
    ahead = (zero_bins, *cots)
    feed_bins = gather_bins(after(first, *ahead), after(second, *ahead), bins, feed_stages)
    attn_w = after(attn_w, *feed_stages[0])

    edges = (0, q_cols, q_cols + k_cols, q_cols + 2 * k_cols, width)
    seg_col = segment[:, :, None]
    seg_row = segment[:, None, :]
    tables = (cosine, sine, seg_col, seg_row)
    x_low, g_low, land, a1, qkv, ob, h, a2, w_qkv, w_o, gains_full = attend(
        own, toks, cots, gains_cols, attn_w, *tables
    )
    feed_w = gather_cores(after(feed_bins, a2), fsdp, f)

    moments = jnp.stack([gate_moment, up_moment, down_moment.T])
    dh2, kept, given, back = feed_forward_back(own, a2, g_low, feed_w[None], moments, h, land)
    one_stages = []
    part_one = reduce_blocks(kept, given, 1, bins, fsdp, f, one_stages)
    back_one = back
    dh2 = after(dh2, one_stages[0])

    moment_zero = jnp.concatenate(
        [query_moment, key_moment, value_moment, output_moment], axis=1
    )
    back, gain_sum, kept, given = attend_back(
        own, x_low, gains_full, w_qkv, w_o, *tables,
        a1, qkv, ob, h, dh2, g_low, land, moment_zero, bins,
    )
    zero_stages = []
    sums = [gain_sum]
    summed = set()

    def beside(axis, count, bit):
        if (axis, bit) not in summed:
            summed.add((axis, bit))
            sums.append(sums[-1] + swap(sums[-1], axis, count, bit))
        return sums[-1]

    part_zero = reduce_blocks(kept[None], given[None], 0, bins, fsdp, f, zero_stages, beside)

    owner = f // split
    state = (0.5 * jnp.where(owner == 0, part_zero, part_one)).astype(BF)
    half = state.shape[0] // 2
    for bit in bits_of(fsdp):
        gain_sum = beside("fsdp", fsdp, bit)
    gain_own = lax.dynamic_slice_in_dim(gain_sum, f * rows_own, rows_own, 1)
    state = gather_bins(state[:half], state[half:], bins)
    home = exchange(after(jnp.concatenate([back_one[:, None], back[:, None]], axis=1), state))
    for bit in bits_of(split):
        state = jnp.concatenate([state, swap(state, "fsdp", fsdp, bit)], axis=1)

    kind = jnp.stack([jnp.where(owner == 0, 1 + (f & 1), 0), b]).astype(jnp.int32)
    ortho = newton(kind, state)
    other = swap(ortho, "fsdp", fsdp, 1)
    block_output, input_gradient = unroute(after(send_map, other), home)
    other = other.reshape(fsdp // 8, 2, -1, width)[:, ::-1].reshape(ortho.shape)
    lane = jnp.arange(width, dtype=jnp.int32)
    first_core = (lane < edges[2]).astype(jnp.int32)
    ortho = jnp.where((owner == 0) & (first_core == (f & 1)), other, ortho)

    def spread(block):
        block = block.reshape(fsdp, rows_own, width)
        low = f % split
        turn = low * 4
        pieces = [pick(block, f ^ turn, 0)]
        for k in range(1, 4):
            sent = pick(block, ((owner ^ k) * split + low) ^ turn, 0)
            pieces.append(swap(sent, "fsdp", fsdp, k * split))
        return [item.astype(F32) for item in ordered(pieces, owner)]

    states = spread(state[0])
    orthos = spread(ortho)
    full = {"q": (model, HEADS * HEAD_DIM), "k": (model, KV_HEADS * HEAD_DIM)}
    kv_rate = -math.sqrt(max(1.0, full["k"][0] / full["k"][1]))
    down_rate = -math.sqrt(max(1.0, down_weight.shape[0] * bins / model))
    gate_rate = -math.sqrt(max(1.0, model / (gate_weight.shape[1] * bins)))
    q_rate = -math.sqrt(max(1.0, full["q"][0] / full["q"][1]))
    rates = (q_rate, kv_rate, kv_rate, q_rate, gate_rate, gate_rate, down_rate)

    def unpack(blocks_now):
        cut = [blocks_now[0][:, edges[i] : edges[i + 1]] for i in range(4)]
        return cut + [blocks_now[1], blocks_now[2], blocks_now[3].T]

    outs = [block_output, input_gradient]
    for value, step, rate in zip(unpack(states), unpack(orthos), rates):
        outs += [value, rate * step]
    gain_rate = 0.1 / math.sqrt(micro * bins * fsdp * slots)
    for moment, grad in zip((attention_moment, feedforward_moment), gain_own):
        value = 0.5 * moment + 0.5 * grad
        outs += [value, -gain_rate * value]
    return tuple(outs)


def solution(mesh):
    rows = P(None, "fsdp", "bins", None)
    matrix = P("fsdp", "bins")
    turned = P("bins", "fsdp")
    vector = P("fsdp")
    params = (matrix,) * 6 + (turned, vector, vector)
    doubled = ()
    for spec in params:
        doubled += (spec, spec)
    return jax.shard_map(
        on_device,
        mesh=mesh,
        in_specs=(rows, rows, P(None, "fsdp", "bins"), rows, rows) + params + params,
        out_specs=(rows, rows) + doubled,
        check_vma=False,
    )
```

```python
import functools
import math

import jax
import jax.numpy as jnp
from jax import lax
from jax.experimental import pallas as pl
from jax.experimental.pallas import tpu as pltpu
from jax.sharding import PartitionSpec as P

HEADS = 9
KV_HEADS = 3
HEAD_DIM = 64
GROUPS = HEADS // KV_HEADS
NS_STEPS = 5
HIDDEN_RATIO = 1536 / 576
DOWN_RATE = math.sqrt(HIDDEN_RATIO)
EPSILON = 1e-05
NEGATIVE = -1e30
ROPE_BASE = 10000.0
COEFF_A = 3.4445
COEFF_B = -4.775
COEFF_C = 2.0315
BF = jnp.bfloat16
F32 = jnp.float32


def dot(left, right, dims):
    return lax.dot_general(left, right, (dims, ((), ())), preferred_element_type=F32)


def mm(left, right):
    return dot(left, right, ((left.ndim - 1,), (0,)))


def mm_t(left, right):
    return dot(left, right, ((left.ndim - 1,), (1,)))


def t_mm(left, right):
    return dot(left, right, ((0,), (0,)))


def swap(value, axis, count, step, keep=None):
    pairs = [(i, i ^ step) for i in range(count) if keep is None or keep(i ^ step)]
    return lax.ppermute(value, axis, pairs)


def bits_of(count):
    return [1 << i for i in range(count.bit_length() - 1)]


def ordered(pieces, index):
    result = list(pieces)
    for bit in bits_of(len(pieces)):
        flag = (index & bit) != 0
        result = [jnp.where(flag, result[j ^ bit], result[j]) for j in range(len(result))]
    return result


def join(mine, other, flag):
    return jnp.stack([jnp.where(flag, other, mine), jnp.where(flag, mine, other)])


def after(value, *others):
    return lax.optimization_barrier((value,) + others)[0]


def bin_orders(bins):
    bits = bits_of(bins)
    half = len(bits) // 2
    return bits, bits[half:] + bits[:half]


def gather_bins(first, second, bins, stages=None):
    orders = bin_orders(bins)
    parts = [first, second]
    for pair in zip(*orders):
        parts = [
            jnp.stack([part, swap(part, "bins", bins, bit)]) for part, bit in zip(parts, pair)
        ]
        if stages is not None:
            stages.append(parts)
    result = []
    for part, order in zip(parts, orders):
        held = list(reversed(order))
        shape = part.shape[len(order) :]
        axes = [held.index(bit) for bit in sorted(order, reverse=True)]
        axes += range(len(order), part.ndim)
        result.append(jnp.transpose(part, axes).reshape((bins,) + shape))
    return jnp.concatenate(result, axis=1)


def gather_chips(piece, fsdp, f):
    chips = fsdp // 2
    pieces = [piece] + [swap(piece, "fsdp", fsdp, 2 * k) for k in range(1, chips)]
    pieces = ordered(pieces, f // 2)
    return jnp.stack(pieces[: chips // 2]), jnp.stack(pieces[chips // 2 :])


def gather_cores(own, fsdp, f):
    bins, chips, rows, width = own.shape
    other = swap(own, "fsdp", fsdp, 1)
    both = jnp.stack(ordered([own, other], f & 1), axis=2)
    return both.reshape(bins, fsdp * rows, width)


def block_of(owner):
    if isinstance(owner, int):
        return owner ^ 1 if owner < 2 else owner
    return jnp.where(owner < 2, owner ^ 1, owner)


def add_low(left, right):
    return (left.astype(F32) + right.astype(F32)).astype(BF)


def pick(value, index, axis):
    return lax.dynamic_index_in_dim(value, index, axis, keepdims=False)


def reduce_blocks(kept, given, first, bins, fsdp, f, stages, beside=None):
    count, _, _, width = kept.shape
    split = fsdp // 4
    bits = bits_of(split)[::-1]
    grads = add_low(kept, swap(given, "fsdp", fsdp, bits[0]))
    for bit in bits[1:]:
        view = grads.reshape(count, bins, 2, grads.shape[2] // 2, width)
        flag = jnp.where((f & bit) != 0, 1, 0)
        got = swap(pick(view, 1 - flag, 2), "fsdp", fsdp, bit)
        grads = add_low(pick(view, flag, 2), got)
    if beside is not None:
        beside("fsdp", fsdp, 1, grads)
    stages.append(grads)
    half = grads.shape[2] // 2
    orders = bin_orders(bins)
    parts, left = [], []
    for start, order in zip((0, half), orders):
        part = grads[:, :, start : start + half]
        parts.append(part.reshape((count,) + (2,) * len(order) + (half, width)))
        left.append(sorted(order, reverse=True))
    for pair in zip(*orders):
        for i, bit in enumerate(pair):
            where = 1 + left[i].index(bit)
            got = swap(lax.index_in_dim(parts[i], 1, where, False), "bins", bins, bit)
            parts[i] = add_low(lax.index_in_dim(parts[i], 0, where, False), got)
            left[i].remove(bit)
        if beside is not None:
            parts = [after(part, beside()) for part in parts]
            beside("bins", bins, pair[0], parts[0])
        stages.append(tuple(parts))
    part = jnp.concatenate(parts, axis=1)
    owner = f // split
    last = count - 1
    total = pick(part, jnp.clip(block_of(owner) - first, 0, last), 0).astype(F32)
    for k in range(1, 4):
        sent = pick(part, jnp.clip(block_of(owner ^ k) - first, 0, last), 0)
        got = swap(
            sent,
            "fsdp",
            fsdp,
            k * split,
            lambda t: first <= block_of(t // split) < first + count,
        )
        total = total + got.astype(F32)
    return total


def route_kernel(own_ref, slot_ref, tok_ref, cot_ref, tok_out, cot_out, map_out):
    model, slots = tok_ref.shape[2:]
    bins, _, cap, wide = tok_out.shape
    shift = slots.bit_length() - 1
    high = max(bins, 8)
    row_of = lax.broadcasted_iota(jnp.int32, (slots, slots), 0)
    col_of = lax.broadcasted_iota(jnp.int32, (slots, slots), 1)
    earlier = jnp.where(row_of < col_of, 1.0, 0.0).astype(BF)
    bin_of = lax.broadcasted_iota(jnp.int32, (high, slots), 0)
    slot = slot_ref[0]
    valid = slot >= 0
    safe = jnp.where(valid, slot, 0)
    relative = jnp.where(valid, (safe >> shift) ^ own_ref[0], high)
    onehot = jnp.where(bin_of == relative, 1.0, 0.0)
    before = mm(onehot.astype(BF), earlier)
    rank = jnp.sum(before * onehot, axis=0, keepdims=True).astype(jnp.int32)
    place = jnp.where(valid, relative * cap + rank, slots)
    send = jnp.where(row_of == place, 1.0, 0.0)
    map_out[0] = send.astype(BF)
    mark = jnp.where(valid, (safe & (slots - 1)) + 1, 0).astype(F32)
    marks = jnp.sum(send * mark, axis=1, keepdims=True)
    marks = jnp.broadcast_to(marks, (slots, wide - model)).astype(BF)
    tok = mm_t(send.astype(BF), tok_ref[0, 0]).astype(BF)
    cot = mm_t(send.astype(BF), cot_ref[0, 0]).astype(BF)
    for k in range(bins):
        rows = slice(k * cap, (k + 1) * cap)
        tok_out[k, 0, :, :model] = tok[rows]
        tok_out[k, 0, :, model:] = marks[rows]
        cot_out[k, 0] = cot[rows]


def vmem_specs(count):
    return [pl.BlockSpec(memory_space=pltpu.VMEM)] * count


def route(own, slot_rows, tokens, cotangent, bins):
    micro, _, model, slots = tokens.shape
    cap = slots // bins
    wide = model + (-model - 1) % 128 + 1
    block = pl.BlockSpec((1, 1, model, slots), lambda i: (i, 0, 0, 0))
    return pl.pallas_call(
        route_kernel,
        grid=(micro,),
        in_specs=[
            pl.BlockSpec(memory_space=pltpu.SMEM),
            pl.BlockSpec((1, 1, slots), lambda i: (i, 0, 0)),
            block,
            block,
        ],
        out_specs=[
            pl.BlockSpec((bins, 1, cap, wide), lambda i: (0, i, 0, 0)),
            pl.BlockSpec((bins, 1, cap, model), lambda i: (0, i, 0, 0)),
            pl.BlockSpec((1, slots, slots), lambda i: (i, 0, 0)),
        ],
        out_shape=[
            jax.ShapeDtypeStruct((bins, micro, cap, wide), BF),
            jax.ShapeDtypeStruct((bins, micro, cap, model), BF),
            jax.ShapeDtypeStruct((micro, slots, slots), BF),
        ],
        name="route",
    )(own, slot_rows, tokens, cotangent)


def unroute_kernel(*refs):
    map_ref = refs[0]
    out_one, out_two, home_ref = refs[-3:]
    pieces = refs[1:-3]
    bins = len(pieces) // 2
    cap = pieces[0].shape[1]
    for out, group in ((out_one, pieces[:bins]), (out_two, pieces[bins:])):
        for k, piece in enumerate(group):
            home_ref[k * cap : (k + 1) * cap, :] = piece[0]
        out[0, 0] = t_mm(home_ref[...], map_ref[0]).astype(BF)


def unroute(send_map, one, two):
    micro, slots, _ = send_map.shape
    cap, model = one[0].shape[1:]
    pieces = list(one) + list(two)
    out = jax.ShapeDtypeStruct((micro, 1, model, slots), BF)
    block = pl.BlockSpec((1, 1, model, slots), lambda i: (i, 0, 0, 0))
    return pl.pallas_call(
        unroute_kernel,
        grid=(micro,),
        in_specs=[pl.BlockSpec((1, slots, slots), lambda i: (i, 0, 0))]
        + [pl.BlockSpec((1, cap, model), lambda i: (i, 0, 0))] * len(pieces),
        out_specs=[block, block],
        out_shape=[out, out],
        scratch_shapes=[pltpu.VMEM((slots, model), BF)],
        name="unroute",
    )(send_map, *pieces)


def split_rows(acc_ref, own_ref, keep_ref, give_ref, index, start, width):
    half = keep_ref.shape[-2]
    mine = pl.ds(pl.multiple_of(own_ref[2] * half, 8), half)
    other = pl.ds(pl.multiple_of((1 - own_ref[2]) * half, 8), half)
    keep_ref[index] = acc_ref[mine, start : start + width].astype(BF)
    give_ref[index] = acc_ref[other, start : start + width].astype(BF)


def add_moment(acc_ref, own_ref, moment, start, width):
    high = moment.shape[0]
    if high % 8 == 0:
        rows = pl.ds(pl.multiple_of(own_ref[1] * high, 8), high)
        acc_ref[rows, start : start + width] += moment
        return
    for i in range(acc_ref.shape[0] // high):

        @pl.when(own_ref[1] == i)
        def _():
            acc_ref[i * high : (i + 1) * high, start : start + width] += moment


def give_back(values, land_ref, back_ref, m):
    bins, _, cap, _ = back_ref.shape
    back = mm(land_ref, values).astype(BF)
    for k in range(bins):
        back_ref[k, m] = back[k * cap : (k + 1) * cap]


def feed_kernel(own_ref, a2_ref, up_grad_ref, w_ref, moment_ref, h_ref, land_ref,
                dh2_ref, keep_ref, give_ref, back_ref,
                a2t_ref, gt_ref, act_ref, du_ref, acc_ref, y_ref):
    step = pl.program_id(0)
    tokens = a2_ref.shape[0]
    chunk = 256

    @pl.when(step == 0)
    def _():
        a2t_ref[...] = a2_ref[...].T
        gt_ref[...] = up_grad_ref[...].T
        y_ref[...] = h_ref[...]
        dh2_ref[...] = jnp.zeros_like(dh2_ref)

    width = w_ref.shape[3] // 3
    w_both = w_ref[0, 0, :, : 2 * width]
    w_down = w_ref[0, 0, :, 2 * width :]
    for start in range(0, tokens, chunk):
        rows = pl.ds(start, chunk)
        a2 = a2_ref[rows, :]
        both = mm(a2, w_both)
        gate = both[:, :width]
        up = both[:, width:]
        dact = mm(up_grad_ref[rows, :], w_down)
        sig = 1.0 / (1.0 + jnp.exp(-gate))
        silu = gate * sig
        act = (silu * up).astype(BF)
        dgate = (dact * up * sig * (1.0 + gate * (1.0 - sig))).astype(BF)
        dup = (dact * silu).astype(BF)
        act_ref[rows, :] = act
        du_ref[rows, :width] = dgate
        du_ref[rows, width:] = dup
        y_ref[rows, :] += mm_t(act, w_down)
        dh2_ref[rows, :] += mm_t(du_ref[rows, :], w_both)
    acc_ref[:, : 2 * width] = mm(a2t_ref[...], du_ref[...])
    acc_ref[:, 2 * width :] = mm(gt_ref[...], act_ref[...])

    @pl.when(step == 0)
    def _():
        for index in range(3):
            add_moment(acc_ref, own_ref, moment_ref[index], index * width, width)

    for index in range(3):
        split_rows(
            acc_ref, own_ref, keep_ref, give_ref, (index, 0), index * width, width
        )

    @pl.when(step == pl.num_programs(0) - 1)
    def _():
        micro, slots, _ = land_ref.shape
        for m in range(micro):
            rows = slice(m * slots, (m + 1) * slots)
            give_back(y_ref[rows, :].astype(BF), land_ref[m], back_ref, m)


def feed_forward_back(own, a2, up_grad, weights, moments, h, land):
    tokens, model = a2.shape
    _, bins, _, width = weights.shape
    width = width // 3
    micro, slots, _ = land.shape
    cap = slots // bins
    whole = pl.BlockSpec((tokens, model), lambda i, own_ref: (0, 0))
    halves = pl.BlockSpec((3, 1, model // 2, width), lambda i, own_ref: (0, i, 0, 0))
    block = pl.BlockSpec((1, 1, model, 3 * width), lambda i, own_ref: (0, i, 0, 0))
    return pl.pallas_call(
        feed_kernel,
        grid_spec=pltpu.PrefetchScalarGridSpec(
            num_scalar_prefetch=1,
            grid=(bins,),
            in_specs=[
                whole,
                whole,
                block,
                pl.BlockSpec(moments.shape, lambda i, own_ref: (0, 0, 0)),
                whole,
                pl.BlockSpec(land.shape, lambda i, own_ref: (0, 0, 0)),
            ],
            out_specs=[
                whole,
                halves,
                halves,
                pl.BlockSpec((bins, micro, cap, model), lambda i, own_ref: (0, 0, 0, 0)),
            ],
            scratch_shapes=[
                pltpu.VMEM((model, tokens), BF),
                pltpu.VMEM((model, tokens), BF),
                pltpu.VMEM((tokens, width), BF),
                pltpu.VMEM((tokens, 2 * width), BF),
                pltpu.VMEM((model, 3 * width), F32),
                pltpu.VMEM((tokens, model), F32),
            ],
        ),
        out_shape=[
            jax.ShapeDtypeStruct((tokens, model), F32),
            jax.ShapeDtypeStruct((3, bins, model // 2, width), BF),
            jax.ShapeDtypeStruct((3, bins, model // 2, width), BF),
            jax.ShapeDtypeStruct((bins, micro, cap, model), BF),
        ],
        name="feed",
    )(own, a2, up_grad, weights, moments, h, land)


def finish_kernel(gain_rate, own_ref, *refs):
    pieces, moments, outs = refs[:4], refs[4:6], refs[6:]
    width = pieces[0].shape[2]
    rows = moments[0].shape[1]
    q_cols = width * 3 // 8
    k_cols = width // 8

    def block(index, kind):
        place = own_ref[0] ^ block_of(index)
        value = pieces[0][kind, :rows].astype(F32)
        for k in range(1, 4):
            value = jnp.where(place == k, pieces[k][kind, :rows].astype(F32), value)
        return value

    def lanes(start, count):
        source = lax.broadcasted_iota(jnp.int32, (width, count), 0)
        target = lax.broadcasted_iota(jnp.int32, (width, count), 1)
        return jnp.where(source == target + start, 1.0, 0.0).astype(BF)

    narrow = -math.sqrt(HEADS / KV_HEADS)
    for kind in range(2):
        zero = block(0, kind).astype(BF)
        for i, start in enumerate((q_cols, q_cols + k_cols)):
            value = dot(lanes(start, k_cols), zero, ((0,), (1,)))
            outs[2 + 2 * i + kind][...] = narrow * value if kind else value
        for i, start in ((0, 0), (6, q_cols + 2 * k_cols)):
            value = mm(zero, lanes(start, q_cols))
            outs[i + kind][...] = -value if kind else value
        for index in range(1, 4):
            value = block(index, kind)
            rate = -DOWN_RATE if index == 3 else -1.0
            outs[6 + 2 * index + kind][...] = rate * value if kind else value
        grad = sum(piece[kind, rows : rows + 1, :rows].astype(F32) for piece in pieces)
        value = 0.5 * moments[kind][...] + 0.5 * grad
        outs[14 + 2 * kind][...] = value
        outs[15 + 2 * kind][...] = -gain_rate * value


def finish(own, pieces, moments, gain_rate):
    width = pieces[0].shape[2]
    rows = moments[0].shape[1]
    q_cols = width * 3 // 8
    k_cols = width // 8
    shapes = [(rows, q_cols)] * 2 + [(k_cols, rows)] * 4 + [(rows, q_cols)] * 2
    shapes += [(rows, width)] * 6 + [(1, rows)] * 4
    return pl.pallas_call(
        functools.partial(finish_kernel, gain_rate),
        grid=(1,),
        in_specs=[pl.BlockSpec(memory_space=pltpu.SMEM)]
        + [full_spec(piece.shape) for piece in (*pieces, *moments)],
        out_specs=[full_spec(shape) for shape in shapes],
        out_shape=[jax.ShapeDtypeStruct(shape, F32) for shape in shapes],
        name="finish",
    )(own, *pieces, *moments)


def newton_kernel(kind_ref, state_ref, out_ref, z_ref, zb_ref, a_ref, ab_ref, pb_ref):
    bins, size, width = state_ref.shape
    quarter = width * 3 // 8
    eighth = width // 8

    def run(size, cols, total):
        groups = [(i, min(128, size - i)) for i in range(0, size, 128)]
        chunks = [(i, min(384, size - i)) for i in range(0, size, 384)]
        scale = 1.0 / (jnp.sqrt(jnp.full((1, 1), total, F32)) + 1e-07)
        for start, high in chunks:
            rows = slice(start, start + high)
            value = z_ref[rows, :cols] * scale
            z_ref[rows, :cols] = value
            zb_ref[rows, :cols] = value.astype(BF)

        def diagonal(ref, target, start, high):
            downs, acrosses = [], []
            for spot, count in groups:
                if start <= spot < start + high:
                    rows = slice(spot, spot + count)
                    tile = ref[spot - start : spot - start + count, rows]
                    row_of = lax.broadcasted_iota(jnp.int32, (count, count), 0)
                    eye = row_of == lax.broadcasted_iota(jnp.int32, (count, count), 1)
                    value = jnp.where(eye, tile, 0.0)
                    target[rows, rows] = jnp.where(eye, 0.0, tile).astype(BF)
                    downs.append(jnp.sum(value, axis=1, keepdims=True))
                    acrosses.append(jnp.sum(value, axis=0, keepdims=True))
            down = downs[0] if len(downs) == 1 else jnp.concatenate(downs, axis=0)
            return down, acrosses

        def step(index, carry):
            downs, across = [], []
            for start, high in chunks:
                rows = slice(start, start + high)
                gram = mm_t(zb_ref[rows, :cols], zb_ref[:size, :cols])
                a_ref[rows, :size] = gram
                ab_ref[rows, :size] = gram.astype(BF)
                down, parts = diagonal(gram, ab_ref, start, high)
                downs.append(down)
                across += parts
            across = jnp.concatenate(across, axis=1)
            diags = []
            for (start, high), down in zip(chunks, downs):
                rows = slice(start, start + high)
                square = mm(ab_ref[rows, :size], ab_ref[:size, :size])
                factor = (COEFF_B + COEFF_C * down) + COEFF_C * across
                poly = a_ref[rows, :size] * factor + COEFF_C * square
                pb_ref[rows, :size] = poly.astype(BF)
                diag, _ = diagonal(poly, pb_ref, start, high)
                diags.append(COEFF_A + diag - COEFF_C * down * down)
            for (start, high), diag in zip(chunks, diags):
                rows = slice(start, start + high)
                value = diag * z_ref[rows, :cols] + mm(pb_ref[rows, :size], zb_ref[:size, :cols])
                z_ref[rows, :cols] = value
            for start, high in chunks:
                rows = slice(start, start + high)
                zb_ref[rows, :cols] = z_ref[rows, :cols].astype(BF)
            return carry

        lax.fori_loop(0, NS_STEPS, step, 0)

    def keep_lanes(first, wide, low, high):
        lane = lax.broadcasted_iota(jnp.int32, (size, wide), 1) + first
        return (lane >= low) & (lane < high)

    def put(first, wide, low, high, mine):
        keep = keep_lanes(first, wide, low, high)
        old = out_ref[:, first : first + wide].astype(F32)
        out_ref[:, first : first + wide] = jnp.where(keep, mine.astype(F32), old).astype(BF)

    def load(wide, fetch):
        total = jnp.zeros((), F32)
        for j in range(bins):
            piece = fetch(j)
            z_ref[:, j * wide : (j + 1) * wide] = piece
            total = total + jnp.sum(piece * piece)
        run(size, wide * bins, total)

    kind = kind_ref[0]

    @pl.when(kind == 0)
    def _():
        load(width, lambda j: state_ref[j].astype(F32))
        out_ref[...] = zb_ref[:, :width]

    large = 256 if width == 384 else width
    small = 128 if width == 384 else width
    middle = 128 if width == 384 else 0
    k_low = jnp.where(kind == 1, quarter, quarter + eighth)

    @pl.when(kind != 0)
    def _():
        out_ref[...] = jnp.zeros_like(out_ref)

        def large_piece(j):
            low = state_ref[j, :, :large].astype(F32)
            low = jnp.where(keep_lanes(0, large, 0, quarter), low, 0.0)
            high = state_ref[j, :, width - large :].astype(F32)
            high = jnp.where(
                keep_lanes(width - large, large, width - quarter, width), high, 0.0
            )
            return jnp.where(kind == 1, low, high)

        load(large, large_piece)

        @pl.when(kind == 1)
        def _():
            put(0, large, 0, quarter, zb_ref[:, :large])

        @pl.when(kind != 1)
        def _():
            put(width - large, large, width - quarter, width, zb_ref[:, :large])

        narrow = bins * eighth
        lane = lax.broadcasted_iota(jnp.int32, (small, narrow), 0) + middle - k_low
        column = lax.broadcasted_iota(jnp.int32, (small, narrow), 1)
        inside = (lane >= 0) & (lane < eighth)
        turned = jnp.zeros((narrow, size), F32)
        for j in range(bins):
            chosen = jnp.where(inside & (column == lane + j * eighth), 1.0, 0.0).astype(BF)
            piece = state_ref[j, :, middle : middle + small]
            turned = turned + dot(chosen, piece, ((0,), (1,)))
        z_ref[:narrow, :size] = turned
        run(narrow, size, jnp.sum(turned * turned))
        chosen = jnp.where(inside & (column == lane), 1.0, 0.0).astype(BF)
        back = dot(zb_ref[:narrow, :size], chosen, ((0,), (1,)))
        put(middle, small, k_low, k_low + eighth, back)


def newton(kind, state):
    bins, size, width = state.shape
    cols = bins * width
    return pl.pallas_call(
        newton_kernel,
        in_specs=[
            pl.BlockSpec(memory_space=pltpu.SMEM),
            pl.BlockSpec(memory_space=pltpu.VMEM),
        ],
        out_specs=pl.BlockSpec(memory_space=pltpu.VMEM),
        out_shape=jax.ShapeDtypeStruct((size, width), BF),
        scratch_shapes=[
            pltpu.VMEM((size, cols), F32),
            pltpu.VMEM((size, cols), BF),
            pltpu.VMEM((size, size), F32),
            pltpu.VMEM((size, size), BF),
            pltpu.VMEM((size, size), BF),
        ],
        name="newton",
    )(kind, state)


def half_swap(value):
    lane = lax.broadcasted_iota(jnp.int32, value.shape, 1)
    low = (lane % HEAD_DIM) < HEAD_DIM // 2
    return jnp.where(low, pltpu.roll(value, 96, 1), pltpu.roll(value, 32, 1))


def twice(value, upper):
    lane = lax.broadcasted_iota(jnp.int32, value.shape, 1)
    keep = (lane >= HEAD_DIM) if upper else (lane < HEAD_DIM)
    part = jnp.where(keep, value, 0.0)
    return part + pltpu.roll(part, HEAD_DIM, 1)


def fold(value):
    return value + pltpu.roll(value, HEAD_DIM, 1)


PAIRS = (HEADS + 1) // 2
KV_PAIRS = (KV_HEADS + 1) // 2
Q_WIDE = PAIRS * 128
KV_WIDE = KV_PAIRS * 128
WIDE = Q_WIDE + 2 * KV_WIDE
SCALE = 1.0 / math.sqrt(HEAD_DIM)


def soft_rows(query, key, allowed):
    scores = jnp.where(allowed, mm_t(query, key) * SCALE, NEGATIVE)
    raised = jnp.exp(scores - jnp.max(scores, axis=1, keepdims=True))
    return raised * (1.0 / jnp.sum(raised, axis=1, keepdims=True))


def allow(seg_col, seg_row):
    size = seg_row.shape[1]
    row = lax.broadcasted_iota(jnp.int32, (size, size), 0)
    col = lax.broadcasted_iota(jnp.int32, (size, size), 1)
    return (seg_col == seg_row) & (col <= row)


def key_pair(qkv, base, kv):
    group = qkv[:, base + (kv // 2) * 128 : base + (kv // 2) * 128 + 128].astype(F32)
    return twice(group, kv % 2 == 1).astype(BF)


def masked_half(group, head):
    lane = lax.broadcasted_iota(jnp.int32, group.shape, 1)
    keep = (lane >= HEAD_DIM) if head % 2 else (lane < HEAD_DIM)
    return jnp.where(keep, group.astype(F32), 0.0).astype(BF)


def take_columns(w_ref, own, kind_start, cols, start, wide, bins):
    width = w_ref.shape[2]
    source = lax.broadcasted_iota(jnp.int32, (width, wide), 0)
    target = lax.broadcasted_iota(jnp.int32, (width, wide), 1) + start
    inside = (source >= kind_start) & (source < kind_start + cols)
    result = None
    for j in range(start // cols, min((start + wide - 1) // cols, bins - 1) + 1):
        chosen = inside & (source - kind_start == target - j * cols)
        part = mm(w_ref[own ^ j], jnp.where(chosen, 1.0, 0.0).astype(BF))
        result = part if result is None else result + part
    return result.astype(BF)


def attend_kernel(*refs):
    own_ref = refs[0]
    bins = (len(refs) - 23) // 2
    toks = refs[1 : 1 + bins]
    cots = refs[1 + bins : 1 + 2 * bins]
    (gain_in, w_ref, cos_ref, sin_ref, sc_ref, sr_ref,
     x_ref, g_ref, land_ref, a1_ref, qkv_ref, ob_ref, h_ref, a2_ref, wqkv_ref, wo_ref, gain_ref,
     got_ref, got2_ref, land_t, keys_ref, values_ref) = refs[1 + 2 * bins :]
    slots, model = x_ref.shape
    cap = slots // bins
    width = w_ref.shape[2]
    q_cols = width * 3 // 8
    k_cols = width // 8

    @pl.when(pl.program_id(0) == 0)
    def _():
        row = lax.broadcasted_iota(jnp.int32, (model, model), 0)
        eye = row == lax.broadcasted_iota(jnp.int32, (model, model), 1)
        for i in range(2):
            column = gain_in[:, i : i + 1].astype(F32)
            gain_ref[i : i + 1, :] = jnp.sum(
                jnp.where(eye, column, 0.0), axis=0, keepdims=True
            )
        for tile in range(WIDE // 128):
            if tile < PAIRS:
                spot = (0, q_cols, tile * 128)
            elif tile < PAIRS + KV_PAIRS:
                spot = (q_cols, k_cols, (tile - PAIRS) * 128)
            else:
                spot = (q_cols + k_cols, k_cols, (tile - PAIRS - KV_PAIRS) * 128)
            wqkv_ref[:, tile * 128 : tile * 128 + 128] = take_columns(
                w_ref, own_ref[0], *spot, 128, bins
            )
        for tile in range(PAIRS):
            wo_ref[:, tile * 128 : tile * 128 + 128] = take_columns(
                w_ref, own_ref[0], q_cols + 2 * k_cols, q_cols, tile * 128, 128, bins
            )

    spot = lax.broadcasted_iota(jnp.int32, (cap, slots), 1)
    for k in range(bins):
        rows = slice(k * cap, (k + 1) * cap)
        place = toks[k][0, :, model : model + 1].astype(F32).astype(jnp.int32) - 1
        land = jnp.where(spot == place, 1.0, 0.0).astype(BF)
        land_t[rows, :] = land
        got_ref[rows, :] = toks[k][0, :, :model]
        got2_ref[rows, :] = cots[k][0]
    land_ref[0] = land_t[...]
    x = t_mm(land_t[...], got_ref[...])
    x_ref[...] = x.astype(BF)
    g_ref[...] = t_mm(land_t[...], got2_ref[...]).astype(BF)
    r1 = lax.rsqrt(jnp.mean(x * x, axis=1, keepdims=True) + EPSILON)
    a1 = (x * r1 * gain_ref[0:1, :]).astype(BF)
    a1_ref[...] = a1
    cosine = cos_ref[...]
    sine = sin_ref[...]
    for start in range(0, WIDE, 256):
        wide = min(256, WIDE - start)
        both = mm(a1, wqkv_ref[:, start : start + wide])
        for spot in range(0, wide, 128):
            value = both[:, spot : spot + 128]
            if start + spot < Q_WIDE + KV_WIDE:
                value = value * cosine + half_swap(value) * sine
            qkv_ref[:, start + spot : start + spot + 128] = value.astype(BF)
    allowed = allow(sc_ref[0], sr_ref[0])
    for kv in range(KV_HEADS):
        keys_ref[kv] = key_pair(qkv_ref, Q_WIDE, kv)
        values_ref[kv] = key_pair(qkv_ref, Q_WIDE + KV_WIDE, kv)
    lane = lax.broadcasted_iota(jnp.int32, (slots, 128), 1)

    def one_pair(pair):
        lanes = slice(pair * 128, pair * 128 + 128)
        group = qkv_ref[:, lanes]
        parts = []
        for half in range(min(2, HEADS - 2 * pair)):
            kv = (2 * pair + half) // GROUPS
            soft = soft_rows(masked_half(group, half), keys_ref[kv], allowed)
            parts.append(mm(soft.astype(BF), values_ref[kv]))
        parts.append(jnp.zeros((slots, 128), F32))
        ob_ref[:, lanes] = jnp.where(lane < HEAD_DIM, parts[0], parts[1]).astype(BF)

    for pair in range(PAIRS):
        one_pair(pair)
    h = x + mm(ob_ref[:, :model], wo_ref[:, :model])
    h_ref[...] = h
    r2 = lax.rsqrt(jnp.mean(h * h, axis=1, keepdims=True) + EPSILON)
    a2_ref[...] = (h * r2 * gain_ref[1:2, :]).astype(BF)


def row_spec(slots, width):
    return pl.BlockSpec((slots, width), lambda i: (i, 0))


def full_spec(shape):
    return pl.BlockSpec(shape, lambda i: (0,) * len(shape))


def attend(own, toks, cots, gains, weights, cosine, sine, seg_col, seg_row):
    bins, model, _ = weights.shape
    micro, _, slots = seg_row.shape
    total = micro * slots
    cap = slots // bins
    row_shapes = ((model, BF), (WIDE, BF), (Q_WIDE, BF), (model, F32), (model, BF))
    wide = toks[0].shape[2]
    return pl.pallas_call(
        attend_kernel,
        grid=(micro,),
        in_specs=[pl.BlockSpec(memory_space=pltpu.SMEM)]
        + [pl.BlockSpec((1, cap, wide), lambda i: (i, 0, 0))] * bins
        + [pl.BlockSpec((1, cap, model), lambda i: (i, 0, 0))] * bins
        + [
            full_spec(gains.shape), full_spec(weights.shape),
            row_spec(slots, 128), row_spec(slots, 128),
            pl.BlockSpec((1, slots, 1), lambda i: (i, 0, 0)),
            pl.BlockSpec((1, 1, slots), lambda i: (i, 0, 0)),
        ],
        out_specs=[
            row_spec(slots, model), row_spec(slots, model),
            pl.BlockSpec((1, slots, slots), lambda i: (i, 0, 0)),
        ]
        + [row_spec(slots, wide) for wide, _ in row_shapes]
        + [full_spec((model, WIDE)), full_spec((model, Q_WIDE)), full_spec((2, model))],
        out_shape=[
            jax.ShapeDtypeStruct((total, model), BF),
            jax.ShapeDtypeStruct((total, model), BF),
            jax.ShapeDtypeStruct((micro, slots, slots), BF),
        ]
        + [jax.ShapeDtypeStruct((total, wide), kind) for wide, kind in row_shapes]
        + [
            jax.ShapeDtypeStruct((model, WIDE), BF),
            jax.ShapeDtypeStruct((model, Q_WIDE), BF),
            jax.ShapeDtypeStruct((2, model), F32),
        ],
        scratch_shapes=[
            pltpu.VMEM((slots, model), BF),
            pltpu.VMEM((slots, model), BF),
            pltpu.VMEM((slots, slots), BF),
            pltpu.VMEM((KV_HEADS, slots, 128), BF),
            pltpu.VMEM((KV_HEADS, slots, 128), BF),
        ],
        name="attend",
    )(own, *toks, *cots, gains, weights, cosine, sine, seg_col, seg_row)


def attend_back_kernel(own_ref, x_ref, gain_ref, wqkv_ref, wo_ref, cos_ref, sin_ref, sc_ref,
                       sr_ref, a1_ref, qkv_ref, ob_ref, h_ref, dh2_ref, g_ref, land_ref,
                       moment_ref, back_ref, gains_ref, keep_ref, give_ref,
                       a1_all, ob_all, d_all, dhb_all, acc_ref, dob_ref,
                       keys_ref, values_ref, dkeys, dvalues):
    step = pl.program_id(0)
    slots, model = x_ref.shape
    rows = pl.ds(pl.multiple_of(step * slots, slots), slots)

    @pl.when(step == 0)
    def _():
        gains_ref[...] = jnp.zeros_like(gains_ref)

    h = h_ref[...]
    dh2 = dh2_ref[...]
    r2 = lax.rsqrt(jnp.mean(h * h, axis=1, keepdims=True) + EPSILON)
    scaled = dh2 * gain_ref[1:2, :]
    inner = jnp.mean(scaled * h, axis=1, keepdims=True)
    dh = g_ref[...].astype(F32) + r2 * scaled - h * (r2 * r2 * r2 * inner)
    gains_ref[1:2, :] += jnp.sum(dh2 * h * r2, axis=0, keepdims=True)
    dhb = dh.astype(BF)
    dhb_all[rows, :] = dhb
    a1_all[:, rows] = a1_ref[...].T
    ob_all[:, rows] = ob_ref[:, :model].T
    allowed = allow(sc_ref[0], sr_ref[0])
    for kv in range(KV_HEADS):
        keys_ref[kv] = key_pair(qkv_ref, Q_WIDE, kv)
        values_ref[kv] = key_pair(qkv_ref, Q_WIDE + KV_WIDE, kv)
    dkeys[...] = jnp.zeros_like(dkeys)
    dvalues[...] = jnp.zeros_like(dvalues)
    dob_ref[:, :model] = mm_t(dhb, wo_ref[:, :model]).astype(BF)
    dob_ref[:, model:] = jnp.zeros((slots, Q_WIDE - model), BF)
    cosine = cos_ref[...]
    sine = sin_ref[...]
    lane = lax.broadcasted_iota(jnp.int32, (slots, 128), 1)

    def one_pair(pair):
        lanes = slice(pair * 128, pair * 128 + 128)
        group = qkv_ref[:, lanes]
        dob = dob_ref[:, lanes]
        parts = []
        for half in range(min(2, HEADS - 2 * pair)):
            kv = (2 * pair + half) // GROUPS
            query = masked_half(group, half)
            soft = soft_rows(query, keys_ref[kv], allowed)
            mine = masked_half(dob, half)
            dp = mm_t(mine, values_ref[kv])
            ds = (soft * (dp - jnp.sum(soft * dp, axis=1, keepdims=True))).astype(BF)
            parts.append(mm(ds, keys_ref[kv]))
            dkeys[kv] += t_mm(ds, query)
            dvalues[kv] += t_mm(soft.astype(BF), mine)
        parts.append(jnp.zeros((slots, 128), F32))
        out = jnp.where(lane < HEAD_DIM, parts[0], parts[1]) * SCALE
        out = out * cosine - half_swap(out) * sine
        d_all[rows, lanes] = out.astype(BF)

    for pair in range(PAIRS):
        one_pair(pair)
    for pair in range(KV_PAIRS):
        lane = lax.broadcasted_iota(jnp.int32, (slots, 128), 1)

        def both(parts):
            low = fold(parts[2 * pair])
            high = fold(parts[2 * pair + 1]) if 2 * pair + 1 < KV_HEADS else 0.0
            return jnp.where(lane < HEAD_DIM, low, high)

        dk = both(dkeys) * SCALE
        dk = dk * cosine - half_swap(dk) * sine
        start = Q_WIDE + pair * 128
        d_all[rows, start : start + 128] = dk.astype(BF)
        start += KV_WIDE
        d_all[rows, start : start + 128] = both(dvalues).astype(BF)
    dh1 = mm_t(d_all[rows, :], wqkv_ref[...])
    x = x_ref[...].astype(F32)
    r1 = lax.rsqrt(jnp.mean(x * x, axis=1, keepdims=True) + EPSILON)
    scaled = dh1 * gain_ref[0:1, :]
    inner = jnp.mean(scaled * x, axis=1, keepdims=True)
    dx = dh + r1 * scaled - x * (r1 * r1 * r1 * inner)
    gains_ref[0:1, :] += jnp.sum(dh1 * x * r1, axis=0, keepdims=True)
    give_back(dx.astype(BF), land_ref[0], back_ref, step)

    @pl.when(step == pl.num_programs(0) - 1)
    def _():
        width = acc_ref.shape[1]
        bins = keep_ref.shape[0]
        q_cols = width * 3 // 8
        k_cols = width // 8
        wide = 256 if width == 384 else width
        skip = width - wide
        spot = lax.broadcasted_iota(jnp.int32, (1, wide), 1)
        late = spot + skip - (q_cols + 2 * k_cols)
        for k in range(bins):
            j = own_ref[0] ^ k
            target = jnp.where(
                spot < q_cols,
                j * q_cols + spot,
                jnp.where(
                    spot < q_cols + k_cols,
                    Q_WIDE + j * k_cols + spot - q_cols,
                    jnp.where(
                        spot < q_cols + 2 * k_cols,
                        Q_WIDE + KV_WIDE + j * k_cols + spot - q_cols - k_cols,
                        -1,
                    ),
                ),
            )
            source = lax.broadcasted_iota(jnp.int32, (WIDE, wide), 0)
            chosen = mm(d_all[...], jnp.where(source == target, 1.0, 0.0).astype(BF))
            first = mm(a1_all[...], chosen.astype(BF))
            target = jnp.where(late >= 0, j * q_cols + late, -1)
            source = lax.broadcasted_iota(jnp.int32, (model, wide), 0)
            chosen = mm(dhb_all[...], jnp.where(source == target, 1.0, 0.0).astype(BF))
            second = mm(ob_all[...], chosen.astype(BF))
            if skip:
                acc_ref[:, :skip] = first[:, :skip]
                acc_ref[:, skip:wide] = first[:, skip:] + second[:, : wide - skip]
                acc_ref[:, wide:] = second[:, wide - skip :]
            else:
                acc_ref[...] = first + second
            if k == 0:
                add_moment(acc_ref, own_ref, moment_ref[...], 0, width)
            split_rows(acc_ref, own_ref, keep_ref, give_ref, k, 0, width)


def attend_back(own, x, gains, wqkv, wo, cosine, sine, seg_col, seg_row,
                a1, qkv, ob, h, dh2, g, land, moment, bins):
    total, model = x.shape
    micro, slots, _ = land.shape
    cap = slots // bins
    width = moment.shape[1]
    return pl.pallas_call(
        attend_back_kernel,
        grid=(micro,),
        in_specs=[
            pl.BlockSpec(memory_space=pltpu.SMEM),
            row_spec(slots, model), full_spec(gains.shape), full_spec(wqkv.shape),
            full_spec(wo.shape), row_spec(slots, 128), row_spec(slots, 128),
            pl.BlockSpec((1, slots, 1), lambda i: (i, 0, 0)),
            pl.BlockSpec((1, 1, slots), lambda i: (i, 0, 0)),
            row_spec(slots, model), row_spec(slots, WIDE), row_spec(slots, Q_WIDE),
            row_spec(slots, model), row_spec(slots, model), row_spec(slots, model),
            pl.BlockSpec((1, slots, slots), lambda i: (i, 0, 0)),
            full_spec(moment.shape),
        ],
        out_specs=[
            full_spec((bins, micro, cap, model)), full_spec((2, model)),
            full_spec((bins, model // 2, width)), full_spec((bins, model // 2, width)),
        ],
        out_shape=[
            jax.ShapeDtypeStruct((bins, micro, cap, model), BF),
            jax.ShapeDtypeStruct((2, model), F32),
            jax.ShapeDtypeStruct((bins, model // 2, width), BF),
            jax.ShapeDtypeStruct((bins, model // 2, width), BF),
        ],
        scratch_shapes=[
            pltpu.VMEM((model, total), BF),
            pltpu.VMEM((model, total), BF),
            pltpu.VMEM((total, WIDE), BF),
            pltpu.VMEM((total, model), BF),
            pltpu.VMEM((model, width), F32),
            pltpu.VMEM((slots, Q_WIDE), BF),
            pltpu.VMEM((KV_HEADS, slots, 128), BF),
            pltpu.VMEM((KV_HEADS, slots, 128), BF),
            pltpu.VMEM((KV_HEADS, slots, 128), F32),
            pltpu.VMEM((KV_HEADS, slots, 128), F32),
        ],
        name="attend_back",
    )(own, x, gains, wqkv, wo, cosine, sine, seg_col, seg_row,
      a1, qkv, ob, h, dh2, g, land, moment)


def rope_tables(positions):
    half_dim = HEAD_DIM // 2
    frequency = jnp.exp(
        -math.log(ROPE_BASE) * 2.0 * jnp.arange(half_dim, dtype=F32) / HEAD_DIM
    )
    angles = positions.reshape(-1).astype(F32)[:, None] * frequency
    cosine = jnp.cos(angles)
    sine = jnp.sin(angles)
    return (
        jnp.concatenate([cosine] * 4, axis=1),
        jnp.concatenate([-sine, sine, -sine, sine], axis=1),
    )


def slot_layout(lengths, starts, bin_slots):
    slot_index = jnp.arange(bin_slots, dtype=jnp.int32)
    inside = (
        (slot_index[:, None] >= starts[..., None, :])
        & (slot_index[:, None] < starts[..., None, :] + lengths[..., None, :])
    ).astype(jnp.int32)
    number = jnp.arange(lengths.shape[-1], dtype=jnp.int32)
    covered = jnp.minimum(jnp.sum(inside, axis=-1), 1)
    segment = jnp.sum(inside * number, axis=-1) + (1 - covered) * (
        lengths.shape[-1] + slot_index
    )
    first_slot = jnp.sum(inside * starts[..., None, :], axis=-1)
    return (segment, slot_index - first_slot)


def on_device(
    tokens, cotangent, token_slots, sequence_lengths, sequence_starts,
    query_weight, key_weight, value_weight, output_weight,
    gate_weight, up_weight, down_weight, attention_gain, feedforward_gain,
    query_moment, key_moment, value_moment, output_moment,
    gate_moment, up_moment, down_moment, attention_moment, feedforward_moment,
):
    bins = lax.axis_size("bins")
    fsdp = lax.axis_size("fsdp")
    b = lax.axis_index("bins")
    f = lax.axis_index("fsdp")
    micro, _, slots, model = tokens.shape
    total = micro * slots
    rows_own = query_weight.shape[0]
    q_cols = query_weight.shape[1]
    k_cols = key_weight.shape[1]
    split = fsdp // 4
    flag = jnp.where((f & (split // 2)) != 0, 1, 0)
    own = jnp.stack([b, f, flag]).astype(jnp.int32)

    block_zero = jnp.concatenate(
        [query_weight, key_weight, value_weight, output_weight], axis=1
    )[None]
    blocks = jnp.concatenate([gate_weight, up_weight, down_weight.T], axis=1)
    gain_lanes = jnp.pad(
        jnp.stack([attention_gain, feedforward_gain], axis=1), ((0, 0), (0, 126))
    )
    width = block_zero.shape[2]
    zero_chips = gather_chips(
        jnp.concatenate([block_zero[0], gain_lanes], axis=1), fsdp, f
    )
    gains_cols = jnp.concatenate([part[:, :, width:] for part in zero_chips])
    gains_cols = gather_cores(gains_cols[None], fsdp, f)[0]
    zero_chips = [part[:, :, :width] for part in zero_chips]

    tok_send, cot_send, send_map = route(
        own, token_slots, tokens.swapaxes(2, 3), cotangent.swapaxes(2, 3), bins
    )

    def exchange(pieces):
        return [pieces[0]] + [swap(pieces[k], "bins", bins, k) for k in range(1, bins)]

    toks = exchange(tok_send)
    zero_stages = []
    zero_chips = [after(part, *toks) for part in zero_chips]
    zero_bins = gather_bins(*zero_chips, bins, zero_stages)
    feed_chips = gather_chips(after(blocks, *zero_stages[0]), fsdp, f)
    cots = exchange(after(cot_send, *zero_stages[0]))

    segment, position = slot_layout(sequence_lengths[:, 0, 0], sequence_starts[:, 0, 0], slots)
    cosine, sine = rope_tables(position)

    attn_w = gather_cores(zero_bins, fsdp, f)
    first, second = feed_chips
    feed_stages = []
    ahead = (zero_bins, *cots)
    feed_bins = gather_bins(after(first, *ahead), after(second, *ahead), bins, feed_stages)
    attn_w = after(attn_w, *feed_stages[0])

    edges = (0, q_cols, q_cols + k_cols, q_cols + 2 * k_cols, width)
    seg_col = segment[:, :, None]
    seg_row = segment[:, None, :]
    tables = (cosine, sine, seg_col, seg_row)
    x_low, g_low, land, a1, qkv, ob, h, a2, w_qkv, w_o, gains_full = attend(
        own, toks, cots, gains_cols, attn_w, *tables
    )
    feed_w = gather_cores(after(feed_bins, a2), fsdp, f)

    moments = jnp.stack([gate_moment, up_moment, down_moment.T])
    dh2, kept, given, back = feed_forward_back(own, a2, g_low, feed_w[None], moments, h, land)
    one_stages = []
    part_one = reduce_blocks(kept, given, 1, bins, fsdp, f, one_stages)
    home_one = exchange(after(back, one_stages[0]))
    dh2 = after(dh2, one_stages[0])

    moment_zero = jnp.concatenate(
        [query_moment, key_moment, value_moment, output_moment], axis=1
    )
    back, gain_sum, kept, given = attend_back(
        own, x_low, gains_full, w_qkv, w_o, *tables,
        a1, qkv, ob, h, dh2, g_low, land, moment_zero, bins,
    )
    zero_stages = []
    sums = [gain_sum]

    def beside(axis=None, count=None, bit=None, token=None):
        if axis is not None:
            sums.append(sums[-1] + swap(after(sums[-1], token), axis, count, bit))
        return sums[-1]

    kept = after(kept, *home_one)
    part_zero = reduce_blocks(kept[None], given[None], 0, bins, fsdp, f, zero_stages, beside)

    owner = f // split
    is_zero = block_of(owner) == 0
    state = (0.5 * jnp.where(is_zero, part_zero, part_one)).astype(BF)
    half = state.shape[0] // 2
    state = gather_bins(state[:half], state[half:], bins)
    home_two = exchange(after(back, state))
    for bit in bits_of(split)[1:]:
        beside("fsdp", fsdp, bit, state)
    gain_rows = jnp.pad(
        beside().astype(BF).reshape(2, fsdp, 1, rows_own),
        ((0, 0), (0, 0), (0, 7), (0, width - rows_own)),
    )
    for bit in bits_of(split):
        state = jnp.concatenate([state, swap(state, "fsdp", fsdp, bit)], axis=1)

    kind = jnp.stack([jnp.where(is_zero, 1 + (f & 1), 0), b]).astype(jnp.int32)
    ortho = newton(kind, state)
    other = swap(ortho, "fsdp", fsdp, 1)
    block_output, input_gradient = unroute(after(send_map, other), home_one, home_two)
    other = other.reshape(fsdp // 8, 2, -1, width)[:, ::-1].reshape(ortho.shape)
    lane = jnp.arange(width, dtype=jnp.int32)
    first_core = (lane < edges[2]).astype(jnp.int32)
    ortho = jnp.where(is_zero & (first_core == (f & 1)), other, ortho)

    both = jnp.stack([state[0], ortho]).reshape(2, fsdp, rows_own, width)
    low = f % split
    turn = low * 4

    def parcel(target):
        return jnp.concatenate(
            [pick(both, target ^ turn, 1), pick(gain_rows, target, 1)], axis=1
        )

    pieces = [parcel(f)]
    for k in range(1, 4):
        sent = parcel((owner ^ k) * split + low)
        pieces.append(swap(sent, "fsdp", fsdp, k * split))
    outs = [block_output.swapaxes(2, 3), input_gradient.swapaxes(2, 3)]
    gain_rate = 0.1 / math.sqrt(micro * bins * fsdp * slots)
    moments = (attention_moment[None], feedforward_moment[None])
    done = finish(owner.astype(jnp.int32)[None], pieces, moments, gain_rate)
    for i, value in enumerate(done):
        if i >= 14:
            outs.append(value[0])
        else:
            outs.append(value.T if i in (2, 3, 4, 5, 12, 13) else value)
    return tuple(outs)


def solution(mesh):
    rows = P(None, "fsdp", "bins", None)
    matrix = P("fsdp", "bins")
    turned = P("bins", "fsdp")
    vector = P("fsdp")
    params = (matrix,) * 6 + (turned, vector, vector)
    doubled = ()
    for spec in params:
        doubled += (spec, spec)
    return jax.shard_map(
        on_device,
        mesh=mesh,
        in_specs=(rows, rows, P(None, "fsdp", "bins"), rows, rows) + params + params,
        out_specs=(rows, rows) + doubled,
        check_vma=False,
    )
```

```python
import functools
import math

import jax
import jax.numpy as jnp
from jax import lax
from jax.experimental import pallas as pl
from jax.experimental.pallas import tpu as pltpu
from jax.sharding import PartitionSpec as P

HEADS = 9
KV_HEADS = 3
HEAD_DIM = 64
GROUPS = HEADS // KV_HEADS
NS_STEPS = 5
HIDDEN_RATIO = 1536 / 576
DOWN_RATE = math.sqrt(HIDDEN_RATIO)
EPSILON = 1e-05
NEGATIVE = -1e30
ROPE_BASE = 10000.0
COEFF_A = 3.4445
COEFF_B = -4.775
COEFF_C = 2.0315
BF = jnp.bfloat16
F32 = jnp.float32


def dot(left, right, dims):
    return lax.dot_general(left, right, (dims, ((), ())), preferred_element_type=F32)


def mm(left, right):
    return dot(left, right, ((left.ndim - 1,), (0,)))


def mm_t(left, right):
    return dot(left, right, ((left.ndim - 1,), (1,)))


def t_mm(left, right):
    return dot(left, right, ((0,), (0,)))


def swap(value, axis, count, step, keep=None):
    pairs = [(i, i ^ step) for i in range(count) if keep is None or keep(i ^ step)]
    return lax.ppermute(value, axis, pairs)


def bits_of(count):
    return [1 << i for i in range(count.bit_length() - 1)]


def ordered(pieces, index):
    result = list(pieces)
    for bit in bits_of(len(pieces)):
        flag = (index & bit) != 0
        result = [jnp.where(flag, result[j ^ bit], result[j]) for j in range(len(result))]
    return result


def join(mine, other, flag):
    return jnp.stack([jnp.where(flag, other, mine), jnp.where(flag, mine, other)])


def after(value, *others):
    return lax.optimization_barrier((value,) + others)[0]


def bin_orders(bins):
    bits = bits_of(bins)
    half = len(bits) // 2
    return bits, bits[half:] + bits[:half]


def gather_bins(first, second, bins, stages=None):
    orders = bin_orders(bins)
    parts = [first, second]
    for pair in zip(*orders):
        parts = [
            jnp.stack([part, swap(part, "bins", bins, bit)]) for part, bit in zip(parts, pair)
        ]
        if stages is not None:
            stages.append(parts)
    result = []
    for part, order in zip(parts, orders):
        held = list(reversed(order))
        shape = part.shape[len(order) :]
        axes = [held.index(bit) for bit in sorted(order, reverse=True)]
        axes += range(len(order), part.ndim)
        result.append(jnp.transpose(part, axes).reshape((bins,) + shape))
    return jnp.concatenate(result, axis=1)


def gather_chips(piece, fsdp, f, wait=None):
    chips = fsdp // 2
    pieces = [piece] + [swap(piece, "fsdp", fsdp, 2 * k) for k in range(1, chips)]
    if wait is not None:
        pieces = [after(item, wait) for item in pieces]
    pieces = ordered(pieces, f // 2)
    return jnp.stack(pieces[: chips // 2]), jnp.stack(pieces[chips // 2 :])


def gather_cores(own, fsdp, f):
    bins, chips, rows, width = own.shape
    other = swap(own, "fsdp", fsdp, 1)
    both = jnp.stack(ordered([own, other], f & 1), axis=2)
    return both.reshape(bins, fsdp * rows, width)


def block_of(owner):
    if isinstance(owner, int):
        return owner ^ 1 if owner < 2 else owner
    return jnp.where(owner < 2, owner ^ 1, owner)


def add_low(left, right):
    return (left.astype(F32) + right.astype(F32)).astype(BF)


def pick(value, index, axis):
    return lax.dynamic_index_in_dim(value, index, axis, keepdims=False)


def reduce_blocks(kept, given, first, bins, fsdp, f, stages, beside=None):
    count, _, _, width = kept.shape
    split = fsdp // 4
    bits = bits_of(split)[::-1]
    grads = add_low(kept, swap(given, "fsdp", fsdp, bits[0]))
    for bit in bits[1:]:
        view = grads.reshape(count, bins, 2, grads.shape[2] // 2, width)
        flag = jnp.where((f & bit) != 0, 1, 0)
        got = swap(pick(view, 1 - flag, 2), "fsdp", fsdp, bit)
        grads = add_low(pick(view, flag, 2), got)
    if beside is not None:
        beside("fsdp", fsdp, 1, grads)
    stages.append(grads)
    half = grads.shape[2] // 2
    orders = bin_orders(bins)
    parts, left = [], []
    for start, order in zip((0, half), orders):
        part = grads[:, :, start : start + half]
        parts.append(part.reshape((count,) + (2,) * len(order) + (half, width)))
        left.append(sorted(order, reverse=True))
    for pair in zip(*orders):
        for i, bit in enumerate(pair):
            where = 1 + left[i].index(bit)
            got = swap(lax.index_in_dim(parts[i], 1, where, False), "bins", bins, bit)
            parts[i] = add_low(lax.index_in_dim(parts[i], 0, where, False), got)
            left[i].remove(bit)
        if beside is not None:
            parts = [after(part, beside()) for part in parts]
            beside("bins", bins, pair[0], parts[0])
        stages.append(tuple(parts))
    part = jnp.concatenate(parts, axis=1)
    owner = f // split
    last = count - 1
    total = pick(part, jnp.clip(block_of(owner) - first, 0, last), 0).astype(F32)
    for k in range(1, 4):
        sent = pick(part, jnp.clip(block_of(owner ^ k) - first, 0, last), 0)
        got = swap(
            sent,
            "fsdp",
            fsdp,
            k * split,
            lambda t: first <= block_of(t // split) < first + count,
        )
        total = total + got.astype(F32)
    return total


def route_kernel(own_ref, slot_ref, tok_ref, cot_ref, tok_out, cot_out, map_out):
    model, slots = tok_ref.shape[2:]
    bins, _, cap, wide = tok_out.shape
    shift = slots.bit_length() - 1
    high = max(bins, 8)
    row_of = lax.broadcasted_iota(jnp.int32, (slots, slots), 0)
    col_of = lax.broadcasted_iota(jnp.int32, (slots, slots), 1)
    earlier = jnp.where(row_of < col_of, 1.0, 0.0).astype(BF)
    bin_of = lax.broadcasted_iota(jnp.int32, (high, slots), 0)
    slot = slot_ref[0]
    valid = slot >= 0
    safe = jnp.where(valid, slot, 0)
    relative = jnp.where(valid, (safe >> shift) ^ own_ref[0], high)
    onehot = jnp.where(bin_of == relative, 1.0, 0.0)
    before = mm(onehot.astype(BF), earlier)
    rank = jnp.sum(before * onehot, axis=0, keepdims=True).astype(jnp.int32)
    place = jnp.where(valid, relative * cap + rank, slots)
    send = jnp.where(row_of == place, 1.0, 0.0)
    map_out[0] = send.astype(BF)
    mark = jnp.where(valid, (safe & (slots - 1)) + 1, 0).astype(F32)
    marks = jnp.sum(send * mark, axis=1, keepdims=True)
    marks = jnp.broadcast_to(marks, (slots, wide - model)).astype(BF)
    tok = mm_t(send.astype(BF), tok_ref[0, 0]).astype(BF)
    cot = mm_t(send.astype(BF), cot_ref[0, 0]).astype(BF)
    for k in range(bins):
        rows = slice(k * cap, (k + 1) * cap)
        tok_out[k, 0, :, :model] = tok[rows]
        tok_out[k, 0, :, model:] = marks[rows]
        cot_out[k, 0] = cot[rows]


def vmem_specs(count):
    return [pl.BlockSpec(memory_space=pltpu.VMEM)] * count


def route(own, slot_rows, tokens, cotangent, bins):
    micro, _, model, slots = tokens.shape
    cap = slots // bins
    wide = model + (-model - 1) % 128 + 1
    block = pl.BlockSpec((1, 1, model, slots), lambda i: (i, 0, 0, 0))
    return pl.pallas_call(
        route_kernel,
        grid=(micro,),
        in_specs=[
            pl.BlockSpec(memory_space=pltpu.SMEM),
            pl.BlockSpec((1, 1, slots), lambda i: (i, 0, 0)),
            block,
            block,
        ],
        out_specs=[
            pl.BlockSpec((bins, 1, cap, wide), lambda i: (0, i, 0, 0)),
            pl.BlockSpec((bins, 1, cap, model), lambda i: (0, i, 0, 0)),
            pl.BlockSpec((1, slots, slots), lambda i: (i, 0, 0)),
        ],
        out_shape=[
            jax.ShapeDtypeStruct((bins, micro, cap, wide), BF),
            jax.ShapeDtypeStruct((bins, micro, cap, model), BF),
            jax.ShapeDtypeStruct((micro, slots, slots), BF),
        ],
        name="route",
    )(own, slot_rows, tokens, cotangent)


def unroute_kernel(*refs):
    map_ref = refs[0]
    out_one, out_two, home_ref = refs[-3:]
    pieces = refs[1:-3]
    bins = len(pieces) // 2
    cap = pieces[0].shape[1]
    for out, group in ((out_one, pieces[:bins]), (out_two, pieces[bins:])):
        for k, piece in enumerate(group):
            home_ref[k * cap : (k + 1) * cap, :] = piece[0]
        out[0, 0] = t_mm(home_ref[...], map_ref[0]).astype(BF)


def unroute(send_map, one, two):
    micro, slots, _ = send_map.shape
    cap, model = one[0].shape[1:]
    pieces = list(one) + list(two)
    out = jax.ShapeDtypeStruct((micro, 1, model, slots), BF)
    block = pl.BlockSpec((1, 1, model, slots), lambda i: (i, 0, 0, 0))
    return pl.pallas_call(
        unroute_kernel,
        grid=(micro,),
        in_specs=[pl.BlockSpec((1, slots, slots), lambda i: (i, 0, 0))]
        + [pl.BlockSpec((1, cap, model), lambda i: (i, 0, 0))] * len(pieces),
        out_specs=[block, block],
        out_shape=[out, out],
        scratch_shapes=[pltpu.VMEM((slots, model), BF)],
        name="unroute",
    )(send_map, *pieces)


def split_rows(acc_ref, own_ref, keep_ref, give_ref, index, start, width):
    half = keep_ref.shape[-2]
    mine = pl.ds(pl.multiple_of(own_ref[2] * half, 8), half)
    other = pl.ds(pl.multiple_of((1 - own_ref[2]) * half, 8), half)
    keep_ref[index] = acc_ref[mine, start : start + width].astype(BF)
    give_ref[index] = acc_ref[other, start : start + width].astype(BF)


def add_moment(acc_ref, own_ref, moment, start, width):
    high = moment.shape[0]
    if high % 8 == 0:
        rows = pl.ds(pl.multiple_of(own_ref[1] * high, 8), high)
        acc_ref[rows, start : start + width] += moment
        return
    for i in range(acc_ref.shape[0] // high):

        @pl.when(own_ref[1] == i)
        def _():
            acc_ref[i * high : (i + 1) * high, start : start + width] += moment


def give_back(values, land_ref, back_ref, m):
    bins, _, cap, _ = back_ref.shape
    back = mm(land_ref, values).astype(BF)
    for k in range(bins):
        back_ref[k, m] = back[k * cap : (k + 1) * cap]


def feed_kernel(own_ref, a2_ref, up_grad_ref, w_ref, moment_ref, h_ref, land_ref,
                dh2_ref, keep_ref, give_ref, back_ref,
                a2t_ref, gt_ref, act_ref, du_ref, acc_ref, y_ref):
    step = pl.program_id(0)
    tokens = a2_ref.shape[0]
    chunk = 256

    @pl.when(step == 0)
    def _():
        a2t_ref[...] = a2_ref[...].T
        gt_ref[...] = up_grad_ref[...].T
        y_ref[...] = h_ref[...]
        dh2_ref[...] = jnp.zeros_like(dh2_ref)

    width = w_ref.shape[3] // 3
    w_both = w_ref[0, 0, :, : 2 * width]
    w_down = w_ref[0, 0, :, 2 * width :]
    for start in range(0, tokens, chunk):
        rows = pl.ds(start, chunk)
        a2 = a2_ref[rows, :]
        both = mm(a2, w_both)
        gate = both[:, :width]
        up = both[:, width:]
        dact = mm(up_grad_ref[rows, :], w_down)
        sig = 1.0 / (1.0 + jnp.exp(-gate))
        silu = gate * sig
        act = (silu * up).astype(BF)
        dgate = (dact * up * sig * (1.0 + gate * (1.0 - sig))).astype(BF)
        dup = (dact * silu).astype(BF)
        act_ref[rows, :] = act
        du_ref[rows, :width] = dgate
        du_ref[rows, width:] = dup
        y_ref[rows, :] += mm_t(act, w_down)
        dh2_ref[rows, :] += mm_t(du_ref[rows, :], w_both)
    acc_ref[:, : 2 * width] = mm(a2t_ref[...], du_ref[...])
    acc_ref[:, 2 * width :] = mm(gt_ref[...], act_ref[...])

    @pl.when(step == 0)
    def _():
        for index in range(3):
            add_moment(acc_ref, own_ref, moment_ref[index], index * width, width)

    for index in range(3):
        split_rows(
            acc_ref, own_ref, keep_ref, give_ref, (index, 0), index * width, width
        )

    @pl.when(step == pl.num_programs(0) - 1)
    def _():
        micro, slots, _ = land_ref.shape
        for m in range(micro):
            rows = slice(m * slots, (m + 1) * slots)
            give_back(y_ref[rows, :].astype(BF), land_ref[m], back_ref, m)


def feed_forward_back(own, a2, up_grad, weights, moments, h, land):
    tokens, model = a2.shape
    _, bins, _, width = weights.shape
    width = width // 3
    micro, slots, _ = land.shape
    cap = slots // bins
    whole = pl.BlockSpec((tokens, model), lambda i, own_ref: (0, 0))
    halves = pl.BlockSpec((3, 1, model // 2, width), lambda i, own_ref: (0, i, 0, 0))
    block = pl.BlockSpec((1, 1, model, 3 * width), lambda i, own_ref: (0, i, 0, 0))
    return pl.pallas_call(
        feed_kernel,
        grid_spec=pltpu.PrefetchScalarGridSpec(
            num_scalar_prefetch=1,
            grid=(bins,),
            in_specs=[
                whole,
                whole,
                block,
                pl.BlockSpec(moments.shape, lambda i, own_ref: (0, 0, 0)),
                whole,
                pl.BlockSpec(land.shape, lambda i, own_ref: (0, 0, 0)),
            ],
            out_specs=[
                whole,
                halves,
                halves,
                pl.BlockSpec((bins, micro, cap, model), lambda i, own_ref: (0, 0, 0, 0)),
            ],
            scratch_shapes=[
                pltpu.VMEM((model, tokens), BF),
                pltpu.VMEM((model, tokens), BF),
                pltpu.VMEM((tokens, width), BF),
                pltpu.VMEM((tokens, 2 * width), BF),
                pltpu.VMEM((model, 3 * width), F32),
                pltpu.VMEM((tokens, model), F32),
            ],
        ),
        out_shape=[
            jax.ShapeDtypeStruct((tokens, model), F32),
            jax.ShapeDtypeStruct((3, bins, model // 2, width), BF),
            jax.ShapeDtypeStruct((3, bins, model // 2, width), BF),
            jax.ShapeDtypeStruct((bins, micro, cap, model), BF),
        ],
        name="feed",
    )(own, a2, up_grad, weights, moments, h, land)


def finish_kernel(gain_rate, own_ref, *refs):
    pieces, moments, outs = refs[:4], refs[4:6], refs[6:]
    width = pieces[0].shape[2]
    rows = moments[0].shape[1]
    q_cols = width * 3 // 8
    k_cols = width // 8

    def block(index, kind):
        place = own_ref[0] ^ block_of(index)
        value = pieces[0][kind, :rows].astype(F32)
        for k in range(1, 4):
            value = jnp.where(place == k, pieces[k][kind, :rows].astype(F32), value)
        return value

    def lanes(start, count):
        source = lax.broadcasted_iota(jnp.int32, (width, count), 0)
        target = lax.broadcasted_iota(jnp.int32, (width, count), 1)
        return jnp.where(source == target + start, 1.0, 0.0).astype(BF)

    narrow = -math.sqrt(HEADS / KV_HEADS)
    for kind in range(2):
        zero = block(0, kind).astype(BF)
        for i, start in enumerate((q_cols, q_cols + k_cols)):
            value = dot(lanes(start, k_cols), zero, ((0,), (1,)))
            outs[2 + 2 * i + kind][...] = narrow * value if kind else value
        for i, start in ((0, 0), (6, q_cols + 2 * k_cols)):
            value = mm(zero, lanes(start, q_cols))
            outs[i + kind][...] = -value if kind else value
        for index in range(1, 4):
            value = block(index, kind)
            rate = -DOWN_RATE if index == 3 else -1.0
            outs[6 + 2 * index + kind][...] = rate * value if kind else value
        grad = sum(piece[kind, rows : rows + 1, :rows].astype(F32) for piece in pieces)
        value = 0.5 * moments[kind][...] + 0.5 * grad
        outs[14 + 2 * kind][...] = value
        outs[15 + 2 * kind][...] = -gain_rate * value


def finish(own, pieces, moments, gain_rate):
    width = pieces[0].shape[2]
    rows = moments[0].shape[1]
    q_cols = width * 3 // 8
    k_cols = width // 8
    shapes = [(rows, q_cols)] * 2 + [(k_cols, rows)] * 4 + [(rows, q_cols)] * 2
    shapes += [(rows, width)] * 6 + [(1, rows)] * 4
    return pl.pallas_call(
        functools.partial(finish_kernel, gain_rate),
        grid=(1,),
        in_specs=[pl.BlockSpec(memory_space=pltpu.SMEM)]
        + [full_spec(piece.shape) for piece in (*pieces, *moments)],
        out_specs=[full_spec(shape) for shape in shapes],
        out_shape=[jax.ShapeDtypeStruct(shape, F32) for shape in shapes],
        name="finish",
    )(own, *pieces, *moments)


def newton_kernel(kind_ref, state_ref, out_ref, z_ref, zb_ref, a_ref, ab_ref, pb_ref):
    bins, size, width = state_ref.shape
    quarter = width * 3 // 8
    eighth = width // 8

    def run(size, cols, total):
        groups = [(i, min(128, size - i)) for i in range(0, size, 128)]
        chunks = [(i, min(384, size - i)) for i in range(0, size, 384)]
        scale = 1.0 / (jnp.sqrt(jnp.full((1, 1), total, F32)) + 1e-07)
        for start, high in chunks:
            rows = slice(start, start + high)
            value = z_ref[rows, :cols] * scale
            z_ref[rows, :cols] = value
            zb_ref[rows, :cols] = value.astype(BF)

        def diagonal(ref, target, start, high):
            downs, acrosses = [], []
            for spot, count in groups:
                if start <= spot < start + high:
                    rows = slice(spot, spot + count)
                    tile = ref[spot - start : spot - start + count, rows]
                    row_of = lax.broadcasted_iota(jnp.int32, (count, count), 0)
                    eye = row_of == lax.broadcasted_iota(jnp.int32, (count, count), 1)
                    value = jnp.where(eye, tile, 0.0)
                    target[rows, rows] = jnp.where(eye, 0.0, tile).astype(BF)
                    downs.append(jnp.sum(value, axis=1, keepdims=True))
                    acrosses.append(jnp.sum(value, axis=0, keepdims=True))
            down = downs[0] if len(downs) == 1 else jnp.concatenate(downs, axis=0)
            return down, acrosses

        def step(index, carry):
            downs, across = [], []
            for start, high in chunks:
                rows = slice(start, start + high)
                gram = mm_t(zb_ref[rows, :cols], zb_ref[:size, :cols])
                a_ref[rows, :size] = gram
                ab_ref[rows, :size] = gram.astype(BF)
                down, parts = diagonal(gram, ab_ref, start, high)
                downs.append(down)
                across += parts
            across = jnp.concatenate(across, axis=1)
            diags = []
            for (start, high), down in zip(chunks, downs):
                rows = slice(start, start + high)
                square = mm(ab_ref[rows, :size], ab_ref[:size, :size])
                factor = (COEFF_B + COEFF_C * down) + COEFF_C * across
                poly = a_ref[rows, :size] * factor + COEFF_C * square
                pb_ref[rows, :size] = poly.astype(BF)
                diag, _ = diagonal(poly, pb_ref, start, high)
                diags.append(COEFF_A + diag - COEFF_C * down * down)
            for (start, high), diag in zip(chunks, diags):
                rows = slice(start, start + high)
                value = diag * z_ref[rows, :cols] + mm(pb_ref[rows, :size], zb_ref[:size, :cols])
                z_ref[rows, :cols] = value
            for start, high in chunks:
                rows = slice(start, start + high)
                zb_ref[rows, :cols] = z_ref[rows, :cols].astype(BF)
            return carry

        lax.fori_loop(0, NS_STEPS, step, 0)

    def keep_lanes(first, wide, low, high):
        lane = lax.broadcasted_iota(jnp.int32, (size, wide), 1) + first
        return (lane >= low) & (lane < high)

    def put(first, wide, low, high, mine):
        keep = keep_lanes(first, wide, low, high)
        old = out_ref[:, first : first + wide].astype(F32)
        out_ref[:, first : first + wide] = jnp.where(keep, mine.astype(F32), old).astype(BF)

    def load(wide, fetch):
        total = jnp.zeros((), F32)
        for j in range(bins):
            piece = fetch(j)
            z_ref[:, j * wide : (j + 1) * wide] = piece
            total = total + jnp.sum(piece * piece)
        run(size, wide * bins, total)

    kind = kind_ref[0]

    @pl.when(kind == 0)
    def _():
        load(width, lambda j: state_ref[j].astype(F32))
        out_ref[...] = zb_ref[:, :width]

    large = 256 if width == 384 else width
    small = 128 if width == 384 else width
    middle = 128 if width == 384 else 0
    k_low = jnp.where(kind == 1, quarter, quarter + eighth)

    @pl.when(kind != 0)
    def _():
        out_ref[...] = jnp.zeros_like(out_ref)

        def large_piece(j):
            low = state_ref[j, :, :large].astype(F32)
            low = jnp.where(keep_lanes(0, large, 0, quarter), low, 0.0)
            high = state_ref[j, :, width - large :].astype(F32)
            high = jnp.where(
                keep_lanes(width - large, large, width - quarter, width), high, 0.0
            )
            return jnp.where(kind == 1, low, high)

        load(large, large_piece)

        @pl.when(kind == 1)
        def _():
            put(0, large, 0, quarter, zb_ref[:, :large])

        @pl.when(kind != 1)
        def _():
            put(width - large, large, width - quarter, width, zb_ref[:, :large])

        narrow = bins * eighth
        lane = lax.broadcasted_iota(jnp.int32, (small, narrow), 0) + middle - k_low
        column = lax.broadcasted_iota(jnp.int32, (small, narrow), 1)
        inside = (lane >= 0) & (lane < eighth)
        turned = jnp.zeros((narrow, size), F32)
        for j in range(bins):
            chosen = jnp.where(inside & (column == lane + j * eighth), 1.0, 0.0).astype(BF)
            piece = state_ref[j, :, middle : middle + small]
            turned = turned + dot(chosen, piece, ((0,), (1,)))
        z_ref[:narrow, :size] = turned
        run(narrow, size, jnp.sum(turned * turned))
        chosen = jnp.where(inside & (column == lane), 1.0, 0.0).astype(BF)
        back = dot(zb_ref[:narrow, :size], chosen, ((0,), (1,)))
        put(middle, small, k_low, k_low + eighth, back)


def newton(kind, state):
    bins, size, width = state.shape
    cols = bins * width
    return pl.pallas_call(
        newton_kernel,
        in_specs=[
            pl.BlockSpec(memory_space=pltpu.SMEM),
            pl.BlockSpec(memory_space=pltpu.VMEM),
        ],
        out_specs=pl.BlockSpec(memory_space=pltpu.VMEM),
        out_shape=jax.ShapeDtypeStruct((size, width), BF),
        scratch_shapes=[
            pltpu.VMEM((size, cols), F32),
            pltpu.VMEM((size, cols), BF),
            pltpu.VMEM((size, size), F32),
            pltpu.VMEM((size, size), BF),
            pltpu.VMEM((size, size), BF),
        ],
        name="newton",
    )(kind, state)


def half_swap(value):
    lane = lax.broadcasted_iota(jnp.int32, value.shape, 1)
    low = (lane % HEAD_DIM) < HEAD_DIM // 2
    return jnp.where(low, pltpu.roll(value, 96, 1), pltpu.roll(value, 32, 1))


def twice(value, upper):
    lane = lax.broadcasted_iota(jnp.int32, value.shape, 1)
    keep = (lane >= HEAD_DIM) if upper else (lane < HEAD_DIM)
    part = jnp.where(keep, value, 0.0)
    return part + pltpu.roll(part, HEAD_DIM, 1)


def fold(value):
    return value + pltpu.roll(value, HEAD_DIM, 1)


PAIRS = (HEADS + 1) // 2
KV_PAIRS = (KV_HEADS + 1) // 2
Q_WIDE = PAIRS * 128
KV_WIDE = KV_PAIRS * 128
WIDE = Q_WIDE + 2 * KV_WIDE
SCALE = 1.0 / math.sqrt(HEAD_DIM)


def soft_rows(query, key, allowed):
    scores = jnp.where(allowed, mm_t(query, key) * SCALE, NEGATIVE)
    raised = jnp.exp(scores - jnp.max(scores, axis=1, keepdims=True))
    return raised * (1.0 / jnp.sum(raised, axis=1, keepdims=True))


def allow(seg_col, seg_row):
    size = seg_row.shape[1]
    row = lax.broadcasted_iota(jnp.int32, (size, size), 0)
    col = lax.broadcasted_iota(jnp.int32, (size, size), 1)
    return (seg_col == seg_row) & (col <= row)


def key_pair(qkv, base, kv):
    group = qkv[:, base + (kv // 2) * 128 : base + (kv // 2) * 128 + 128].astype(F32)
    return twice(group, kv % 2 == 1).astype(BF)


def masked_half(group, head):
    lane = lax.broadcasted_iota(jnp.int32, group.shape, 1)
    keep = (lane >= HEAD_DIM) if head % 2 else (lane < HEAD_DIM)
    return jnp.where(keep, group.astype(F32), 0.0).astype(BF)


def take_columns(w_ref, own, kind_start, cols, start, wide, bins):
    width = w_ref.shape[2]
    source = lax.broadcasted_iota(jnp.int32, (width, wide), 0)
    target = lax.broadcasted_iota(jnp.int32, (width, wide), 1) + start
    inside = (source >= kind_start) & (source < kind_start + cols)
    result = None
    for j in range(start // cols, min((start + wide - 1) // cols, bins - 1) + 1):
        chosen = inside & (source - kind_start == target - j * cols)
        part = mm(w_ref[own ^ j], jnp.where(chosen, 1.0, 0.0).astype(BF))
        result = part if result is None else result + part
    return result.astype(BF)


def attend_kernel(*refs):
    own_ref = refs[0]
    bins = (len(refs) - 23) // 2
    toks = refs[1 : 1 + bins]
    cots = refs[1 + bins : 1 + 2 * bins]
    (gain_in, w_ref, cos_ref, sin_ref, sc_ref, sr_ref,
     x_ref, g_ref, land_ref, a1_ref, qkv_ref, ob_ref, h_ref, a2_ref, wqkv_ref, wo_ref, gain_ref,
     got_ref, got2_ref, land_t, keys_ref, values_ref) = refs[1 + 2 * bins :]
    slots, model = x_ref.shape
    cap = slots // bins
    width = w_ref.shape[2]
    q_cols = width * 3 // 8
    k_cols = width // 8

    @pl.when(pl.program_id(0) == 0)
    def _():
        row = lax.broadcasted_iota(jnp.int32, (model, model), 0)
        eye = row == lax.broadcasted_iota(jnp.int32, (model, model), 1)
        for i in range(2):
            column = gain_in[:, i : i + 1].astype(F32)
            gain_ref[i : i + 1, :] = jnp.sum(
                jnp.where(eye, column, 0.0), axis=0, keepdims=True
            )
        for tile in range(WIDE // 128):
            if tile < PAIRS:
                spot = (0, q_cols, tile * 128)
            elif tile < PAIRS + KV_PAIRS:
                spot = (q_cols, k_cols, (tile - PAIRS) * 128)
            else:
                spot = (q_cols + k_cols, k_cols, (tile - PAIRS - KV_PAIRS) * 128)
            wqkv_ref[:, tile * 128 : tile * 128 + 128] = take_columns(
                w_ref, own_ref[0], *spot, 128, bins
            )
        for tile in range(PAIRS):
            wo_ref[:, tile * 128 : tile * 128 + 128] = take_columns(
                w_ref, own_ref[0], q_cols + 2 * k_cols, q_cols, tile * 128, 128, bins
            )

    spot = lax.broadcasted_iota(jnp.int32, (cap, slots), 1)
    for k in range(bins):
        rows = slice(k * cap, (k + 1) * cap)
        place = toks[k][0, :, model : model + 1].astype(F32).astype(jnp.int32) - 1
        land = jnp.where(spot == place, 1.0, 0.0).astype(BF)
        land_t[rows, :] = land
        got_ref[rows, :] = toks[k][0, :, :model]
        got2_ref[rows, :] = cots[k][0]
    land_ref[0] = land_t[...]
    x = t_mm(land_t[...], got_ref[...])
    x_ref[...] = x.astype(BF)
    g_ref[...] = t_mm(land_t[...], got2_ref[...]).astype(BF)
    r1 = lax.rsqrt(jnp.mean(x * x, axis=1, keepdims=True) + EPSILON)
    a1 = (x * r1 * gain_ref[0:1, :]).astype(BF)
    a1_ref[...] = a1
    cosine = cos_ref[...]
    sine = sin_ref[...]
    for start in range(0, WIDE, 256):
        wide = min(256, WIDE - start)
        both = mm(a1, wqkv_ref[:, start : start + wide])
        for spot in range(0, wide, 128):
            value = both[:, spot : spot + 128]
            if start + spot < Q_WIDE + KV_WIDE:
                value = value * cosine + half_swap(value) * sine
            qkv_ref[:, start + spot : start + spot + 128] = value.astype(BF)
    allowed = allow(sc_ref[0], sr_ref[0])
    for kv in range(KV_HEADS):
        keys_ref[kv] = key_pair(qkv_ref, Q_WIDE, kv)
        values_ref[kv] = key_pair(qkv_ref, Q_WIDE + KV_WIDE, kv)
    lane = lax.broadcasted_iota(jnp.int32, (slots, 128), 1)

    def one_pair(pair):
        lanes = slice(pair * 128, pair * 128 + 128)
        group = qkv_ref[:, lanes]
        parts = []
        for half in range(min(2, HEADS - 2 * pair)):
            kv = (2 * pair + half) // GROUPS
            soft = soft_rows(masked_half(group, half), keys_ref[kv], allowed)
            parts.append(mm(soft.astype(BF), values_ref[kv]))
        parts.append(jnp.zeros((slots, 128), F32))
        ob_ref[:, lanes] = jnp.where(lane < HEAD_DIM, parts[0], parts[1]).astype(BF)

    for pair in range(PAIRS):
        one_pair(pair)
    h = x + mm(ob_ref[:, :model], wo_ref[:, :model])
    h_ref[...] = h
    r2 = lax.rsqrt(jnp.mean(h * h, axis=1, keepdims=True) + EPSILON)
    a2_ref[...] = (h * r2 * gain_ref[1:2, :]).astype(BF)


def row_spec(slots, width):
    return pl.BlockSpec((slots, width), lambda i: (i, 0))


def full_spec(shape):
    return pl.BlockSpec(shape, lambda i: (0,) * len(shape))


def attend(own, toks, cots, gains, weights, cosine, sine, seg_col, seg_row):
    bins, model, _ = weights.shape
    micro, _, slots = seg_row.shape
    total = micro * slots
    cap = slots // bins
    row_shapes = ((model, BF), (WIDE, BF), (Q_WIDE, BF), (model, F32), (model, BF))
    wide = toks[0].shape[2]
    return pl.pallas_call(
        attend_kernel,
        grid=(micro,),
        in_specs=[pl.BlockSpec(memory_space=pltpu.SMEM)]
        + [pl.BlockSpec((1, cap, wide), lambda i: (i, 0, 0))] * bins
        + [pl.BlockSpec((1, cap, model), lambda i: (i, 0, 0))] * bins
        + [
            full_spec(gains.shape), full_spec(weights.shape),
            row_spec(slots, 128), row_spec(slots, 128),
            pl.BlockSpec((1, slots, 1), lambda i: (i, 0, 0)),
            pl.BlockSpec((1, 1, slots), lambda i: (i, 0, 0)),
        ],
        out_specs=[
            row_spec(slots, model), row_spec(slots, model),
            pl.BlockSpec((1, slots, slots), lambda i: (i, 0, 0)),
        ]
        + [row_spec(slots, wide) for wide, _ in row_shapes]
        + [full_spec((model, WIDE)), full_spec((model, Q_WIDE)), full_spec((2, model))],
        out_shape=[
            jax.ShapeDtypeStruct((total, model), BF),
            jax.ShapeDtypeStruct((total, model), BF),
            jax.ShapeDtypeStruct((micro, slots, slots), BF),
        ]
        + [jax.ShapeDtypeStruct((total, wide), kind) for wide, kind in row_shapes]
        + [
            jax.ShapeDtypeStruct((model, WIDE), BF),
            jax.ShapeDtypeStruct((model, Q_WIDE), BF),
            jax.ShapeDtypeStruct((2, model), F32),
        ],
        scratch_shapes=[
            pltpu.VMEM((slots, model), BF),
            pltpu.VMEM((slots, model), BF),
            pltpu.VMEM((slots, slots), BF),
            pltpu.VMEM((KV_HEADS, slots, 128), BF),
            pltpu.VMEM((KV_HEADS, slots, 128), BF),
        ],
        name="attend",
    )(own, *toks, *cots, gains, weights, cosine, sine, seg_col, seg_row)


def attend_back_kernel(own_ref, x_ref, gain_ref, wqkv_ref, wo_ref, cos_ref, sin_ref, sc_ref,
                       sr_ref, a1_ref, qkv_ref, ob_ref, h_ref, dh2_ref, g_ref, land_ref,
                       moment_ref, back_ref, gains_ref, keep_ref, give_ref,
                       a1_all, ob_all, d_all, dhb_all, acc_ref, dob_ref,
                       keys_ref, values_ref, dkeys, dvalues):
    step = pl.program_id(0)
    slots, model = x_ref.shape
    rows = pl.ds(pl.multiple_of(step * slots, slots), slots)

    @pl.when(step == 0)
    def _():
        gains_ref[...] = jnp.zeros_like(gains_ref)

    h = h_ref[...]
    dh2 = dh2_ref[...]
    r2 = lax.rsqrt(jnp.mean(h * h, axis=1, keepdims=True) + EPSILON)
    scaled = dh2 * gain_ref[1:2, :]
    inner = jnp.mean(scaled * h, axis=1, keepdims=True)
    dh = g_ref[...].astype(F32) + r2 * scaled - h * (r2 * r2 * r2 * inner)
    gains_ref[1:2, :] += jnp.sum(dh2 * h * r2, axis=0, keepdims=True)
    dhb = dh.astype(BF)
    dhb_all[rows, :] = dhb
    a1_all[:, rows] = a1_ref[...].T
    ob_all[:, rows] = ob_ref[:, :model].T
    allowed = allow(sc_ref[0], sr_ref[0])
    for kv in range(KV_HEADS):
        keys_ref[kv] = key_pair(qkv_ref, Q_WIDE, kv)
        values_ref[kv] = key_pair(qkv_ref, Q_WIDE + KV_WIDE, kv)
    dkeys[...] = jnp.zeros_like(dkeys)
    dvalues[...] = jnp.zeros_like(dvalues)
    dob_ref[:, :model] = mm_t(dhb, wo_ref[:, :model]).astype(BF)
    dob_ref[:, model:] = jnp.zeros((slots, Q_WIDE - model), BF)
    cosine = cos_ref[...]
    sine = sin_ref[...]
    lane = lax.broadcasted_iota(jnp.int32, (slots, 128), 1)

    def one_pair(pair):
        lanes = slice(pair * 128, pair * 128 + 128)
        group = qkv_ref[:, lanes]
        dob = dob_ref[:, lanes]
        parts = []
        for half in range(min(2, HEADS - 2 * pair)):
            kv = (2 * pair + half) // GROUPS
            query = masked_half(group, half)
            soft = soft_rows(query, keys_ref[kv], allowed)
            mine = masked_half(dob, half)
            dp = mm_t(mine, values_ref[kv])
            ds = (soft * (dp - jnp.sum(soft * dp, axis=1, keepdims=True))).astype(BF)
            parts.append(mm(ds, keys_ref[kv]))
            dkeys[kv] += t_mm(ds, query)
            dvalues[kv] += t_mm(soft.astype(BF), mine)
        parts.append(jnp.zeros((slots, 128), F32))
        out = jnp.where(lane < HEAD_DIM, parts[0], parts[1]) * SCALE
        out = out * cosine - half_swap(out) * sine
        d_all[rows, lanes] = out.astype(BF)

    for pair in range(PAIRS):
        one_pair(pair)
    for pair in range(KV_PAIRS):
        lane = lax.broadcasted_iota(jnp.int32, (slots, 128), 1)

        def both(parts):
            low = fold(parts[2 * pair])
            high = fold(parts[2 * pair + 1]) if 2 * pair + 1 < KV_HEADS else 0.0
            return jnp.where(lane < HEAD_DIM, low, high)

        dk = both(dkeys) * SCALE
        dk = dk * cosine - half_swap(dk) * sine
        start = Q_WIDE + pair * 128
        d_all[rows, start : start + 128] = dk.astype(BF)
        start += KV_WIDE
        d_all[rows, start : start + 128] = both(dvalues).astype(BF)
    dh1 = mm_t(d_all[rows, :], wqkv_ref[...])
    x = x_ref[...].astype(F32)
    r1 = lax.rsqrt(jnp.mean(x * x, axis=1, keepdims=True) + EPSILON)
    scaled = dh1 * gain_ref[0:1, :]
    inner = jnp.mean(scaled * x, axis=1, keepdims=True)
    dx = dh + r1 * scaled - x * (r1 * r1 * r1 * inner)
    gains_ref[0:1, :] += jnp.sum(dh1 * x * r1, axis=0, keepdims=True)
    give_back(dx.astype(BF), land_ref[0], back_ref, step)

    @pl.when(step == pl.num_programs(0) - 1)
    def _():
        width = acc_ref.shape[1]
        bins = keep_ref.shape[0]
        q_cols = width * 3 // 8
        k_cols = width // 8
        wide = 256 if width == 384 else width
        skip = width - wide
        spot = lax.broadcasted_iota(jnp.int32, (1, wide), 1)
        late = spot + skip - (q_cols + 2 * k_cols)
        for k in range(bins):
            j = own_ref[0] ^ k
            target = jnp.where(
                spot < q_cols,
                j * q_cols + spot,
                jnp.where(
                    spot < q_cols + k_cols,
                    Q_WIDE + j * k_cols + spot - q_cols,
                    jnp.where(
                        spot < q_cols + 2 * k_cols,
                        Q_WIDE + KV_WIDE + j * k_cols + spot - q_cols - k_cols,
                        -1,
                    ),
                ),
            )
            source = lax.broadcasted_iota(jnp.int32, (WIDE, wide), 0)
            chosen = mm(d_all[...], jnp.where(source == target, 1.0, 0.0).astype(BF))
            first = mm(a1_all[...], chosen.astype(BF))
            target = jnp.where(late >= 0, j * q_cols + late, -1)
            source = lax.broadcasted_iota(jnp.int32, (model, wide), 0)
            chosen = mm(dhb_all[...], jnp.where(source == target, 1.0, 0.0).astype(BF))
            second = mm(ob_all[...], chosen.astype(BF))
            if skip:
                acc_ref[:, :skip] = first[:, :skip]
                acc_ref[:, skip:wide] = first[:, skip:] + second[:, : wide - skip]
                acc_ref[:, wide:] = second[:, wide - skip :]
            else:
                acc_ref[...] = first + second
            if k == 0:
                add_moment(acc_ref, own_ref, moment_ref[...], 0, width)
            split_rows(acc_ref, own_ref, keep_ref, give_ref, k, 0, width)


def attend_back(own, x, gains, wqkv, wo, cosine, sine, seg_col, seg_row,
                a1, qkv, ob, h, dh2, g, land, moment, bins):
    total, model = x.shape
    micro, slots, _ = land.shape
    cap = slots // bins
    width = moment.shape[1]
    return pl.pallas_call(
        attend_back_kernel,
        grid=(micro,),
        in_specs=[
            pl.BlockSpec(memory_space=pltpu.SMEM),
            row_spec(slots, model), full_spec(gains.shape), full_spec(wqkv.shape),
            full_spec(wo.shape), row_spec(slots, 128), row_spec(slots, 128),
            pl.BlockSpec((1, slots, 1), lambda i: (i, 0, 0)),
            pl.BlockSpec((1, 1, slots), lambda i: (i, 0, 0)),
            row_spec(slots, model), row_spec(slots, WIDE), row_spec(slots, Q_WIDE),
            row_spec(slots, model), row_spec(slots, model), row_spec(slots, model),
            pl.BlockSpec((1, slots, slots), lambda i: (i, 0, 0)),
            full_spec(moment.shape),
        ],
        out_specs=[
            full_spec((bins, micro, cap, model)), full_spec((2, model)),
            full_spec((bins, model // 2, width)), full_spec((bins, model // 2, width)),
        ],
        out_shape=[
            jax.ShapeDtypeStruct((bins, micro, cap, model), BF),
            jax.ShapeDtypeStruct((2, model), F32),
            jax.ShapeDtypeStruct((bins, model // 2, width), BF),
            jax.ShapeDtypeStruct((bins, model // 2, width), BF),
        ],
        scratch_shapes=[
            pltpu.VMEM((model, total), BF),
            pltpu.VMEM((model, total), BF),
            pltpu.VMEM((total, WIDE), BF),
            pltpu.VMEM((total, model), BF),
            pltpu.VMEM((model, width), F32),
            pltpu.VMEM((slots, Q_WIDE), BF),
            pltpu.VMEM((KV_HEADS, slots, 128), BF),
            pltpu.VMEM((KV_HEADS, slots, 128), BF),
            pltpu.VMEM((KV_HEADS, slots, 128), F32),
            pltpu.VMEM((KV_HEADS, slots, 128), F32),
        ],
        name="attend_back",
    )(own, x, gains, wqkv, wo, cosine, sine, seg_col, seg_row,
      a1, qkv, ob, h, dh2, g, land, moment)


def rope_tables(positions):
    half_dim = HEAD_DIM // 2
    frequency = jnp.exp(
        -math.log(ROPE_BASE) * 2.0 * jnp.arange(half_dim, dtype=F32) / HEAD_DIM
    )
    angles = positions.reshape(-1).astype(F32)[:, None] * frequency
    cosine = jnp.cos(angles)
    sine = jnp.sin(angles)
    return (
        jnp.concatenate([cosine] * 4, axis=1),
        jnp.concatenate([-sine, sine, -sine, sine], axis=1),
    )


def slot_layout(lengths, starts, bin_slots):
    slot_index = jnp.arange(bin_slots, dtype=jnp.int32)
    inside = (
        (slot_index[:, None] >= starts[..., None, :])
        & (slot_index[:, None] < starts[..., None, :] + lengths[..., None, :])
    ).astype(jnp.int32)
    number = jnp.arange(lengths.shape[-1], dtype=jnp.int32)
    covered = jnp.minimum(jnp.sum(inside, axis=-1), 1)
    segment = jnp.sum(inside * number, axis=-1) + (1 - covered) * (
        lengths.shape[-1] + slot_index
    )
    first_slot = jnp.sum(inside * starts[..., None, :], axis=-1)
    return (segment, slot_index - first_slot)


def on_device(
    tokens, cotangent, token_slots, sequence_lengths, sequence_starts,
    query_weight, key_weight, value_weight, output_weight,
    gate_weight, up_weight, down_weight, attention_gain, feedforward_gain,
    query_moment, key_moment, value_moment, output_moment,
    gate_moment, up_moment, down_moment, attention_moment, feedforward_moment,
):
    bins = lax.axis_size("bins")
    fsdp = lax.axis_size("fsdp")
    b = lax.axis_index("bins")
    f = lax.axis_index("fsdp")
    micro, _, slots, model = tokens.shape
    total = micro * slots
    rows_own = query_weight.shape[0]
    q_cols = query_weight.shape[1]
    k_cols = key_weight.shape[1]
    split = fsdp // 4
    flag = jnp.where((f & (split // 2)) != 0, 1, 0)
    own = jnp.stack([b, f, flag]).astype(jnp.int32)

    block_zero = jnp.concatenate(
        [query_weight, key_weight, value_weight, output_weight], axis=1
    )[None]
    blocks = jnp.concatenate([gate_weight, up_weight, down_weight.T], axis=1)
    gain_lanes = jnp.pad(
        jnp.stack([attention_gain, feedforward_gain], axis=1), ((0, 0), (0, 126))
    )
    width = block_zero.shape[2]
    zero_chips = gather_chips(
        jnp.concatenate([block_zero[0], gain_lanes], axis=1), fsdp, f
    )
    gains_cols = jnp.concatenate([part[:, :, width:] for part in zero_chips])
    gains_cols = gather_cores(gains_cols[None], fsdp, f)[0]
    zero_chips = [part[:, :, :width] for part in zero_chips]

    tok_send, cot_send, send_map = route(
        own, token_slots, tokens.swapaxes(2, 3), cotangent.swapaxes(2, 3), bins
    )

    def exchange(pieces):
        return [pieces[0]] + [swap(pieces[k], "bins", bins, k) for k in range(1, bins)]

    toks = exchange(tok_send)
    zero_stages = []
    raw_chips = zero_chips
    zero_chips = [after(part, *toks) for part in zero_chips]
    zero_bins = gather_bins(*zero_chips, bins, zero_stages)
    feed_chips = gather_chips(after(blocks, *raw_chips), fsdp, f, zero_bins)
    cots = exchange(after(cot_send, *toks))

    segment, position = slot_layout(sequence_lengths[:, 0, 0], sequence_starts[:, 0, 0], slots)
    cosine, sine = rope_tables(position)

    attn_w = gather_cores(zero_bins, fsdp, f)
    first, second = feed_chips
    feed_stages = []
    ahead = (zero_bins, *cots)
    feed_bins = gather_bins(after(first, *ahead), after(second, *ahead), bins, feed_stages)
    attn_w = after(attn_w, *feed_stages[0])

    edges = (0, q_cols, q_cols + k_cols, q_cols + 2 * k_cols, width)
    seg_col = segment[:, :, None]
    seg_row = segment[:, None, :]
    tables = (cosine, sine, seg_col, seg_row)
    moments = jnp.stack([gate_moment, up_moment, down_moment.T])
    moment_zero = jnp.concatenate(
        [query_moment, key_moment, value_moment, output_moment], axis=1
    )
    gains_cols = after(gains_cols, moments, moment_zero)
    x_low, g_low, land, a1, qkv, ob, h, a2, w_qkv, w_o, gains_full = attend(
        own, toks, cots, gains_cols, attn_w, *tables
    )
    feed_w = gather_cores(after(feed_bins, a2), fsdp, f)

    dh2, kept, given, back = feed_forward_back(own, a2, g_low, feed_w[None], moments, h, land)
    one_stages = []
    part_one = reduce_blocks(kept, given, 1, bins, fsdp, f, one_stages)
    home_one = exchange(back)
    dh2 = after(dh2, one_stages[0])

    back, gain_sum, kept, given = attend_back(
        own, x_low, gains_full, w_qkv, w_o, *tables,
        a1, qkv, ob, h, dh2, g_low, land, moment_zero, bins,
    )
    zero_stages = []
    sums = [gain_sum]

    def beside(axis=None, count=None, bit=None, token=None):
        if axis is not None:
            sums.append(sums[-1] + swap(after(sums[-1], token), axis, count, bit))
        return sums[-1]

    kept = after(kept, *home_one)
    part_zero = reduce_blocks(kept[None], given[None], 0, bins, fsdp, f, zero_stages, beside)

    owner = f // split
    is_zero = block_of(owner) == 0
    state = (0.5 * jnp.where(is_zero, part_zero, part_one)).astype(BF)
    half = state.shape[0] // 2
    state = gather_bins(state[:half], state[half:], bins)
    home_two = exchange(after(back, state))
    for bit in bits_of(split)[1:]:
        beside("fsdp", fsdp, bit, state)
    gain_rows = jnp.pad(
        beside().astype(BF).reshape(2, fsdp, 1, rows_own),
        ((0, 0), (0, 0), (0, 7), (0, width - rows_own)),
    )
    for bit in bits_of(split):
        state = jnp.concatenate([state, swap(state, "fsdp", fsdp, bit)], axis=1)

    kind = jnp.stack([jnp.where(is_zero, 1 + (f & 1), 0), b]).astype(jnp.int32)
    ortho = newton(kind, state)
    other = swap(ortho, "fsdp", fsdp, 1)
    block_output, input_gradient = unroute(after(send_map, other), home_one, home_two)
    other = other.reshape(fsdp // 8, 2, -1, width)[:, ::-1].reshape(ortho.shape)
    lane = jnp.arange(width, dtype=jnp.int32)
    first_core = (lane < edges[2]).astype(jnp.int32)
    ortho = jnp.where(is_zero & (first_core == (f & 1)), other, ortho)

    both = jnp.stack([state[0], ortho]).reshape(2, fsdp, rows_own, width)
    low = f % split
    turn = low * 4

    def parcel(target):
        return jnp.concatenate(
            [pick(both, target ^ turn, 1), pick(gain_rows, target, 1)], axis=1
        )

    pieces = [parcel(f)]
    for k in range(1, 4):
        sent = parcel((owner ^ k) * split + low)
        pieces.append(swap(sent, "fsdp", fsdp, k * split))
    outs = [block_output.swapaxes(2, 3), input_gradient.swapaxes(2, 3)]
    gain_rate = 0.1 / math.sqrt(micro * bins * fsdp * slots)
    moments = (attention_moment[None], feedforward_moment[None])
    done = finish(owner.astype(jnp.int32)[None], pieces, moments, gain_rate)
    for i, value in enumerate(done):
        if i >= 14:
            outs.append(value[0])
        else:
            outs.append(value.T if i in (2, 3, 4, 5, 12, 13) else value)
    return tuple(outs)


def solution(mesh):
    rows = P(None, "fsdp", "bins", None)
    matrix = P("fsdp", "bins")
    turned = P("bins", "fsdp")
    vector = P("fsdp")
    params = (matrix,) * 6 + (turned, vector, vector)
    doubled = ()
    for spec in params:
        doubled += (spec, spec)
    return jax.shard_map(
        on_device,
        mesh=mesh,
        in_specs=(rows, rows, P(None, "fsdp", "bins"), rows, rows) + params + params,
        out_specs=(rows, rows) + doubled,
        check_vma=False,
    )
```

```python
import functools
import math

import jax
import jax.numpy as jnp
from jax import lax
from jax.experimental import pallas as pl
from jax.experimental.pallas import tpu as pltpu
from jax.sharding import PartitionSpec as P

HEADS = 9
KV_HEADS = 3
HEAD_DIM = 64
GROUPS = HEADS // KV_HEADS
NS_STEPS = 5
HIDDEN_RATIO = 1536 / 576
DOWN_RATE = math.sqrt(HIDDEN_RATIO)
EPSILON = 1e-05
NEGATIVE = -1e30
ROPE_BASE = 10000.0
COEFF_A = 3.4445
COEFF_B = -4.775
COEFF_C = 2.0315
BF = jnp.bfloat16
F32 = jnp.float32


def dot(left, right, dims):
    return lax.dot_general(left, right, (dims, ((), ())), preferred_element_type=F32)


def mm(left, right):
    return dot(left, right, ((left.ndim - 1,), (0,)))


def mm_t(left, right):
    return dot(left, right, ((left.ndim - 1,), (1,)))


def t_mm(left, right):
    return dot(left, right, ((0,), (0,)))


def swap(value, axis, count, step, keep=None):
    pairs = [(i, i ^ step) for i in range(count) if keep is None or keep(i ^ step)]
    return lax.ppermute(value, axis, pairs)


def bits_of(count):
    return [1 << i for i in range(count.bit_length() - 1)]


def ordered(pieces, index):
    result = list(pieces)
    for bit in bits_of(len(pieces)):
        flag = (index & bit) != 0
        result = [jnp.where(flag, result[j ^ bit], result[j]) for j in range(len(result))]
    return result


def join(mine, other, flag):
    return jnp.stack([jnp.where(flag, other, mine), jnp.where(flag, mine, other)])


def after(value, *others):
    return lax.optimization_barrier((value,) + others)[0]


def bin_orders(bins):
    bits = bits_of(bins)
    half = len(bits) // 2
    return bits, bits[half:] + bits[:half]


def gather_bins(first, second, bins, stages=None):
    orders = bin_orders(bins)
    parts = [first, second]
    for pair in zip(*orders):
        parts = [
            jnp.stack([part, swap(part, "bins", bins, bit)]) for part, bit in zip(parts, pair)
        ]
        if stages is not None:
            stages.append(parts)
    result = []
    for part, order in zip(parts, orders):
        held = list(reversed(order))
        shape = part.shape[len(order) :]
        axes = [held.index(bit) for bit in sorted(order, reverse=True)]
        axes += range(len(order), part.ndim)
        result.append(jnp.transpose(part, axes).reshape((bins,) + shape))
    return jnp.concatenate(result, axis=1)


def gather_chips(piece, fsdp, f, wait=None):
    chips = fsdp // 2
    pieces = [piece] + [swap(piece, "fsdp", fsdp, 2 * k) for k in range(1, chips)]
    if wait is not None:
        pieces = [after(item, wait) for item in pieces]
    pieces = ordered(pieces, f // 2)
    return jnp.stack(pieces[: chips // 2]), jnp.stack(pieces[chips // 2 :])


def gather_cores(own, fsdp, f):
    bins, chips, rows, width = own.shape
    other = swap(own, "fsdp", fsdp, 1)
    both = jnp.stack(ordered([own, other], f & 1), axis=2)
    return both.reshape(bins, fsdp * rows, width)


def block_of(owner):
    if isinstance(owner, int):
        return owner ^ 1 if owner < 2 else owner
    return jnp.where(owner < 2, owner ^ 1, owner)


def add_low(left, right):
    return (left.astype(F32) + right.astype(F32)).astype(BF)


def pick(value, index, axis):
    return lax.dynamic_index_in_dim(value, index, axis, keepdims=False)


def reduce_blocks(kept, given, first, bins, fsdp, f, stages, beside=None):
    count, _, _, width = kept.shape
    split = fsdp // 4
    bits = bits_of(split)[::-1]
    grads = add_low(kept, swap(given, "fsdp", fsdp, bits[0]))
    for bit in bits[1:]:
        view = grads.reshape(count, bins, 2, grads.shape[2] // 2, width)
        flag = jnp.where((f & bit) != 0, 1, 0)
        got = swap(pick(view, 1 - flag, 2), "fsdp", fsdp, bit)
        grads = add_low(pick(view, flag, 2), got)
    if beside is not None:
        beside("fsdp", fsdp, 1, grads)
    stages.append(grads)
    half = grads.shape[2] // 2
    orders = bin_orders(bins)
    parts, left = [], []
    for start, order in zip((0, half), orders):
        part = grads[:, :, start : start + half]
        parts.append(part.reshape((count,) + (2,) * len(order) + (half, width)))
        left.append(sorted(order, reverse=True))
    for pair in zip(*orders):
        for i, bit in enumerate(pair):
            where = 1 + left[i].index(bit)
            got = swap(lax.index_in_dim(parts[i], 1, where, False), "bins", bins, bit)
            parts[i] = add_low(lax.index_in_dim(parts[i], 0, where, False), got)
            left[i].remove(bit)
        if beside is not None:
            parts = [after(part, beside()) for part in parts]
            beside("bins", bins, pair[0], parts[0])
        stages.append(tuple(parts))
    part = jnp.concatenate(parts, axis=1)
    owner = f // split
    last = count - 1
    total = pick(part, jnp.clip(block_of(owner) - first, 0, last), 0).astype(F32)
    for k in range(1, 4):
        sent = pick(part, jnp.clip(block_of(owner ^ k) - first, 0, last), 0)
        got = swap(
            sent,
            "fsdp",
            fsdp,
            k * split,
            lambda t: first <= block_of(t // split) < first + count,
        )
        total = total + got.astype(F32)
    return total


def route_kernel(own_ref, slot_ref, tok_ref, cot_ref, tok_out, cot_out, map_out):
    model, slots = tok_ref.shape[2:]
    bins, _, cap, wide = tok_out.shape
    shift = slots.bit_length() - 1
    high = max(bins, 8)
    row_of = lax.broadcasted_iota(jnp.int32, (slots, slots), 0)
    col_of = lax.broadcasted_iota(jnp.int32, (slots, slots), 1)
    earlier = jnp.where(row_of < col_of, 1.0, 0.0).astype(BF)
    bin_of = lax.broadcasted_iota(jnp.int32, (high, slots), 0)
    slot = slot_ref[0]
    valid = slot >= 0
    safe = jnp.where(valid, slot, 0)
    relative = jnp.where(valid, (safe >> shift) ^ own_ref[0], high)
    onehot = jnp.where(bin_of == relative, 1.0, 0.0)
    before = mm(onehot.astype(BF), earlier)
    rank = jnp.sum(before * onehot, axis=0, keepdims=True).astype(jnp.int32)
    place = jnp.where(valid, relative * cap + rank, slots)
    send = jnp.where(row_of == place, 1.0, 0.0)
    map_out[0] = send.astype(BF)
    mark = jnp.where(valid, (safe & (slots - 1)) + 1, 0).astype(F32)
    marks = jnp.sum(send * mark, axis=1, keepdims=True)
    marks = jnp.broadcast_to(marks, (slots, wide - model)).astype(BF)
    tok = mm_t(send.astype(BF), tok_ref[0, 0]).astype(BF)
    cot = mm_t(send.astype(BF), cot_ref[0, 0]).astype(BF)
    for k in range(bins):
        rows = slice(k * cap, (k + 1) * cap)
        tok_out[k, 0, :, :model] = tok[rows]
        tok_out[k, 0, :, model:] = marks[rows]
        cot_out[k, 0] = cot[rows]


def vmem_specs(count):
    return [pl.BlockSpec(memory_space=pltpu.VMEM)] * count


def route(own, slot_rows, tokens, cotangent, bins):
    micro, _, model, slots = tokens.shape
    cap = slots // bins
    wide = model + (-model - 1) % 128 + 1
    block = pl.BlockSpec((1, 1, model, slots), lambda i: (i, 0, 0, 0))
    return pl.pallas_call(
        route_kernel,
        grid=(micro,),
        in_specs=[
            pl.BlockSpec(memory_space=pltpu.SMEM),
            pl.BlockSpec((1, 1, slots), lambda i: (i, 0, 0)),
            block,
            block,
        ],
        out_specs=[
            pl.BlockSpec((bins, 1, cap, wide), lambda i: (0, i, 0, 0)),
            pl.BlockSpec((bins, 1, cap, model), lambda i: (0, i, 0, 0)),
            pl.BlockSpec((1, slots, slots), lambda i: (i, 0, 0)),
        ],
        out_shape=[
            jax.ShapeDtypeStruct((bins, micro, cap, wide), BF),
            jax.ShapeDtypeStruct((bins, micro, cap, model), BF),
            jax.ShapeDtypeStruct((micro, slots, slots), BF),
        ],
        name="route",
    )(own, slot_rows, tokens, cotangent)


def unroute_kernel(*refs):
    map_ref = refs[0]
    out_one, out_two, home_ref = refs[-3:]
    pieces = refs[1:-3]
    bins = len(pieces) // 2
    cap = pieces[0].shape[1]
    for out, group in ((out_one, pieces[:bins]), (out_two, pieces[bins:])):
        for k, piece in enumerate(group):
            home_ref[k * cap : (k + 1) * cap, :] = piece[0]
        out[0, 0] = t_mm(home_ref[...], map_ref[0]).astype(BF)


def unroute(send_map, one, two):
    micro, slots, _ = send_map.shape
    cap, model = one[0].shape[1:]
    pieces = list(one) + list(two)
    out = jax.ShapeDtypeStruct((micro, 1, model, slots), BF)
    block = pl.BlockSpec((1, 1, model, slots), lambda i: (i, 0, 0, 0))
    return pl.pallas_call(
        unroute_kernel,
        grid=(micro,),
        in_specs=[pl.BlockSpec((1, slots, slots), lambda i: (i, 0, 0))]
        + [pl.BlockSpec((1, cap, model), lambda i: (i, 0, 0))] * len(pieces),
        out_specs=[block, block],
        out_shape=[out, out],
        scratch_shapes=[pltpu.VMEM((slots, model), BF)],
        name="unroute",
    )(send_map, *pieces)


def split_rows(acc_ref, own_ref, keep_ref, give_ref, index, start, width):
    half = keep_ref.shape[-2]
    mine = pl.ds(pl.multiple_of(own_ref[2] * half, 8), half)
    other = pl.ds(pl.multiple_of((1 - own_ref[2]) * half, 8), half)
    keep_ref[index] = acc_ref[mine, start : start + width].astype(BF)
    give_ref[index] = acc_ref[other, start : start + width].astype(BF)


def add_moment(acc_ref, own_ref, moment, start, width):
    high = moment.shape[0]
    if high % 8 == 0:
        rows = pl.ds(pl.multiple_of(own_ref[1] * high, 8), high)
        acc_ref[rows, start : start + width] += moment
        return
    for i in range(acc_ref.shape[0] // high):

        @pl.when(own_ref[1] == i)
        def _():
            acc_ref[i * high : (i + 1) * high, start : start + width] += moment


def give_back(values, land_ref, back_ref, m):
    bins, _, cap, _ = back_ref.shape
    back = mm(land_ref, values).astype(BF)
    for k in range(bins):
        back_ref[k, m] = back[k * cap : (k + 1) * cap]


def feed_kernel(own_ref, a2_ref, up_grad_ref, w_ref, moment_ref, h_ref, land_ref,
                dh2_ref, keep_ref, give_ref, back_ref,
                a2t_ref, gt_ref, act_ref, du_ref, acc_ref, y_ref):
    step = pl.program_id(0)
    tokens = a2_ref.shape[0]
    chunk = 256

    @pl.when(step == 0)
    def _():
        a2t_ref[...] = a2_ref[...].T
        gt_ref[...] = up_grad_ref[...].T
        y_ref[...] = h_ref[...]
        dh2_ref[...] = jnp.zeros_like(dh2_ref)

    width = w_ref.shape[3] // 3
    w_both = w_ref[0, 0, :, : 2 * width]
    w_down = w_ref[0, 0, :, 2 * width :]
    for start in range(0, tokens, chunk):
        rows = pl.ds(start, chunk)
        a2 = a2_ref[rows, :]
        both = mm(a2, w_both)
        gate = both[:, :width]
        up = both[:, width:]
        dact = mm(up_grad_ref[rows, :], w_down)
        sig = 1.0 / (1.0 + jnp.exp(-gate))
        silu = gate * sig
        act = (silu * up).astype(BF)
        dgate = (dact * up * sig * (1.0 + gate * (1.0 - sig))).astype(BF)
        dup = (dact * silu).astype(BF)
        act_ref[rows, :] = act
        du_ref[rows, :width] = dgate
        du_ref[rows, width:] = dup
        y_ref[rows, :] += mm_t(act, w_down)
        dh2_ref[rows, :] += mm_t(du_ref[rows, :], w_both)
    acc_ref[:, : 2 * width] = mm(a2t_ref[...], du_ref[...])
    acc_ref[:, 2 * width :] = mm(gt_ref[...], act_ref[...])

    @pl.when(step == 0)
    def _():
        for index in range(3):
            add_moment(acc_ref, own_ref, moment_ref[index], index * width, width)

    for index in range(3):
        split_rows(
            acc_ref, own_ref, keep_ref, give_ref, (index, 0), index * width, width
        )

    @pl.when(step == pl.num_programs(0) - 1)
    def _():
        micro, slots, _ = land_ref.shape
        for m in range(micro):
            rows = slice(m * slots, (m + 1) * slots)
            give_back(y_ref[rows, :].astype(BF), land_ref[m], back_ref, m)


def feed_forward_back(own, a2, up_grad, weights, moments, h, land):
    tokens, model = a2.shape
    _, bins, _, width = weights.shape
    width = width // 3
    micro, slots, _ = land.shape
    cap = slots // bins
    whole = pl.BlockSpec((tokens, model), lambda i, own_ref: (0, 0))
    halves = pl.BlockSpec((3, 1, model // 2, width), lambda i, own_ref: (0, i, 0, 0))
    block = pl.BlockSpec((1, 1, model, 3 * width), lambda i, own_ref: (0, i, 0, 0))
    return pl.pallas_call(
        feed_kernel,
        grid_spec=pltpu.PrefetchScalarGridSpec(
            num_scalar_prefetch=1,
            grid=(bins,),
            in_specs=[
                whole,
                whole,
                block,
                pl.BlockSpec(moments.shape, lambda i, own_ref: (0, 0, 0)),
                whole,
                pl.BlockSpec(land.shape, lambda i, own_ref: (0, 0, 0)),
            ],
            out_specs=[
                whole,
                halves,
                halves,
                pl.BlockSpec((bins, micro, cap, model), lambda i, own_ref: (0, 0, 0, 0)),
            ],
            scratch_shapes=[
                pltpu.VMEM((model, tokens), BF),
                pltpu.VMEM((model, tokens), BF),
                pltpu.VMEM((tokens, width), BF),
                pltpu.VMEM((tokens, 2 * width), BF),
                pltpu.VMEM((model, 3 * width), F32),
                pltpu.VMEM((tokens, model), F32),
            ],
        ),
        out_shape=[
            jax.ShapeDtypeStruct((tokens, model), F32),
            jax.ShapeDtypeStruct((3, bins, model // 2, width), BF),
            jax.ShapeDtypeStruct((3, bins, model // 2, width), BF),
            jax.ShapeDtypeStruct((bins, micro, cap, model), BF),
        ],
        name="feed",
    )(own, a2, up_grad, weights, moments, h, land)


def finish_kernel(gain_rate, own_ref, *refs):
    pieces, moments, outs = refs[:4], refs[4:6], refs[6:]
    width = pieces[0].shape[2]
    rows = moments[0].shape[1]
    q_cols = width * 3 // 8
    k_cols = width // 8

    def block(index, kind):
        place = own_ref[0] ^ block_of(index)
        value = pieces[0][kind, :rows].astype(F32)
        for k in range(1, 4):
            value = jnp.where(place == k, pieces[k][kind, :rows].astype(F32), value)
        return value

    def lanes(start, count):
        source = lax.broadcasted_iota(jnp.int32, (width, count), 0)
        target = lax.broadcasted_iota(jnp.int32, (width, count), 1)
        return jnp.where(source == target + start, 1.0, 0.0).astype(BF)

    narrow = -math.sqrt(HEADS / KV_HEADS)
    for kind in range(2):
        zero = block(0, kind).astype(BF)
        for i, start in enumerate((q_cols, q_cols + k_cols)):
            value = dot(lanes(start, k_cols), zero, ((0,), (1,)))
            outs[2 + 2 * i + kind][...] = narrow * value if kind else value
        for i, start in ((0, 0), (6, q_cols + 2 * k_cols)):
            value = mm(zero, lanes(start, q_cols))
            outs[i + kind][...] = -value if kind else value
        for index in range(1, 4):
            value = block(index, kind)
            rate = -DOWN_RATE if index == 3 else -1.0
            outs[6 + 2 * index + kind][...] = rate * value if kind else value
        grad = sum(piece[kind, rows : rows + 1, :rows].astype(F32) for piece in pieces)
        value = 0.5 * moments[kind][...] + 0.5 * grad
        outs[14 + 2 * kind][...] = value
        outs[15 + 2 * kind][...] = -gain_rate * value


def finish(own, pieces, moments, gain_rate):
    width = pieces[0].shape[2]
    rows = moments[0].shape[1]
    q_cols = width * 3 // 8
    k_cols = width // 8
    shapes = [(rows, q_cols)] * 2 + [(k_cols, rows)] * 4 + [(rows, q_cols)] * 2
    shapes += [(rows, width)] * 6 + [(1, rows)] * 4
    return pl.pallas_call(
        functools.partial(finish_kernel, gain_rate),
        grid=(1,),
        in_specs=[pl.BlockSpec(memory_space=pltpu.SMEM)]
        + [full_spec(piece.shape) for piece in (*pieces, *moments)],
        out_specs=[full_spec(shape) for shape in shapes],
        out_shape=[jax.ShapeDtypeStruct(shape, F32) for shape in shapes],
        name="finish",
    )(own, *pieces, *moments)


def newton_kernel(kind_ref, state_ref, out_ref, z_ref, zb_ref, a_ref, ab_ref, pb_ref):
    bins, size, width = state_ref.shape
    quarter = width * 3 // 8
    eighth = width // 8

    def run(size, cols, total):
        groups = [(i, min(128, size - i)) for i in range(0, size, 128)]
        chunks = [(i, min(384, size - i)) for i in range(0, size, 384)]
        scale = 1.0 / (jnp.sqrt(jnp.full((1, 1), total, F32)) + 1e-07)
        for start, high in chunks:
            rows = slice(start, start + high)
            value = z_ref[rows, :cols] * scale
            z_ref[rows, :cols] = value
            zb_ref[rows, :cols] = value.astype(BF)

        def diagonal(ref, target, start, high):
            downs, acrosses = [], []
            for spot, count in groups:
                if start <= spot < start + high:
                    rows = slice(spot, spot + count)
                    tile = ref[spot - start : spot - start + count, rows]
                    row_of = lax.broadcasted_iota(jnp.int32, (count, count), 0)
                    eye = row_of == lax.broadcasted_iota(jnp.int32, (count, count), 1)
                    value = jnp.where(eye, tile, 0.0)
                    target[rows, rows] = jnp.where(eye, 0.0, tile).astype(BF)
                    downs.append(jnp.sum(value, axis=1, keepdims=True))
                    acrosses.append(jnp.sum(value, axis=0, keepdims=True))
            down = downs[0] if len(downs) == 1 else jnp.concatenate(downs, axis=0)
            return down, acrosses

        def step(index, carry):
            downs, across = [], []
            for start, high in chunks:
                rows = slice(start, start + high)
                gram = mm_t(zb_ref[rows, :cols], zb_ref[:size, :cols])
                a_ref[rows, :size] = gram
                ab_ref[rows, :size] = gram.astype(BF)
                down, parts = diagonal(gram, ab_ref, start, high)
                downs.append(down)
                across += parts
            across = jnp.concatenate(across, axis=1)
            diags = []
            for (start, high), down in zip(chunks, downs):
                rows = slice(start, start + high)
                square = mm(ab_ref[rows, :size], ab_ref[:size, :size])
                factor = (COEFF_B + COEFF_C * down) + COEFF_C * across
                poly = a_ref[rows, :size] * factor + COEFF_C * square
                pb_ref[rows, :size] = poly.astype(BF)
                diag, _ = diagonal(poly, pb_ref, start, high)
                diags.append(COEFF_A + diag - COEFF_C * down * down)
            for (start, high), diag in zip(chunks, diags):
                rows = slice(start, start + high)
                value = diag * z_ref[rows, :cols] + mm(pb_ref[rows, :size], zb_ref[:size, :cols])
                z_ref[rows, :cols] = value
            for start, high in chunks:
                rows = slice(start, start + high)
                zb_ref[rows, :cols] = z_ref[rows, :cols].astype(BF)
            return carry

        lax.fori_loop(0, NS_STEPS, step, 0)

    def keep_lanes(first, wide, low, high):
        lane = lax.broadcasted_iota(jnp.int32, (size, wide), 1) + first
        return (lane >= low) & (lane < high)

    def put(first, wide, low, high, mine):
        keep = keep_lanes(first, wide, low, high)
        old = out_ref[:, first : first + wide].astype(F32)
        out_ref[:, first : first + wide] = jnp.where(keep, mine.astype(F32), old).astype(BF)

    def load(wide, fetch):
        total = jnp.zeros((), F32)
        for j in range(bins):
            piece = fetch(j)
            z_ref[:, j * wide : (j + 1) * wide] = piece
            total = total + jnp.sum(piece * piece)
        run(size, wide * bins, total)

    kind = kind_ref[0]

    @pl.when(kind == 0)
    def _():
        load(width, lambda j: state_ref[j].astype(F32))
        out_ref[...] = zb_ref[:, :width]

    large = 256 if width == 384 else width
    small = 128 if width == 384 else width
    middle = 128 if width == 384 else 0
    k_low = jnp.where(kind == 1, quarter, quarter + eighth)

    @pl.when(kind != 0)
    def _():
        out_ref[...] = jnp.zeros_like(out_ref)

        def large_piece(j):
            low = state_ref[j, :, :large].astype(F32)
            low = jnp.where(keep_lanes(0, large, 0, quarter), low, 0.0)
            high = state_ref[j, :, width - large :].astype(F32)
            high = jnp.where(
                keep_lanes(width - large, large, width - quarter, width), high, 0.0
            )
            return jnp.where(kind == 1, low, high)

        load(large, large_piece)

        @pl.when(kind == 1)
        def _():
            put(0, large, 0, quarter, zb_ref[:, :large])

        @pl.when(kind != 1)
        def _():
            put(width - large, large, width - quarter, width, zb_ref[:, :large])

        narrow = bins * eighth
        lane = lax.broadcasted_iota(jnp.int32, (small, narrow), 0) + middle - k_low
        column = lax.broadcasted_iota(jnp.int32, (small, narrow), 1)
        inside = (lane >= 0) & (lane < eighth)
        turned = jnp.zeros((narrow, size), F32)
        for j in range(bins):
            chosen = jnp.where(inside & (column == lane + j * eighth), 1.0, 0.0).astype(BF)
            piece = state_ref[j, :, middle : middle + small]
            turned = turned + dot(chosen, piece, ((0,), (1,)))
        z_ref[:narrow, :size] = turned
        run(narrow, size, jnp.sum(turned * turned))
        chosen = jnp.where(inside & (column == lane), 1.0, 0.0).astype(BF)
        back = dot(zb_ref[:narrow, :size], chosen, ((0,), (1,)))
        put(middle, small, k_low, k_low + eighth, back)


def newton(kind, state):
    bins, size, width = state.shape
    cols = bins * width
    return pl.pallas_call(
        newton_kernel,
        in_specs=[
            pl.BlockSpec(memory_space=pltpu.SMEM),
            pl.BlockSpec(memory_space=pltpu.VMEM),
        ],
        out_specs=pl.BlockSpec(memory_space=pltpu.VMEM),
        out_shape=jax.ShapeDtypeStruct((size, width), BF),
        scratch_shapes=[
            pltpu.VMEM((size, cols), F32),
            pltpu.VMEM((size, cols), BF),
            pltpu.VMEM((size, size), F32),
            pltpu.VMEM((size, size), BF),
            pltpu.VMEM((size, size), BF),
        ],
        name="newton",
    )(kind, state)


def half_swap(value):
    lane = lax.broadcasted_iota(jnp.int32, value.shape, 1)
    low = (lane % HEAD_DIM) < HEAD_DIM // 2
    return jnp.where(low, pltpu.roll(value, 96, 1), pltpu.roll(value, 32, 1))


def twice(value, upper):
    lane = lax.broadcasted_iota(jnp.int32, value.shape, 1)
    keep = (lane >= HEAD_DIM) if upper else (lane < HEAD_DIM)
    part = jnp.where(keep, value, 0.0)
    return part + pltpu.roll(part, HEAD_DIM, 1)


def fold(value):
    return value + pltpu.roll(value, HEAD_DIM, 1)


PAIRS = (HEADS + 1) // 2
KV_PAIRS = (KV_HEADS + 1) // 2
Q_WIDE = PAIRS * 128
KV_WIDE = KV_PAIRS * 128
WIDE = Q_WIDE + 2 * KV_WIDE
SCALE = 1.0 / math.sqrt(HEAD_DIM)


def soft_rows(query, key, allowed):
    scores = jnp.where(allowed, mm_t(query, key) * SCALE, NEGATIVE)
    raised = jnp.exp(scores - jnp.max(scores, axis=1, keepdims=True))
    return raised * (1.0 / jnp.sum(raised, axis=1, keepdims=True))


def allow(seg_col, seg_row):
    size = seg_row.shape[1]
    row = lax.broadcasted_iota(jnp.int32, (size, size), 0)
    col = lax.broadcasted_iota(jnp.int32, (size, size), 1)
    return (seg_col == seg_row) & (col <= row)


def key_pair(qkv, base, kv):
    group = qkv[:, base + (kv // 2) * 128 : base + (kv // 2) * 128 + 128].astype(F32)
    return twice(group, kv % 2 == 1).astype(BF)


def masked_half(group, head):
    lane = lax.broadcasted_iota(jnp.int32, group.shape, 1)
    keep = (lane >= HEAD_DIM) if head % 2 else (lane < HEAD_DIM)
    return jnp.where(keep, group.astype(F32), 0.0).astype(BF)


def take_columns(w_ref, own, kind_start, cols, start, wide, bins):
    width = w_ref.shape[2]
    source = lax.broadcasted_iota(jnp.int32, (width, wide), 0)
    target = lax.broadcasted_iota(jnp.int32, (width, wide), 1) + start
    inside = (source >= kind_start) & (source < kind_start + cols)
    result = None
    for j in range(start // cols, min((start + wide - 1) // cols, bins - 1) + 1):
        chosen = inside & (source - kind_start == target - j * cols)
        part = mm(w_ref[own ^ j], jnp.where(chosen, 1.0, 0.0).astype(BF))
        result = part if result is None else result + part
    return result.astype(BF)


def attend_kernel(*refs):
    own_ref = refs[0]
    bins = (len(refs) - 23) // 2
    toks = refs[1 : 1 + bins]
    cots = refs[1 + bins : 1 + 2 * bins]
    (gain_in, w_ref, cos_ref, sin_ref, sc_ref, sr_ref,
     x_ref, g_ref, land_ref, a1_ref, qkv_ref, ob_ref, h_ref, a2_ref, wqkv_ref, wo_ref, gain_ref,
     got_ref, got2_ref, land_t, keys_ref, values_ref) = refs[1 + 2 * bins :]
    slots, model = x_ref.shape
    cap = slots // bins
    width = w_ref.shape[2]
    q_cols = width * 3 // 8
    k_cols = width // 8

    @pl.when(pl.program_id(0) == 0)
    def _():
        row = lax.broadcasted_iota(jnp.int32, (model, model), 0)
        eye = row == lax.broadcasted_iota(jnp.int32, (model, model), 1)
        for i in range(2):
            column = gain_in[:, i : i + 1].astype(F32)
            gain_ref[i : i + 1, :] = jnp.sum(
                jnp.where(eye, column, 0.0), axis=0, keepdims=True
            )
        for tile in range(WIDE // 128):
            if tile < PAIRS:
                spot = (0, q_cols, tile * 128)
            elif tile < PAIRS + KV_PAIRS:
                spot = (q_cols, k_cols, (tile - PAIRS) * 128)
            else:
                spot = (q_cols + k_cols, k_cols, (tile - PAIRS - KV_PAIRS) * 128)
            wqkv_ref[:, tile * 128 : tile * 128 + 128] = take_columns(
                w_ref, own_ref[0], *spot, 128, bins
            )
        for tile in range(PAIRS):
            wo_ref[:, tile * 128 : tile * 128 + 128] = take_columns(
                w_ref, own_ref[0], q_cols + 2 * k_cols, q_cols, tile * 128, 128, bins
            )

    spot = lax.broadcasted_iota(jnp.int32, (cap, slots), 1)
    for k in range(bins):
        rows = slice(k * cap, (k + 1) * cap)
        place = toks[k][0, :, model : model + 1].astype(F32).astype(jnp.int32) - 1
        land = jnp.where(spot == place, 1.0, 0.0).astype(BF)
        land_t[rows, :] = land
        got_ref[rows, :] = toks[k][0, :, :model]
        got2_ref[rows, :] = cots[k][0]
    land_ref[0] = land_t[...]
    x = t_mm(land_t[...], got_ref[...])
    x_ref[...] = x.astype(BF)
    g_ref[...] = t_mm(land_t[...], got2_ref[...]).astype(BF)
    r1 = lax.rsqrt(jnp.mean(x * x, axis=1, keepdims=True) + EPSILON)
    a1 = (x * r1 * gain_ref[0:1, :]).astype(BF)
    a1_ref[...] = a1
    cosine = cos_ref[...]
    sine = sin_ref[...]
    for start in range(0, WIDE, 256):
        wide = min(256, WIDE - start)
        both = mm(a1, wqkv_ref[:, start : start + wide])
        for spot in range(0, wide, 128):
            value = both[:, spot : spot + 128]
            if start + spot < Q_WIDE + KV_WIDE:
                value = value * cosine + half_swap(value) * sine
            qkv_ref[:, start + spot : start + spot + 128] = value.astype(BF)
    allowed = allow(sc_ref[0], sr_ref[0])
    for kv in range(KV_HEADS):
        keys_ref[kv] = key_pair(qkv_ref, Q_WIDE, kv)
        values_ref[kv] = key_pair(qkv_ref, Q_WIDE + KV_WIDE, kv)
    lane = lax.broadcasted_iota(jnp.int32, (slots, 128), 1)

    def one_pair(pair):
        lanes = slice(pair * 128, pair * 128 + 128)
        group = qkv_ref[:, lanes]
        parts = []
        for half in range(min(2, HEADS - 2 * pair)):
            kv = (2 * pair + half) // GROUPS
            soft = soft_rows(masked_half(group, half), keys_ref[kv], allowed)
            parts.append(mm(soft.astype(BF), values_ref[kv]))
        parts.append(jnp.zeros((slots, 128), F32))
        ob_ref[:, lanes] = jnp.where(lane < HEAD_DIM, parts[0], parts[1]).astype(BF)

    for pair in range(PAIRS):
        one_pair(pair)
    h = x + mm(ob_ref[:, :model], wo_ref[:, :model])
    h_ref[...] = h
    r2 = lax.rsqrt(jnp.mean(h * h, axis=1, keepdims=True) + EPSILON)
    a2_ref[...] = (h * r2 * gain_ref[1:2, :]).astype(BF)


def row_spec(slots, width):
    return pl.BlockSpec((slots, width), lambda i: (i, 0))


def full_spec(shape):
    return pl.BlockSpec(shape, lambda i: (0,) * len(shape))


def attend(own, toks, cots, gains, weights, cosine, sine, seg_col, seg_row):
    bins, model, _ = weights.shape
    micro, _, slots = seg_row.shape
    total = micro * slots
    cap = slots // bins
    row_shapes = ((model, BF), (WIDE, BF), (Q_WIDE, BF), (model, F32), (model, BF))
    wide = toks[0].shape[2]
    return pl.pallas_call(
        attend_kernel,
        grid=(micro,),
        in_specs=[pl.BlockSpec(memory_space=pltpu.SMEM)]
        + [pl.BlockSpec((1, cap, wide), lambda i: (i, 0, 0))] * bins
        + [pl.BlockSpec((1, cap, model), lambda i: (i, 0, 0))] * bins
        + [
            full_spec(gains.shape), full_spec(weights.shape),
            row_spec(slots, 128), row_spec(slots, 128),
            pl.BlockSpec((1, slots, 1), lambda i: (i, 0, 0)),
            pl.BlockSpec((1, 1, slots), lambda i: (i, 0, 0)),
        ],
        out_specs=[
            row_spec(slots, model), row_spec(slots, model),
            pl.BlockSpec((1, slots, slots), lambda i: (i, 0, 0)),
        ]
        + [row_spec(slots, wide) for wide, _ in row_shapes]
        + [full_spec((model, WIDE)), full_spec((model, Q_WIDE)), full_spec((2, model))],
        out_shape=[
            jax.ShapeDtypeStruct((total, model), BF),
            jax.ShapeDtypeStruct((total, model), BF),
            jax.ShapeDtypeStruct((micro, slots, slots), BF),
        ]
        + [jax.ShapeDtypeStruct((total, wide), kind) for wide, kind in row_shapes]
        + [
            jax.ShapeDtypeStruct((model, WIDE), BF),
            jax.ShapeDtypeStruct((model, Q_WIDE), BF),
            jax.ShapeDtypeStruct((2, model), F32),
        ],
        scratch_shapes=[
            pltpu.VMEM((slots, model), BF),
            pltpu.VMEM((slots, model), BF),
            pltpu.VMEM((slots, slots), BF),
            pltpu.VMEM((KV_HEADS, slots, 128), BF),
            pltpu.VMEM((KV_HEADS, slots, 128), BF),
        ],
        name="attend",
    )(own, *toks, *cots, gains, weights, cosine, sine, seg_col, seg_row)


def attend_back_kernel(own_ref, x_ref, gain_ref, wqkv_ref, wo_ref, cos_ref, sin_ref, sc_ref,
                       sr_ref, a1_ref, qkv_ref, ob_ref, h_ref, dh2_ref, g_ref, land_ref,
                       moment_ref, back_ref, gains_ref, keep_ref, give_ref,
                       a1_all, ob_all, d_all, dhb_all, acc_ref, dob_ref,
                       keys_ref, values_ref, dkeys, dvalues):
    step = pl.program_id(0)
    slots, model = x_ref.shape
    rows = pl.ds(pl.multiple_of(step * slots, slots), slots)

    @pl.when(step == 0)
    def _():
        gains_ref[...] = jnp.zeros_like(gains_ref)

    h = h_ref[...]
    dh2 = dh2_ref[...]
    r2 = lax.rsqrt(jnp.mean(h * h, axis=1, keepdims=True) + EPSILON)
    scaled = dh2 * gain_ref[1:2, :]
    inner = jnp.mean(scaled * h, axis=1, keepdims=True)
    dh = g_ref[...].astype(F32) + r2 * scaled - h * (r2 * r2 * r2 * inner)
    gains_ref[1:2, :] += jnp.sum(dh2 * h * r2, axis=0, keepdims=True)
    dhb = dh.astype(BF)
    dhb_all[rows, :] = dhb
    a1_all[:, rows] = a1_ref[...].T
    ob_all[:, rows] = ob_ref[:, :model].T
    allowed = allow(sc_ref[0], sr_ref[0])
    for kv in range(KV_HEADS):
        keys_ref[kv] = key_pair(qkv_ref, Q_WIDE, kv)
        values_ref[kv] = key_pair(qkv_ref, Q_WIDE + KV_WIDE, kv)
    dkeys[...] = jnp.zeros_like(dkeys)
    dvalues[...] = jnp.zeros_like(dvalues)
    dob_ref[:, :model] = mm_t(dhb, wo_ref[:, :model]).astype(BF)
    dob_ref[:, model:] = jnp.zeros((slots, Q_WIDE - model), BF)
    cosine = cos_ref[...]
    sine = sin_ref[...]
    lane = lax.broadcasted_iota(jnp.int32, (slots, 128), 1)

    def one_pair(pair):
        lanes = slice(pair * 128, pair * 128 + 128)
        group = qkv_ref[:, lanes]
        dob = dob_ref[:, lanes]
        parts = []
        for half in range(min(2, HEADS - 2 * pair)):
            kv = (2 * pair + half) // GROUPS
            query = masked_half(group, half)
            soft = soft_rows(query, keys_ref[kv], allowed)
            mine = masked_half(dob, half)
            dp = mm_t(mine, values_ref[kv])
            ds = (soft * (dp - jnp.sum(soft * dp, axis=1, keepdims=True))).astype(BF)
            parts.append(mm(ds, keys_ref[kv]))
            dkeys[kv] += t_mm(ds, query)
            dvalues[kv] += t_mm(soft.astype(BF), mine)
        parts.append(jnp.zeros((slots, 128), F32))
        out = jnp.where(lane < HEAD_DIM, parts[0], parts[1]) * SCALE
        out = out * cosine - half_swap(out) * sine
        d_all[rows, lanes] = out.astype(BF)

    for pair in range(PAIRS):
        one_pair(pair)
    for pair in range(KV_PAIRS):
        lane = lax.broadcasted_iota(jnp.int32, (slots, 128), 1)

        def both(parts):
            low = fold(parts[2 * pair])
            high = fold(parts[2 * pair + 1]) if 2 * pair + 1 < KV_HEADS else 0.0
            return jnp.where(lane < HEAD_DIM, low, high)

        dk = both(dkeys) * SCALE
        dk = dk * cosine - half_swap(dk) * sine
        start = Q_WIDE + pair * 128
        d_all[rows, start : start + 128] = dk.astype(BF)
        start += KV_WIDE
        d_all[rows, start : start + 128] = both(dvalues).astype(BF)
    dh1 = mm_t(d_all[rows, :], wqkv_ref[...])
    x = x_ref[...].astype(F32)
    r1 = lax.rsqrt(jnp.mean(x * x, axis=1, keepdims=True) + EPSILON)
    scaled = dh1 * gain_ref[0:1, :]
    inner = jnp.mean(scaled * x, axis=1, keepdims=True)
    dx = dh + r1 * scaled - x * (r1 * r1 * r1 * inner)
    gains_ref[0:1, :] += jnp.sum(dh1 * x * r1, axis=0, keepdims=True)
    give_back(dx.astype(BF), land_ref[0], back_ref, step)

    @pl.when(step == pl.num_programs(0) - 1)
    def _():
        width = acc_ref.shape[1]
        bins = keep_ref.shape[0]
        q_cols = width * 3 // 8
        k_cols = width // 8
        wide = 256 if width == 384 else width
        skip = width - wide
        spot = lax.broadcasted_iota(jnp.int32, (1, wide), 1)
        late = spot + skip - (q_cols + 2 * k_cols)
        for k in range(bins):
            j = own_ref[0] ^ k
            target = jnp.where(
                spot < q_cols,
                j * q_cols + spot,
                jnp.where(
                    spot < q_cols + k_cols,
                    Q_WIDE + j * k_cols + spot - q_cols,
                    jnp.where(
                        spot < q_cols + 2 * k_cols,
                        Q_WIDE + KV_WIDE + j * k_cols + spot - q_cols - k_cols,
                        -1,
                    ),
                ),
            )
            source = lax.broadcasted_iota(jnp.int32, (WIDE, wide), 0)
            chosen = mm(d_all[...], jnp.where(source == target, 1.0, 0.0).astype(BF))
            first = mm(a1_all[...], chosen.astype(BF))
            target = jnp.where(late >= 0, j * q_cols + late, -1)
            source = lax.broadcasted_iota(jnp.int32, (model, wide), 0)
            chosen = mm(dhb_all[...], jnp.where(source == target, 1.0, 0.0).astype(BF))
            second = mm(ob_all[...], chosen.astype(BF))
            if skip:
                acc_ref[:, :skip] = first[:, :skip]
                acc_ref[:, skip:wide] = first[:, skip:] + second[:, : wide - skip]
                acc_ref[:, wide:] = second[:, wide - skip :]
            else:
                acc_ref[...] = first + second
            if k == 0:
                add_moment(acc_ref, own_ref, moment_ref[...], 0, width)
            split_rows(acc_ref, own_ref, keep_ref, give_ref, k, 0, width)


def attend_back(own, x, gains, wqkv, wo, cosine, sine, seg_col, seg_row,
                a1, qkv, ob, h, dh2, g, land, moment, bins):
    total, model = x.shape
    micro, slots, _ = land.shape
    cap = slots // bins
    width = moment.shape[1]
    return pl.pallas_call(
        attend_back_kernel,
        grid=(micro,),
        in_specs=[
            pl.BlockSpec(memory_space=pltpu.SMEM),
            row_spec(slots, model), full_spec(gains.shape), full_spec(wqkv.shape),
            full_spec(wo.shape), row_spec(slots, 128), row_spec(slots, 128),
            pl.BlockSpec((1, slots, 1), lambda i: (i, 0, 0)),
            pl.BlockSpec((1, 1, slots), lambda i: (i, 0, 0)),
            row_spec(slots, model), row_spec(slots, WIDE), row_spec(slots, Q_WIDE),
            row_spec(slots, model), row_spec(slots, model), row_spec(slots, model),
            pl.BlockSpec((1, slots, slots), lambda i: (i, 0, 0)),
            full_spec(moment.shape),
        ],
        out_specs=[
            full_spec((bins, micro, cap, model)), full_spec((2, model)),
            full_spec((bins, model // 2, width)), full_spec((bins, model // 2, width)),
        ],
        out_shape=[
            jax.ShapeDtypeStruct((bins, micro, cap, model), BF),
            jax.ShapeDtypeStruct((2, model), F32),
            jax.ShapeDtypeStruct((bins, model // 2, width), BF),
            jax.ShapeDtypeStruct((bins, model // 2, width), BF),
        ],
        scratch_shapes=[
            pltpu.VMEM((model, total), BF),
            pltpu.VMEM((model, total), BF),
            pltpu.VMEM((total, WIDE), BF),
            pltpu.VMEM((total, model), BF),
            pltpu.VMEM((model, width), F32),
            pltpu.VMEM((slots, Q_WIDE), BF),
            pltpu.VMEM((KV_HEADS, slots, 128), BF),
            pltpu.VMEM((KV_HEADS, slots, 128), BF),
            pltpu.VMEM((KV_HEADS, slots, 128), F32),
            pltpu.VMEM((KV_HEADS, slots, 128), F32),
        ],
        name="attend_back",
    )(own, x, gains, wqkv, wo, cosine, sine, seg_col, seg_row,
      a1, qkv, ob, h, dh2, g, land, moment)


def rope_tables(positions):
    half_dim = HEAD_DIM // 2
    frequency = jnp.exp(
        -math.log(ROPE_BASE) * 2.0 * jnp.arange(half_dim, dtype=F32) / HEAD_DIM
    )
    angles = positions.reshape(-1).astype(F32)[:, None] * frequency
    cosine = jnp.cos(angles)
    sine = jnp.sin(angles)
    return (
        jnp.concatenate([cosine] * 4, axis=1),
        jnp.concatenate([-sine, sine, -sine, sine], axis=1),
    )


def slot_layout(lengths, starts, bin_slots):
    slot_index = jnp.arange(bin_slots, dtype=jnp.int32)
    inside = (
        (slot_index[:, None] >= starts[..., None, :])
        & (slot_index[:, None] < starts[..., None, :] + lengths[..., None, :])
    ).astype(jnp.int32)
    number = jnp.arange(lengths.shape[-1], dtype=jnp.int32)
    covered = jnp.minimum(jnp.sum(inside, axis=-1), 1)
    segment = jnp.sum(inside * number, axis=-1) + (1 - covered) * (
        lengths.shape[-1] + slot_index
    )
    first_slot = jnp.sum(inside * starts[..., None, :], axis=-1)
    return (segment, slot_index - first_slot)


def on_device(
    tokens, cotangent, token_slots, sequence_lengths, sequence_starts,
    query_weight, key_weight, value_weight, output_weight,
    gate_weight, up_weight, down_weight, attention_gain, feedforward_gain,
    query_moment, key_moment, value_moment, output_moment,
    gate_moment, up_moment, down_moment, attention_moment, feedforward_moment,
):
    bins = lax.axis_size("bins")
    fsdp = lax.axis_size("fsdp")
    b = lax.axis_index("bins")
    f = lax.axis_index("fsdp")
    micro, _, slots, model = tokens.shape
    total = micro * slots
    rows_own = query_weight.shape[0]
    q_cols = query_weight.shape[1]
    k_cols = key_weight.shape[1]
    split = fsdp // 4
    flag = jnp.where((f & (split // 2)) != 0, 1, 0)
    own = jnp.stack([b, f, flag]).astype(jnp.int32)

    block_zero = jnp.concatenate(
        [query_weight, key_weight, value_weight, output_weight], axis=1
    )[None]
    blocks = jnp.concatenate([gate_weight, up_weight, down_weight.T], axis=1)
    gain_lanes = jnp.pad(
        jnp.stack([attention_gain, feedforward_gain], axis=1), ((0, 0), (0, 126))
    )
    width = block_zero.shape[2]
    zero_chips = gather_chips(
        jnp.concatenate([block_zero[0], gain_lanes], axis=1), fsdp, f
    )
    gains_cols = jnp.concatenate([part[:, :, width:] for part in zero_chips])
    gains_cols = gather_cores(gains_cols[None], fsdp, f)[0]
    zero_chips = [part[:, :, :width] for part in zero_chips]

    tok_send, cot_send, send_map = route(
        own, token_slots, tokens.swapaxes(2, 3), cotangent.swapaxes(2, 3), bins
    )

    def exchange(pieces):
        return [pieces[0]] + [swap(pieces[k], "bins", bins, k) for k in range(1, bins)]

    toks = exchange(tok_send)
    zero_stages = []
    zero_chips = [after(part, *toks) for part in zero_chips]
    zero_bins = gather_bins(*zero_chips, bins, zero_stages)
    feed_chips = gather_chips(after(blocks, tok_send), fsdp, f, zero_bins)
    cots = exchange(after(cot_send, *toks))

    segment, position = slot_layout(sequence_lengths[:, 0, 0], sequence_starts[:, 0, 0], slots)
    cosine, sine = rope_tables(position)

    attn_w = gather_cores(zero_bins, fsdp, f)
    first, second = feed_chips
    feed_stages = []
    ahead = (zero_bins, *cots)
    feed_bins = gather_bins(after(first, *ahead), after(second, *ahead), bins, feed_stages)
    attn_w = after(attn_w, *feed_stages[0])

    edges = (0, q_cols, q_cols + k_cols, q_cols + 2 * k_cols, width)
    seg_col = segment[:, :, None]
    seg_row = segment[:, None, :]
    tables = (cosine, sine, seg_col, seg_row)
    moments = jnp.stack([gate_moment, up_moment, down_moment.T])
    moment_zero = jnp.concatenate(
        [query_moment, key_moment, value_moment, output_moment], axis=1
    )
    gains_cols = after(gains_cols, moments, moment_zero)
    x_low, g_low, land, a1, qkv, ob, h, a2, w_qkv, w_o, gains_full = attend(
        own, toks, cots, gains_cols, attn_w, *tables
    )
    feed_w = gather_cores(after(feed_bins, a2), fsdp, f)

    dh2, kept, given, back = feed_forward_back(own, a2, g_low, feed_w[None], moments, h, land)
    one_stages = []
    part_one = reduce_blocks(kept, given, 1, bins, fsdp, f, one_stages)
    home_one = exchange(back)
    dh2 = after(dh2, one_stages[0])

    back, gain_sum, kept, given = attend_back(
        own, x_low, gains_full, w_qkv, w_o, *tables,
        a1, qkv, ob, h, dh2, g_low, land, moment_zero, bins,
    )
    zero_stages = []
    sums = [gain_sum]

    def beside(axis=None, count=None, bit=None, token=None):
        if axis is not None:
            sums.append(sums[-1] + swap(after(sums[-1], token), axis, count, bit))
        return sums[-1]

    kept = after(kept, *home_one)
    part_zero = reduce_blocks(kept[None], given[None], 0, bins, fsdp, f, zero_stages, beside)

    owner = f // split
    is_zero = block_of(owner) == 0
    state = (0.5 * jnp.where(is_zero, part_zero, part_one)).astype(BF)
    half = state.shape[0] // 2
    state = gather_bins(state[:half], state[half:], bins)
    home_two = exchange(after(back, state))
    for bit in bits_of(split)[1:]:
        beside("fsdp", fsdp, bit, state)
    gain_rows = jnp.pad(
        beside().astype(BF).reshape(2, fsdp, 1, rows_own),
        ((0, 0), (0, 0), (0, 7), (0, width - rows_own)),
    )
    for bit in bits_of(split):
        state = jnp.concatenate([state, swap(state, "fsdp", fsdp, bit)], axis=1)

    kind = jnp.stack([jnp.where(is_zero, 1 + (f & 1), 0), b]).astype(jnp.int32)
    ortho = newton(kind, state)
    other = swap(ortho, "fsdp", fsdp, 1)
    block_output, input_gradient = unroute(after(send_map, other), home_one, home_two)
    other = other.reshape(fsdp // 8, 2, -1, width)[:, ::-1].reshape(ortho.shape)
    lane = jnp.arange(width, dtype=jnp.int32)
    first_core = (lane < edges[2]).astype(jnp.int32)
    ortho = jnp.where(is_zero & (first_core == (f & 1)), other, ortho)

    both = jnp.stack([state[0], ortho]).reshape(2, fsdp, rows_own, width)
    low = f % split
    turn = low * 4

    def parcel(target):
        return jnp.concatenate(
            [pick(both, target ^ turn, 1), pick(gain_rows, target, 1)], axis=1
        )

    pieces = [parcel(f)]
    for k in range(1, 4):
        sent = parcel((owner ^ k) * split + low)
        pieces.append(swap(sent, "fsdp", fsdp, k * split))
    outs = [block_output.swapaxes(2, 3), input_gradient.swapaxes(2, 3)]
    gain_rate = 0.1 / math.sqrt(micro * bins * fsdp * slots)
    moments = (attention_moment[None], feedforward_moment[None])
    done = finish(owner.astype(jnp.int32)[None], pieces, moments, gain_rate)
    for i, value in enumerate(done):
        if i >= 14:
            outs.append(value[0])
        else:
            outs.append(value.T if i in (2, 3, 4, 5, 12, 13) else value)
    return tuple(outs)


def solution(mesh):
    rows = P(None, "fsdp", "bins", None)
    matrix = P("fsdp", "bins")
    turned = P("bins", "fsdp")
    vector = P("fsdp")
    params = (matrix,) * 6 + (turned, vector, vector)
    doubled = ()
    for spec in params:
        doubled += (spec, spec)
    return jax.shard_map(
        on_device,
        mesh=mesh,
        in_specs=(rows, rows, P(None, "fsdp", "bins"), rows, rows) + params + params,
        out_specs=(rows, rows) + doubled,
        check_vma=False,
    )
```
